256 devices in a mesh: dp: 64 (over z, y, x_hi), mp: 4 (over x_lo, core).
Axes of the slice: x: 4 (x_hi: 2, x_lo: 2; x = x_hi * 2 + x_lo), y: 4, z: 8, core: 2. Of those that a mesh axis runs over, the one named last changes fastest.
Arguments:
- hidden_states: bfloat16 [32768, 3584], P('dp'), may hold values from -6 to 6
- token_ids: int32 [2048, 16], P('dp'), may hold values from 0 to 152063, as said below
- norm_gain: float32 [3584], replicated, may hold values from 0.5 to 1.5
- q_weight: bfloat16 [3584, 3584], P('dp', 'mp'), may hold values from -0.09375 to 0.09375
- key_matrix: bfloat16 [3584, 512], P('dp', 'mp'), may hold values from -0.09375 to 0.09375
- value_matrix: bfloat16 [3584, 512], P('dp', 'mp'), may hold values from -0.09375 to 0.09375
- out_weight: bfloat16 [3584, 3584], P('dp', 'mp'), may hold values from -0.09375 to 0.09375
- label_table: bfloat16 [65536, 3584], P(('dp', 'mp')), may hold values from -6 to 6
- refresh_rows: int32 [2048], P(('dp', 'mp')), may hold values from 0 to 255, as said below
- label_counts: int32 [65536], P(('dp', 'mp')), may hold values from 1 to 8191
- queries: bfloat16 [128, 3584], replicated, may hold values from -6 to 6
- positives: int32 [128, 8], replicated, may hold values from 0 to 65535
Outputs:
- label_grad: float32 [65536, 3584], P(('dp', 'mp'))
- query_grad: float32 [128, 3584], replicated
- loss: float32 [], replicated
The draws below stay inside these ranges and needn't reach their ends.
Inputs may be any that keep to these rules, and one draw needn't show every extreme that they name: `token_ids`: in every text the first id is not 0, and after an id 0 all later ids of that text are 0. `refresh_rows`: the 8 entries of each aligned block of 8 entries are distinct.
All inputs are finite; a program needn't handle non-finite values.
Results may differ from the reference program's by a relative error of at most 0.003.
Values may be sent and summed in bfloat16 or wider, within the bound.
No kernel may reach another device: no remote copies, remote signals or barrier semaphores. Data moves between devices by JAX's collectives and lax.ppermute only.
A program may use at most 128 MiB of HBM per device.

```python
import math
import jax
import jax.numpy as jnp
from jax import lax

MODEL_WIDTH = 3584
HQ = 28
KEY_VALUE_HEADS = 4
HEAD_WIDTH = 128
VOCAB = 152064
TXT = 16
POS = 8
LAB_GRP = 32
LAB_OWN = 256
BATCH = 128
TEXTS = 2048
TOKENS = 32768
REF = 8
LABELS = 65536
N_DP = 64


def draw_token_ids(key, part):
    first_key, second_key = jax.random.split(key)
    lengths = jax.random.randint(first_key, (TEXTS, 1), 1, TXT + 1)
    values = jax.random.randint(second_key, (TEXTS, TXT), 1, VOCAB)
    places = jnp.arange(TXT, dtype=jnp.int32)[None, :]
    return jnp.where(places < lengths, values, 0).astype(jnp.int32)


def draw_refresh_rows(key, part):
    blocks = TEXTS // REF
    keys = jax.random.split(key, blocks)
    selected_rows = jax.vmap(lambda block_key: jax.random.permutation(block_key, LAB_OWN)[:REF])(keys)
    return selected_rows.reshape(-1).astype(jnp.int32)


def draw_label_counts(key, part):
    first_key, second_key = jax.random.split(key)
    places = jnp.arange(LABELS, dtype=jnp.int32)
    ceiling = 2 + 12 * places // LABELS
    exponent = jax.random.randint(first_key, (LABELS,), 0, 1 << 20) % ceiling
    power = jnp.left_shift(jnp.ones((LABELS,), jnp.int32), exponent)
    extra = jax.random.randint(second_key, (LABELS,), 0, 1 << 20) % power
    counts = power + extra
    counts = jnp.where(places == 0, 1, counts)
    counts = jnp.where(places == LABELS - 1, 8191, counts)
    return counts.astype(jnp.int32)


def with_ends(array, rng, low, top_value):
    dims = array.shape
    index_at = [jax.random.randint(jax.random.fold_in(rng, axis), (), 0, dims[axis]) for axis in range(len(dims))]
    array = array.at[tuple(index_at)].set(low)
    longest = dims.index(max(dims))
    index_at[longest] = (index_at[longest] + 1) % dims[longest]
    return array.at[tuple(index_at)].set(top_value)


def levels(key, extent, pieces, low, largest):
    level, own = 1.0, jax.random.fold_in(key, 6)
    for position, parts in pieces:
        steps = jnp.exp(jax.random.uniform(jax.random.fold_in(own, position), (parts,), jnp.float32, low / len(pieces), largest / len(pieces)))
        level = level * jnp.repeat(steps, extent[position] // parts).reshape([-1 if axis == position else 1 for axis in range(len(extent))])
    return level


def scatter_about(stream_key, dims, deviation, limit, cuts=(), held_as=jnp.bfloat16):
    result = jax.random.normal(stream_key, dims, jnp.float32) * deviation
    if len(cuts) > 0:
        result = levels(stream_key, dims, cuts, -0.22, 0.18) * result
    return jnp.clip(result, min=-limit, max=limit).astype(held_as)


def setup_inputs(seed: int = 0) -> dict:
    arg_keys = jax.random.split(jax.random.key(seed), 13)
    hidden_states = scatter_about(arg_keys[0], (TOKENS, MODEL_WIDTH), 1.0, 6.0, ((0, 64),))
    token_ids = draw_token_ids(jax.random.fold_in(arg_keys[12], 71), 0)
    norm_gain = jnp.clip(1.0 + 0.1 * jax.random.normal(arg_keys[2], (MODEL_WIDTH,), jnp.float32), 0.5, 1.5)
    q_weight = scatter_about(arg_keys[3], (MODEL_WIDTH, HQ * HEAD_WIDTH), MODEL_WIDTH ** -0.5, 0.09375, ((0, 64), (1, 4)))
    key_matrix = scatter_about(arg_keys[4], (MODEL_WIDTH, KEY_VALUE_HEADS * HEAD_WIDTH), MODEL_WIDTH ** -0.5, 0.09375, ((0, 64), (1, 4)))
    value_matrix = scatter_about(arg_keys[5], (MODEL_WIDTH, KEY_VALUE_HEADS * HEAD_WIDTH), MODEL_WIDTH ** -0.5, 0.09375, ((0, 64), (1, 4)))
    out_weight = scatter_about(arg_keys[6], (MODEL_WIDTH, HQ * HEAD_WIDTH), (HQ * HEAD_WIDTH) ** -0.5, 0.09375, ((0, 64), (1, 4)))
    label_table = scatter_about(arg_keys[7], (LABELS, MODEL_WIDTH), 1.0, 6.0, ((0, 256),))
    refresh_rows = draw_refresh_rows(jax.random.fold_in(arg_keys[12], 71), 0)
    label_counts = draw_label_counts(jax.random.fold_in(arg_keys[12], 71), 0)
    queries = scatter_about(arg_keys[10], (BATCH, MODEL_WIDTH), 1.0, 6.0)
    positives = with_ends(jax.random.randint(arg_keys[11], (BATCH, POS), 0, LABELS), jax.random.fold_in(arg_keys[11], 1), 0, LABELS - 1).astype(jnp.int32)
    return dict(hidden_states=hidden_states, token_ids=token_ids, norm_gain=norm_gain, q_weight=q_weight, key_matrix=key_matrix, value_matrix=value_matrix, out_weight=out_weight, label_table=label_table, refresh_rows=refresh_rows, label_counts=label_counts, queries=queries, positives=positives)


rope_theta = 1000000.0
norm_eps = 1e-06
focal_beta = 0.9999

def rotary(values, head_size):
    length = values.shape[1]
    half = head_size // 2
    frequency = rope_theta ** (-2.0 * jnp.arange(half, dtype=jnp.float32) / head_size)
    angles = jnp.arange(length, dtype=jnp.float32)[:, None] * frequency[None, :]
    cosine = jnp.concatenate([jnp.cos(angles), jnp.cos(angles)], axis=1)[None, :, None, :]
    sine = jnp.concatenate([jnp.sin(angles), jnp.sin(angles)], axis=1)[None, :, None, :]
    turned = jnp.concatenate([-values[..., half:], values[..., :half]], axis=-1)
    return values * cosine + turned * sine

def attend(query_rows, key_rows, value_rows, text_ids, head_size):
    texts, length = text_ids.shape
    kv_heads = key_rows.shape[1] // head_size
    repeat = query_rows.shape[1] // head_size // kv_heads
    query_r = query_rows.astype(jnp.float32).reshape(texts, length, kv_heads, repeat, head_size)
    key_r = key_rows.astype(jnp.float32).reshape(texts, length, kv_heads, head_size)
    value_r = value_rows.astype(jnp.float32).reshape(texts, length, kv_heads, head_size)
    scores = jnp.einsum('ntgrd,nsgd->ngrts', query_r, key_r) / math.sqrt(head_size)
    causal = jnp.arange(length)[:, None] >= jnp.arange(length)[None, :]
    allowed = causal[None, None, None, :, :] & (text_ids != 0)[:, None, None, None, :]
    weights = jnp.where(allowed, jnp.exp(scores), 0.0)
    probs = (weights / lax.optimization_barrier(jnp.sum(weights, axis=-1, keepdims=True))).astype(jnp.bfloat16)
    mixed = jnp.einsum('ngrts,nsgd->ntgrd', probs.astype(jnp.float32), value_r)
    return mixed.reshape(texts * length, -1).astype(jnp.bfloat16)

def reference(hidden_states, token_ids, norm_gain, q_weight, key_matrix, value_matrix, out_weight, label_table, refresh_rows, label_counts, queries, positives):
    grouped = hidden_states.reshape(N_DP, LAB_GRP * TXT, MODEL_WIDTH)
    grouped_ids = token_ids.reshape(N_DP, LAB_GRP, TXT)

    def encode(pair):
        states = pair[0].astype(jnp.float32)
        text_ids = pair[1]
        scaled = lax.rsqrt(lax.optimization_barrier(jnp.mean(states * states, axis=1, keepdims=True)) + norm_eps)
        normed = (states * scaled * norm_gain).astype(jnp.bfloat16)
        query_raw = jnp.dot(normed, q_weight, preferred_element_type=jnp.float32)
        key_raw = jnp.dot(normed, key_matrix, preferred_element_type=jnp.float32)
        value_raw = jnp.dot(normed, value_matrix, preferred_element_type=jnp.float32)
        count_tokens = states.shape[0]
        queries_rot = rotary(query_raw.reshape(LAB_GRP, TXT, -1, HEAD_WIDTH), HEAD_WIDTH).reshape(count_tokens, -1).astype(jnp.bfloat16)
        rotary_keys = rotary(key_raw.reshape(LAB_GRP, TXT, -1, HEAD_WIDTH), HEAD_WIDTH).reshape(count_tokens, -1).astype(jnp.bfloat16)
        values_rot = value_raw.astype(jnp.bfloat16)
        attended = attend(queries_rot, rotary_keys, values_rot, text_ids, HEAD_WIDTH)
        projected = jnp.dot(attended, out_weight.T, preferred_element_type=jnp.float32)
        live = (text_ids != 0).astype(jnp.float32)
        summed = lax.optimization_barrier(jnp.sum((states + projected).reshape(LAB_GRP, TXT, MODEL_WIDTH) * live[:, :, None], axis=1))
        return (summed / lax.optimization_barrier(jnp.sum(live, axis=1, keepdims=True))).astype(jnp.bfloat16)
    refreshed = lax.map(encode, (grouped, grouped_ids)).reshape(TEXTS, MODEL_WIDTH)
    owners = jnp.arange(TEXTS, dtype=jnp.int32) // REF
    rows = (owners * LAB_OWN + refresh_rows).astype(jnp.int32)
    table = label_table.at[rows].set(refreshed)
    root = math.sqrt(MODEL_WIDTH)
    logits = jnp.dot(queries, table.T, preferred_element_type=jnp.float32) / root
    targets = jnp.zeros((BATCH, LABELS), jnp.float32).at[jnp.arange(BATCH, dtype=jnp.int32)[:, None], positives].set(1.0)
    signs = 2.0 * targets - 1.0
    margin = signs * logits
    balance = (1.0 - focal_beta) / -jnp.expm1(label_counts.astype(jnp.float32) * math.log(focal_beta))
    factor = LABELS / jnp.sum(balance)
    missed = jax.nn.sigmoid(-margin)
    softened = jax.nn.softplus(-margin)
    slopes = (balance[None, :] * signs * (-(missed * missed) * (2.0 * jax.nn.sigmoid(margin) * softened + missed))).astype(jnp.bfloat16)
    label_grad = factor * (jnp.dot(slopes.T, queries, preferred_element_type=jnp.float32) / root)
    query_grad = factor * (jnp.dot(slopes, table, preferred_element_type=jnp.float32) / root)
    loss = factor * jnp.sum(balance[None, :] * missed * missed * softened) / (BATCH * LABELS)
    return (label_grad, query_grad, loss)
```

```python
import math

import jax
import jax.numpy as jnp
from jax import lax
from jax.sharding import Mesh, PartitionSpec as P

HEAD_WIDTH = 128

rope_theta = 1000000.0
norm_eps = 1e-06
focal_beta = 0.9999

AXES = ("z", "y", "xh", "xl", "c")
SIZES = (8, 4, 2, 2, 2)
DP = ("z", "y", "xh")
MP = ("xl", "c")
RING_X = ("xh", "xl")


def rotary(values, head_size):
    length = values.shape[1]
    half = head_size // 2
    frequency = rope_theta ** (-2.0 * jnp.arange(half, dtype=jnp.float32) / head_size)
    angles = jnp.arange(length, dtype=jnp.float32)[:, None] * frequency[None, :]
    cosine = jnp.concatenate([jnp.cos(angles), jnp.cos(angles)], axis=1)[None, :, None, :]
    sine = jnp.concatenate([jnp.sin(angles), jnp.sin(angles)], axis=1)[None, :, None, :]
    turned = jnp.concatenate([-values[..., half:], values[..., :half]], axis=-1)
    return values * cosine + turned * sine


def attend_pooled(query_rows, key_rows, value_rows, text_ids, head_size):
    texts, length = text_ids.shape
    kv_heads = key_rows.shape[1] // head_size
    repeat = query_rows.shape[1] // head_size // kv_heads
    query_r = query_rows.reshape(texts, length, kv_heads, repeat, head_size)
    key_r = key_rows.reshape(texts, length, kv_heads, head_size)
    value_r = value_rows.reshape(texts, length, kv_heads, head_size)
    scores = jnp.einsum(
        "ntgrd,nsgd->ngrts", query_r, key_r, preferred_element_type=jnp.float32
    ) / math.sqrt(head_size)
    causal = jnp.arange(length)[:, None] >= jnp.arange(length)[None, :]
    live = text_ids != 0
    allowed = causal[None, None, None, :, :] & live[:, None, None, None, :]
    weights = jnp.where(allowed, jnp.exp(scores), 0.0)
    probs = weights / jnp.sum(weights, axis=-1, keepdims=True)
    column = jnp.sum(probs * live.astype(jnp.float32)[:, None, None, :, None], axis=3)
    pooled = jnp.sum(column[..., None] * value_r.transpose(0, 2, 1, 3)[:, :, None], axis=3)
    return pooled.reshape(texts, -1)


def shift(x, axis, size, by):
    return lax.ppermute(x, axis, [(i, (i + by) % size) for i in range(size)])


def ring_gather(own, axis, size):
    got = {0: own}
    up, down = own, own
    for step in range(1, (size + 1) // 2):
        up = shift(up, axis, size, -1)
        down = shift(down, axis, size, 1)
        got[step], got[size - step] = up, down
    half = own.shape[0] // 2
    far_a = shift(up[:half], axis, size, -1)
    far_b = shift(down[half:], axis, size, 1)
    got[size // 2] = jnp.concatenate([far_a, far_b], axis=0)
    return [got[d] for d in range(size)]


def in_order(parts, index):
    n = len(parts)
    out = jnp.zeros((n,) + parts[0].shape, parts[0].dtype)
    for d, part in enumerate(parts):
        out = lax.dynamic_update_slice_in_dim(out, part[None], (index + d) % n, 0)
    return out


def spread(x, axes, size):
    return lax.all_to_all(jnp.broadcast_to(x[None], (size,) + x.shape), axes, 0, 0, tiled=True)


def focal(margin):
    missed = jax.nn.sigmoid(-margin)
    softened = jax.nn.softplus(-margin)
    return missed * missed * softened, -(missed * missed) * (
        2.0 * jax.nn.sigmoid(margin) * softened + missed
    )


def shards(
    hidden_states,
    token_ids,
    norm_gain,
    q_weight,
    key_matrix,
    value_matrix,
    out_weight,
    label_table,
    refresh_rows,
    label_counts,
    queries,
    positives,
):
    f32, bf16 = jnp.float32, jnp.bfloat16
    width = hidden_states.shape[1]
    group_tokens = hidden_states.shape[0]
    texts, length = token_ids.shape
    z, y, xh = lax.axis_index("z"), lax.axis_index("y"), lax.axis_index("xh")
    member = lax.axis_index(MP)
    ndp, nmp = 64, 4
    rows = q_weight.shape[0]

    packed = jnp.concatenate([key_matrix, value_matrix, q_weight], axis=1)
    other = shift(packed, "xh", 2, 1)
    pair = jnp.concatenate(
        [jnp.where(xh == 0, packed, other), jnp.where(xh == 0, other, packed)], axis=0
    )
    cut = 512
    part_a, part_b = pair[:, :cut], pair[:, cut:]
    a_y = in_order([part_a] + [shift(part_a, "y", 4, -d) for d in (1, 2, 3)], y)
    b_z = in_order(ring_gather(part_b, "z", 8), z)
    a_all = in_order(ring_gather(a_y, "z", 8), z).reshape(width, cut)
    b_all = in_order(ring_gather(b_z, "y", 4), y)
    b_all = b_all.transpose(1, 0, 2, 3).reshape(width, -1)
    out_all = lax.all_gather(out_weight, ("z", "y"), axis=0, tiled=True)

    balance = (1.0 - focal_beta) / -jnp.expm1(
        label_counts.astype(f32) * math.log(focal_beta)
    )
    owned = label_table.shape[0]
    sums = lax.all_gather(
        jnp.sum(balance.reshape(2, 128), axis=0, keepdims=True), AXES, axis=0, tiled=True
    )
    total_labels = owned * ndp * nmp
    factor = total_labels / jnp.sum(sums)

    root = math.sqrt(width)
    first_label = (lax.axis_index(DP) * nmp + member) * owned
    own_rows = jnp.arange(owned, dtype=jnp.int32)
    chosen = refresh_rows[:, None] == own_rows[None, :]
    kept = ~jnp.any(chosen, axis=0)
    kept_balance = jnp.where(kept, balance, 0.0)
    matched = jnp.any(positives[:, :, None] == (first_label + own_rows)[None, None, :], axis=1)
    signs = jnp.where(matched, 1.0, -1.0)
    logits = (
        lax.dot_general(
            queries, label_table, (((1,), (1,)), ((), ())), preferred_element_type=f32
        )
        / root
    )
    terms, slope = focal(signs * logits)
    kept_loss = jnp.sum(kept_balance[None, :] * terms)
    kept_slopes = (kept_balance[None, :] * signs * slope).astype(bf16)
    kept_query = jnp.dot(kept_slopes, label_table, preferred_element_type=f32)
    new_balance = jnp.sum(jnp.where(chosen, balance[None, :], 0.0), axis=1)
    new_signs = jnp.where(
        jnp.any(positives[:, :, None] == (first_label + refresh_rows)[None, None, :], axis=1),
        1.0,
        -1.0,
    )

    states = hidden_states.astype(f32)
    scaled = lax.rsqrt(jnp.mean(states * states, axis=1, keepdims=True) + norm_eps)
    normed = (states * scaled * norm_gain).astype(bf16)
    live = (token_ids != 0).astype(f32)
    share = texts // nmp
    live_own = lax.dynamic_slice_in_dim(live, member * share, share, 0)
    states_own = lax.dynamic_slice_in_dim(
        hidden_states, member * share * length, share * length, 0
    ).reshape(share, length, width)
    counted = jnp.sum(live_own, axis=1, keepdims=True)
    states_sum = jnp.sum(states_own.astype(f32) * live_own[:, :, None], axis=1)

    raw_a = jnp.dot(normed, a_all, preferred_element_type=f32)
    raw_b = jnp.dot(normed, b_all, preferred_element_type=f32)
    key_raw, value_raw = raw_a[:, :128], raw_a[:, 128:256]
    query_raw = jnp.concatenate([raw_a[:, 256:], raw_b], axis=1)
    queries_rot = (
        rotary(query_raw.reshape(texts, length, -1, HEAD_WIDTH), HEAD_WIDTH)
        .reshape(group_tokens, -1)
        .astype(bf16)
    )
    rotary_keys = (
        rotary(key_raw.reshape(texts, length, -1, HEAD_WIDTH), HEAD_WIDTH)
        .reshape(group_tokens, -1)
        .astype(bf16)
    )
    pooled = attend_pooled(queries_rot, rotary_keys, value_raw, token_ids, HEAD_WIDTH).astype(bf16)

    pooled_other = shift(pooled, "xh", 2, 1)
    both = jnp.concatenate(
        [jnp.where(xh == 0, pooled, pooled_other), jnp.where(xh == 0, pooled_other, pooled)], axis=0
    )
    head_terms = lax.dot_general(
        both, out_all, (((1,), (1,)), ((), ())), preferred_element_type=f32
    )
    exchanged = lax.all_to_all(
        head_terms.reshape(8, share, -1), ("xh", "xl", "c"), 0, 0, tiled=True
    )
    summed = jnp.sum(exchanged.reshape(2, nmp, share, -1), axis=1)
    output_own = (
        summed.reshape(2, share, ndp // 2, rows).transpose(1, 2, 0, 3).reshape(share, width)
    )
    refreshed = ((states_sum + output_own) / counted).astype(bf16)

    new_logits = (
        lax.dot_general(
            queries, refreshed, (((1,), (1,)), ((), ())), preferred_element_type=f32
        )
        / root
    )
    new_terms, new_slope = focal(new_signs * new_logits)
    new_loss = jnp.sum(new_balance[None, :] * new_terms)
    new_slopes = (new_balance[None, :] * new_signs * new_slope).astype(bf16)
    query_part = kept_query + jnp.dot(new_slopes, refreshed, preferred_element_type=f32)
    slopes = kept_slopes + jnp.dot(
        new_slopes, chosen.astype(bf16), preferred_element_type=f32
    ).astype(bf16)
    label_part = lax.dot_general(
        slopes, queries, (((0,), (0,)), ((), ())), preferred_element_type=f32
    )

    batch = queries.shape[0]
    loss_lanes = jnp.full((batch, 128), (kept_loss + new_loss) / batch)
    payload = jnp.concatenate([query_part, loss_lanes], axis=1)
    core = lax.axis_index("c")
    halves = payload.reshape(2, batch // 2, -1)
    mine = lax.dynamic_index_in_dim(halves, core, 0, keepdims=False)
    theirs = lax.dynamic_index_in_dim(halves, 1 - core, 0, keepdims=False)
    part = mine + shift(theirs, "c", 2, 1)
    part = jnp.sum(
        lax.all_to_all(part.reshape(4, batch // 8, -1), "y", 0, 0, tiled=True), axis=0
    )
    part = jnp.sum(
        lax.all_to_all(part.reshape(4, batch // 32, -1), RING_X, 0, 0, tiled=True), axis=0
    )
    part = jnp.sum(spread(part, "z", 8), axis=0)
    part = spread(part, RING_X, 4).reshape(batch // 8, -1)
    part = spread(part, "y", 4).reshape(batch // 2, -1)
    back = shift(part, "c", 2, 1)
    whole = jnp.concatenate(
        [jnp.where(core == 0, part, back), jnp.where(core == 0, back, part)], axis=0
    )
    scale = factor / root
    loss = factor * jnp.sum(whole[:, width]) / (batch * total_labels)
    return (scale * label_part, scale * whole[:, :width], loss)


def solution(mesh):
    grid = Mesh(mesh.devices.reshape(SIZES), AXES)
    in_specs = (
        P(DP, None),
        P(DP, None),
        P(),
        P(DP, MP),
        P(DP, MP),
        P(DP, MP),
        P(DP, MP),
        P(AXES, None),
        P(AXES),
        P(AXES),
        P(),
        P(),
    )
    out_specs = (P(AXES, None), P(), P())
    return jax.shard_map(shards, mesh=grid, in_specs=in_specs, out_specs=out_specs, check_vma=False)
```

```python
import math

import jax
import jax.numpy as jnp
from jax import lax
from jax.sharding import Mesh, PartitionSpec as P

HEAD_WIDTH = 128

rope_theta = 1000000.0
norm_eps = 1e-06
focal_beta = 0.9999

AXES = ("z", "y", "xh", "xl", "c")
SIZES = (8, 4, 2, 2, 2)
DP = ("z", "y", "xh")
MP = ("xl", "c")
RING_X = ("xh", "xl")


def rotary(values, head_size):
    length = values.shape[1]
    half = head_size // 2
    frequency = rope_theta ** (-2.0 * jnp.arange(half, dtype=jnp.float32) / head_size)
    angles = jnp.arange(length, dtype=jnp.float32)[:, None] * frequency[None, :]
    cosine = jnp.concatenate([jnp.cos(angles), jnp.cos(angles)], axis=1)[None, :, None, :]
    sine = jnp.concatenate([jnp.sin(angles), jnp.sin(angles)], axis=1)[None, :, None, :]
    turned = jnp.concatenate([-values[..., half:], values[..., :half]], axis=-1)
    return values * cosine + turned * sine


def attend_pooled(query_rows, key_rows, value_rows, text_ids, head_size):
    texts, length = text_ids.shape
    kv_heads = key_rows.shape[1] // head_size
    repeat = query_rows.shape[1] // head_size // kv_heads
    query_r = query_rows.reshape(texts, length, kv_heads, repeat, head_size)
    key_r = key_rows.reshape(texts, length, kv_heads, head_size)
    value_r = value_rows.reshape(texts, length, kv_heads, head_size)
    scores = jnp.einsum(
        "ntgrd,nsgd->ngrts", query_r, key_r, preferred_element_type=jnp.float32
    ) / math.sqrt(head_size)
    causal = jnp.arange(length)[:, None] >= jnp.arange(length)[None, :]
    live = text_ids != 0
    allowed = causal[None, None, None, :, :] & live[:, None, None, None, :]
    weights = jnp.where(allowed, jnp.exp(scores), 0.0)
    probs = weights / jnp.sum(weights, axis=-1, keepdims=True)
    column = jnp.sum(probs * live.astype(jnp.float32)[:, None, None, :, None], axis=3)
    pooled = jnp.sum(column[..., None] * value_r.transpose(0, 2, 1, 3)[:, :, None], axis=3)
    return pooled.reshape(texts, -1)


def shift(x, axis, size, by):
    return lax.ppermute(x, axis, [(i, (i + by) % size) for i in range(size)])


def swap(x, axis, size, bit):
    return lax.ppermute(x, axis, [(i, i ^ bit) for i in range(size)])


def spread(x, axes, size):
    return lax.all_to_all(jnp.broadcast_to(x[None], (size,) + x.shape), axes, 0, 0, tiled=True)


def focal(margin):
    missed = jax.nn.sigmoid(-margin)
    softened = jax.nn.softplus(-margin)
    return missed * missed * softened, -(missed * missed) * (
        2.0 * jax.nn.sigmoid(margin) * softened + missed
    )


def shards(
    hidden_states,
    token_ids,
    norm_gain,
    q_weight,
    key_matrix,
    value_matrix,
    out_weight,
    label_table,
    refresh_rows,
    label_counts,
    queries,
    positives,
):
    f32, bf16 = jnp.float32, jnp.bfloat16
    width = hidden_states.shape[1]
    group_tokens = hidden_states.shape[0]
    texts, length = token_ids.shape
    xh, core = lax.axis_index("xh"), lax.axis_index("c")
    member = lax.axis_index(MP)
    ndp, nmp = 64, 4
    rows = q_weight.shape[0]

    packed = jnp.concatenate([key_matrix, value_matrix, q_weight, out_weight], axis=1)
    moved = lax.ppermute(
        packed,
        ("xh", "xl", "c"),
        [(4 * h + 2 * l + k, 4 * l + 2 * k + h) for h in (0, 1) for l in (0, 1) for k in (0, 1)],
    )
    cut = packed.shape[1] - out_weight.shape[1]
    in_all = lax.all_gather(moved[:, :cut], ("z", "y"), axis=0, tiled=True)
    out_all = lax.all_gather(moved[:, cut:], ("z", "y"), axis=0, tiled=True)

    balance = (1.0 - focal_beta) / -jnp.expm1(
        label_counts.astype(f32) * math.log(focal_beta)
    )
    owned = label_table.shape[0]
    total = jnp.full((8, 128), jnp.sum(balance))
    for axis, size in zip(AXES[::-1], SIZES[::-1]):
        bit = 1
        while bit < size:
            total = total + swap(total, axis, size, bit)
            bit *= 2
    total_labels = owned * ndp * nmp
    factor = total_labels / total[0, 0]

    root = math.sqrt(width)
    first_label = (lax.axis_index(DP) * nmp + member) * owned
    own_rows = jnp.arange(owned, dtype=jnp.int32)
    chosen = refresh_rows[:, None] == own_rows[None, :]
    kept = ~jnp.any(chosen, axis=0)
    kept_balance = jnp.where(kept, balance, 0.0)
    matched = jnp.any(positives[:, :, None] == (first_label + own_rows)[None, None, :], axis=1)
    signs = jnp.where(matched, 1.0, -1.0)
    logits = (
        lax.dot_general(
            queries, label_table, (((1,), (1,)), ((), ())), preferred_element_type=f32
        )
        / root
    )
    terms, slope = focal(signs * logits)
    kept_loss = jnp.sum(kept_balance[None, :] * terms)
    kept_slopes = (kept_balance[None, :] * signs * slope).astype(bf16)
    kept_query = jnp.dot(kept_slopes, label_table, preferred_element_type=f32)
    new_balance = jnp.sum(jnp.where(chosen, balance[None, :], 0.0), axis=1)
    new_signs = jnp.where(
        jnp.any(positives[:, :, None] == (first_label + refresh_rows)[None, None, :], axis=1),
        1.0,
        -1.0,
    )

    states = hidden_states.astype(f32)
    scaled = lax.rsqrt(jnp.mean(states * states, axis=1, keepdims=True) + norm_eps)
    normed = (states * scaled * norm_gain).astype(bf16)
    live = (token_ids != 0).astype(f32)
    share = texts // nmp
    live_own = lax.dynamic_slice_in_dim(live, member * share, share, 0)
    states_own = lax.dynamic_slice_in_dim(
        hidden_states, member * share * length, share * length, 0
    ).reshape(share, length, width)
    counted = jnp.sum(live_own, axis=1, keepdims=True)
    states_sum = jnp.sum(states_own.astype(f32) * live_own[:, :, None], axis=1)

    half = normed.T.reshape(ndp // 2, 2, rows, group_tokens)
    half = lax.dynamic_index_in_dim(half, core, 1, keepdims=False).reshape(-1, group_tokens)
    facing = [(i, 3 - i) for i in range(4)]
    half_other = lax.ppermute(half, RING_X, facing)
    ids_other = lax.ppermute(token_ids, RING_X, facing)
    keeps = xh == core
    give = jnp.where(keeps, half_other, half)
    keep = jnp.where(keeps, half, half_other)
    ids = jnp.where(keeps, token_ids, ids_other)
    contract = (((0,), (0,)), ((), ()))
    given = lax.dot_general(give, in_all, contract, preferred_element_type=f32)
    taken = shift(given, "c", 2, 1)
    raw = lax.dot_general(keep, in_all, contract, preferred_element_type=f32) + taken
    key_raw, value_raw, query_raw = raw[:, :128], raw[:, 128:256], raw[:, 256:]
    queries_rot = (
        rotary(query_raw.reshape(texts, length, -1, HEAD_WIDTH), HEAD_WIDTH)
        .reshape(group_tokens, -1)
        .astype(bf16)
    )
    rotary_keys = (
        rotary(key_raw.reshape(texts, length, -1, HEAD_WIDTH), HEAD_WIDTH)
        .reshape(group_tokens, -1)
        .astype(bf16)
    )
    pooled = attend_pooled(queries_rot, rotary_keys, value_raw, ids, HEAD_WIDTH).astype(bf16)

    pooled_other = shift(pooled, "c", 2, 1)
    both = jnp.concatenate(
        [jnp.where(core == 0, pooled, pooled_other), jnp.where(core == 0, pooled_other, pooled)],
        axis=0,
    )
    head_terms = lax.dot_general(
        both, out_all, (((1,), (1,)), ((), ())), preferred_element_type=f32
    )
    exchanged = lax.all_to_all(
        head_terms.reshape(8, share, -1), ("xh", "xl", "c"), 0, 0, tiled=True
    )
    summed = jnp.sum(exchanged.reshape(nmp, 2, share, -1), axis=0)
    output_own = (
        summed.reshape(2, share, ndp // 2, rows).transpose(1, 2, 0, 3).reshape(share, width)
    )
    refreshed = ((states_sum + output_own) / counted).astype(bf16)

    new_logits = (
        lax.dot_general(
            queries, refreshed, (((1,), (1,)), ((), ())), preferred_element_type=f32
        )
        / root
    )
    new_terms, new_slope = focal(new_signs * new_logits)
    new_loss = jnp.sum(new_balance[None, :] * new_terms)
    new_slopes = (new_balance[None, :] * new_signs * new_slope).astype(bf16)
    query_part = kept_query + jnp.dot(new_slopes, refreshed, preferred_element_type=f32)
    slopes = kept_slopes + jnp.dot(
        new_slopes, chosen.astype(bf16), preferred_element_type=f32
    ).astype(bf16)
    label_part = lax.dot_general(
        slopes, queries, (((0,), (0,)), ((), ())), preferred_element_type=f32
    )

    batch = queries.shape[0]
    loss_lanes = jnp.full((batch, 128), (kept_loss + new_loss) / batch)
    payload = jnp.concatenate([query_part, loss_lanes], axis=1)
    halves = payload.reshape(2, batch // 2, -1)
    mine = lax.dynamic_index_in_dim(halves, core, 0, keepdims=False)
    theirs = lax.dynamic_index_in_dim(halves, 1 - core, 0, keepdims=False)
    part = mine + shift(theirs, "c", 2, 1)
    part = jnp.sum(
        lax.all_to_all(part.reshape(4, batch // 8, -1), "y", 0, 0, tiled=True), axis=0
    )
    part = jnp.sum(
        lax.all_to_all(part.reshape(4, batch // 32, -1), RING_X, 0, 0, tiled=True), axis=0
    )
    part = jnp.sum(spread(part, "z", 8), axis=0)
    part = spread(part, RING_X, 4).reshape(batch // 8, -1)
    part = spread(part, "y", 4).reshape(batch // 2, -1)
    back = shift(part, "c", 2, 1)
    whole = jnp.concatenate(
        [jnp.where(core == 0, part, back), jnp.where(core == 0, back, part)], axis=0
    )
    scale = factor / root
    loss = factor * jnp.sum(whole[:, width]) / (batch * total_labels)
    return (scale * label_part, scale * whole[:, :width], loss)


def solution(mesh):
    grid = Mesh(mesh.devices.reshape(SIZES), AXES)
    in_specs = (
        P(DP, None),
        P(DP, None),
        P(),
        P(DP, MP),
        P(DP, MP),
        P(DP, MP),
        P(DP, MP),
        P(AXES, None),
        P(AXES),
        P(AXES),
        P(),
        P(),
    )
    out_specs = (P(AXES, None), P(), P())
    return jax.shard_map(shards, mesh=grid, in_specs=in_specs, out_specs=out_specs, check_vma=False)
```

```python
import math

import jax
import jax.numpy as jnp
import numpy as np
from jax import lax
from jax.experimental import pallas as pl
from jax.experimental.pallas import tpu as pltpu
from jax.sharding import Mesh, PartitionSpec as P

HEAD_WIDTH = 128

rope_theta = 1000000.0
norm_eps = 1e-06
focal_beta = 0.9999

AXES = ("z", "y", "xh", "xl", "c")
SIZES = (8, 4, 2, 2, 2)
DP = ("z", "y", "xh")
MP = ("xl", "c")
RING_X = ("xh", "xl")


BLOCK = 128
CUT = 384


def rotary_tables(length):
    half = HEAD_WIDTH // 2
    frequency = rope_theta ** (-2.0 * np.arange(half) / HEAD_WIDTH)
    angles = np.arange(length)[:, None] * frequency[None, :]
    cosine = np.concatenate([np.cos(angles), np.cos(angles)], axis=1)
    sine = np.concatenate([-np.sin(angles), np.sin(angles)], axis=1)
    repeat = BLOCK // length
    return (
        jnp.asarray(np.tile(cosine, (repeat, 1)), jnp.float32),
        jnp.asarray(np.tile(sine, (repeat, 1)), jnp.float32),
    )


def project_kernel(place_ref, whole_ref, part_ref, a_ref, b0_ref, b1_ref, b2a_ref, b2b_ref, b3_ref, out_ref):
    contract = (((0,), (0,)), ((), ()))

    def dot(x, w):
        return lax.dot_general(x, w, contract, preferred_element_type=jnp.float32)

    y = place_ref[0]
    cut = a_ref.shape[1]
    half = b2a_ref.shape[0]
    out_ref[:, :cut] = dot(whole_ref[...], a_ref[...])
    far = part_ref[(y + 2) % 4]
    out_ref[:, cut:] = (
        dot(part_ref[y], b0_ref[...])
        + dot(part_ref[(y + 1) % 4], b1_ref[...])
        + dot(part_ref[(y + 3) % 4], b3_ref[...])
        + dot(far[:half], b2a_ref[...])
        + dot(far[half:], b2b_ref[...])
    )


def project(y, whole, part, a_all, pieces):
    depth, tokens = whole.shape
    columns = a_all.shape[1] + pieces[0].shape[1]
    block = tokens // 2
    fixed = [pl.BlockSpec(w.shape, lambda i, _: (0, 0)) for w in (a_all, *pieces)]
    return pl.pallas_call(
        project_kernel,
        out_shape=jax.ShapeDtypeStruct((tokens, columns), jnp.float32),
        grid_spec=pltpu.PrefetchScalarGridSpec(
            num_scalar_prefetch=1,
            grid=(tokens // block,),
            in_specs=[
                pl.BlockSpec((depth, block), lambda i, _: (0, i)),
                pl.BlockSpec((4, depth // 4, block), lambda i, _: (0, 0, i)),
                *fixed,
            ],
            out_specs=pl.BlockSpec((block, columns), lambda i, _: (i, 0)),
        ),
        compiler_params=pltpu.CompilerParams(vmem_limit_bytes=40 << 20),
        cost_estimate=pl.CostEstimate(
            flops=2 * depth * tokens * columns,
            bytes_accessed=4 * tokens * columns + 2 * depth * (2 * tokens + columns),
            transcendentals=0,
        ),
        name="project",
    )(y.reshape(1).astype(jnp.int32), whole, part, a_all, *pieces)


def attend_kernel(raw_ref, add_ref, allowed_ref, live_ref, member_ref, cos_ref, sin_ref, out_ref):
    width = HEAD_WIDTH
    cosine, sine = cos_ref[...], sin_ref[...]
    members = member_ref[...]
    heads = raw_ref.shape[1] // width - 2
    texts = members.shape[0] // heads

    def rotate(x):
        return (x * cosine + pltpu.roll(x, width // 2, 1) * sine).astype(jnp.bfloat16)

    for block in range(raw_ref.shape[0] // BLOCK):
        rows = slice(block * BLOCK, (block + 1) * BLOCK)

        def column(index):
            lanes = slice(index * width, (index + 1) * width)
            return raw_ref[rows, lanes] + add_ref[rows, lanes]

        allowed = jnp.concatenate([allowed_ref[rows, :]] * heads, axis=0)
        live = jnp.concatenate([live_ref[rows, :]] * heads, axis=0)
        keys = rotate(column(0))
        values = column(1).astype(jnp.bfloat16)
        rotated = jnp.concatenate([rotate(column(h + 2)) for h in range(heads)], axis=0)
        scores = lax.dot_general(
            rotated, keys, (((1,), (1,)), ((), ())), preferred_element_type=jnp.float32
        ) * (1.0 / math.sqrt(width))
        weights = jnp.where(allowed > 0.0, jnp.exp(scores), 0.0)
        total = jnp.sum(weights, axis=1, keepdims=True)
        probs = (weights * (live / total)).astype(jnp.bfloat16)
        shares = jnp.dot(members, probs, preferred_element_type=jnp.float32)
        high = shares.astype(jnp.bfloat16)
        low = (shares - high.astype(jnp.float32)).astype(jnp.bfloat16)
        pooled = jnp.dot(high, values, preferred_element_type=jnp.float32) + jnp.dot(
            low, values, preferred_element_type=jnp.float32
        )
        for head in range(heads):
            out_ref[block * texts : (block + 1) * texts, head * width : (head + 1) * width] = pooled[
                head * texts : (head + 1) * texts
            ]


def attend_pooled(raw, add, text_ids):
    texts, length = text_ids.shape
    tokens, columns = raw.shape
    per = BLOCK // length
    heads = columns // HEAD_WIDTH - 2
    live = (text_ids != 0).reshape(texts // per, BLOCK)
    place = np.arange(BLOCK)
    shape = (place[:, None] // length == place[None, :] // length) & (
        place[:, None] >= place[None, :]
    )
    allowed = (jnp.asarray(shape)[None] & live[:, None, :]).astype(jnp.float32)
    owner = (np.arange(per)[:, None] == place[None, :] // length).astype(np.float32)
    members = jnp.asarray(np.kron(np.eye(heads), owner), jnp.bfloat16)
    cosine, sine = rotary_tables(length)
    step = 2 * BLOCK
    return pl.pallas_call(
        attend_kernel,
        out_shape=jax.ShapeDtypeStruct((texts, heads * HEAD_WIDTH), jnp.float32),
        grid=(tokens // step,),
        in_specs=[
            pl.BlockSpec((step, columns), lambda i: (i, 0)),
            pl.BlockSpec((step, columns), lambda i: (i, 0)),
            pl.BlockSpec((step, BLOCK), lambda i: (i, 0)),
            pl.BlockSpec((step, 1), lambda i: (i, 0)),
            pl.BlockSpec(members.shape, lambda i: (0, 0)),
            pl.BlockSpec((BLOCK, HEAD_WIDTH), lambda i: (0, 0)),
            pl.BlockSpec((BLOCK, HEAD_WIDTH), lambda i: (0, 0)),
        ],
        out_specs=pl.BlockSpec((2 * per, heads * HEAD_WIDTH), lambda i: (i, 0)),
        compiler_params=pltpu.CompilerParams(vmem_limit_bytes=32 << 20),
        cost_estimate=pl.CostEstimate(
            flops=4 * tokens * BLOCK * heads * HEAD_WIDTH,
            bytes_accessed=raw.size * 8,
            transcendentals=tokens * BLOCK * heads,
        ),
        name="attend",
    )(
        raw,
        add,
        allowed.reshape(tokens, BLOCK),
        live.astype(jnp.float32).reshape(tokens, 1),
        members,
        cosine,
        sine,
    )


def shift(x, axis, size, by):
    return lax.ppermute(x, axis, [(i, (i + by) % size) for i in range(size)])


def ring_pieces(own):
    up, down = shift(own, "y", 4, -1), shift(own, "y", 4, 1)
    half = own.shape[0] // 2
    return own, up, shift(up[:half], "y", 4, -1), shift(down[half:], "y", 4, 1), down


def in_order(parts, index):
    n = len(parts)
    out = jnp.zeros((n,) + parts[0].shape, parts[0].dtype)
    for d, part in enumerate(parts):
        out = lax.dynamic_update_slice_in_dim(out, part[None], (index + d) % n, 0)
    return out


def spread(x, axes, size):
    return lax.all_to_all(jnp.broadcast_to(x[None], (size,) + x.shape), axes, 0, 0, tiled=True)


def focal(margin):
    missed = jax.nn.sigmoid(-margin)
    softened = jax.nn.softplus(-margin)
    return missed * missed * softened, -(missed * missed) * (
        2.0 * jax.nn.sigmoid(margin) * softened + missed
    )


def shards(
    hidden_states,
    token_ids,
    norm_gain,
    q_weight,
    key_matrix,
    value_matrix,
    out_weight,
    label_table,
    refresh_rows,
    label_counts,
    queries,
    positives,
):
    f32, bf16 = jnp.float32, jnp.bfloat16
    width = hidden_states.shape[1]
    group_tokens = hidden_states.shape[0]
    texts, length = token_ids.shape
    xh, core = lax.axis_index("xh"), lax.axis_index("c")
    member = lax.axis_index(MP)
    ndp, nmp = 64, 4
    rows = q_weight.shape[0]

    packed = jnp.concatenate([key_matrix, value_matrix, q_weight, out_weight], axis=1)
    moved = lax.ppermute(
        packed,
        ("xh", "xl", "c"),
        [(4 * h + 2 * l + k, 4 * l + 2 * k + h) for h in (0, 1) for l in (0, 1) for k in (0, 1)],
    )
    cut = packed.shape[1] - out_weight.shape[1]
    y = lax.axis_index("y")
    far_z = lax.all_gather(moved[:, CUT:], "z", axis=0, tiled=True)
    part_a = moved[:, :CUT]
    a_y = in_order([part_a] + [shift(part_a, "y", 4, -d) for d in (1, 2, 3)], y)
    a_all = lax.all_gather(a_y.reshape(-1, CUT), "z", axis=0, tiled=True)
    pieces = ring_pieces(far_z[:, : cut - CUT])
    out_pieces = ring_pieces(far_z[:, cut - CUT :])

    balance = (1.0 - focal_beta) / -jnp.expm1(
        label_counts.astype(f32) * math.log(focal_beta)
    )
    owned = label_table.shape[0]
    root = math.sqrt(width)
    first_label = (lax.axis_index(DP) * nmp + member) * owned
    own_rows = jnp.arange(owned, dtype=jnp.int32)
    chosen = refresh_rows[:, None] == own_rows[None, :]
    kept = ~jnp.any(chosen, axis=0)
    kept_balance = jnp.where(kept, balance, 0.0)
    matched = jnp.any(positives[:, :, None] == (first_label + own_rows)[None, None, :], axis=1)
    signs = jnp.where(matched, 1.0, -1.0)
    logits = (
        lax.dot_general(
            queries, label_table, (((1,), (1,)), ((), ())), preferred_element_type=f32
        )
        / root
    )
    terms, slope = focal(signs * logits)
    kept_loss = jnp.sum(kept_balance[None, :] * terms)
    kept_slopes = (kept_balance[None, :] * signs * slope).astype(bf16)
    kept_query = jnp.dot(kept_slopes, label_table, preferred_element_type=f32)
    new_balance = jnp.sum(jnp.where(chosen, balance[None, :], 0.0), axis=1)
    new_signs = jnp.where(
        jnp.any(positives[:, :, None] == (first_label + refresh_rows)[None, None, :], axis=1),
        1.0,
        -1.0,
    )

    states = hidden_states.astype(f32)
    scaled = lax.rsqrt(jnp.mean(states * states, axis=1, keepdims=True) + norm_eps)
    normed = (states * scaled * norm_gain).astype(bf16)
    live = (token_ids != 0).astype(f32)
    share = texts // nmp
    live_own = lax.dynamic_slice_in_dim(live, member * share, share, 0)
    states_own = lax.dynamic_slice_in_dim(
        hidden_states, member * share * length, share * length, 0
    ).reshape(share, length, width)
    counted = jnp.sum(live_own, axis=1, keepdims=True)
    states_sum = jnp.sum(states_own.astype(f32) * live_own[:, :, None], axis=1)

    half = normed.T.reshape(ndp // 2, 2, rows, group_tokens)
    half = lax.dynamic_index_in_dim(half, core, 1, keepdims=False).reshape(-1, group_tokens)
    facing = [(i, 3 - i) for i in range(4)]
    half_other = lax.ppermute(half, RING_X, facing)
    ids_other = lax.ppermute(token_ids, RING_X, facing)
    keeps = xh == core
    give = jnp.where(keeps, half_other, half)
    keep = jnp.where(keeps, half, half_other)
    ids = jnp.where(keeps, token_ids, ids_other)

    def by_y(block):
        return block.reshape(8, 4, rows, -1).transpose(1, 0, 2, 3).reshape(4, 8 * rows, -1)

    taken = shift(project(y, give, by_y(give), a_all, pieces), "c", 2, 1)
    raw = project(y, keep, by_y(keep), a_all, pieces)
    pooled = attend_pooled(raw, taken, ids).astype(bf16)

    pooled_other = shift(pooled, "c", 2, 1)
    both = jnp.concatenate(
        [jnp.where(core == 0, pooled, pooled_other), jnp.where(core == 0, pooled_other, pooled)],
        axis=0,
    )
    out_all = jnp.concatenate(out_pieces, axis=0)
    head_terms = lax.dot_general(
        both, out_all, (((1,), (1,)), ((), ())), preferred_element_type=f32
    )
    blocks = head_terms.reshape(8, share, 4, 8 * rows)
    turned = jnp.concatenate([blocks, blocks], axis=2)
    head_terms = lax.dynamic_slice_in_dim(turned, 4 - y, 4, 2)
    exchanged = lax.all_to_all(
        head_terms.reshape(8, share, -1), ("xh", "xl", "c"), 0, 0, tiled=True
    )
    summed = jnp.sum(exchanged.reshape(nmp, 2, share, -1), axis=0)
    output_own = (
        summed.reshape(2, share, 4, 8, rows).transpose(1, 3, 2, 0, 4).reshape(share, width)
    )
    refreshed = ((states_sum + output_own) / counted).astype(bf16)

    new_logits = (
        lax.dot_general(
            queries, refreshed, (((1,), (1,)), ((), ())), preferred_element_type=f32
        )
        / root
    )
    new_terms, new_slope = focal(new_signs * new_logits)
    new_loss = jnp.sum(new_balance[None, :] * new_terms)
    new_slopes = (new_balance[None, :] * new_signs * new_slope).astype(bf16)
    query_part = kept_query + jnp.dot(new_slopes, refreshed, preferred_element_type=f32)
    slopes = kept_slopes + jnp.dot(
        new_slopes, chosen.astype(bf16), preferred_element_type=f32
    ).astype(bf16)
    label_part = lax.dot_general(
        slopes, queries, (((0,), (0,)), ((), ())), preferred_element_type=f32
    )

    batch = queries.shape[0]
    extra = jnp.stack([kept_loss + new_loss, jnp.sum(balance)]) / batch
    lanes = jnp.broadcast_to(jnp.repeat(extra, 64)[None, :], (batch, 128))
    payload = jnp.concatenate([query_part, lanes], axis=1)
    near = ("y", "xh", "xl", "c")
    part = jnp.sum(
        lax.all_to_all(payload.reshape(32, batch // 32, -1), near, 0, 0, tiled=True), axis=0
    )
    part = jnp.sum(spread(part, "z", 8), axis=0)
    whole = spread(part, near, 32).reshape(batch, -1)
    sums = jnp.sum(whole[:, width:], axis=0)
    total_labels = owned * ndp * nmp
    factor = total_labels / sums[64]
    scale = factor / root
    loss = factor * sums[0] / (batch * total_labels)
    return (scale * label_part, scale * whole[:, :width], loss)


def solution(mesh):
    grid = Mesh(mesh.devices.reshape(SIZES), AXES)
    in_specs = (
        P(DP, None),
        P(DP, None),
        P(),
        P(DP, MP),
        P(DP, MP),
        P(DP, MP),
        P(DP, MP),
        P(AXES, None),
        P(AXES),
        P(AXES),
        P(),
        P(),
    )
    out_specs = (P(AXES, None), P(), P())
    return jax.shard_map(shards, mesh=grid, in_specs=in_specs, out_specs=out_specs, check_vma=False)
```

```python
import math

import jax
import jax.numpy as jnp
import numpy as np
from jax import lax
from jax.experimental import pallas as pl
from jax.experimental.pallas import tpu as pltpu
from jax.sharding import Mesh, PartitionSpec as P

HEAD_WIDTH = 128

rope_theta = 1000000.0
norm_eps = 1e-06
focal_beta = 0.9999

AXES = ("z", "y", "xh", "xl", "c")
SIZES = (8, 4, 2, 2, 2)
DP = ("z", "y", "xh")
MP = ("xl", "c")
RING_X = ("xh", "xl")


BLOCK = 128
CUT = 256
HALF = 1920


def rotary_tables(length):
    half = HEAD_WIDTH // 2
    frequency = rope_theta ** (-2.0 * np.arange(half) / HEAD_WIDTH)
    angles = np.arange(length)[:, None] * frequency[None, :]
    cosine = np.concatenate([np.cos(angles), np.cos(angles)], axis=1)
    sine = np.concatenate([-np.sin(angles), np.sin(angles)], axis=1)
    repeat = BLOCK // length
    return (
        jnp.asarray(np.tile(cosine, (repeat, 1)), jnp.float32),
        jnp.asarray(np.tile(sine, (repeat, 1)), jnp.float32),
    )


def project_kernel(place_ref, whole_ref, part_ref, a_ref, b0_ref, b1_ref, b2a_ref, b2b_ref, b3_ref, out_ref):
    contract = (((0,), (0,)), ((), ()))

    def dot(x, w):
        return lax.dot_general(x, w, contract, preferred_element_type=jnp.float32)

    y = place_ref[0]
    cut = a_ref.shape[1]
    half = b2a_ref.shape[0]
    out_ref[:, :cut] = dot(whole_ref[...], a_ref[...])
    far = part_ref[(y + 2) % 4]
    out_ref[:, cut:] = (
        dot(part_ref[y], b0_ref[...])
        + dot(part_ref[(y + 1) % 4], b1_ref[...])
        + dot(part_ref[(y + 3) % 4], b3_ref[...])
        + dot(far[:half], b2a_ref[...])
        + dot(far[half:], b2b_ref[...])
    )


def project(y, whole, part, a_all, pieces):
    depth, tokens = whole.shape
    columns = a_all.shape[1] + pieces[0].shape[1]
    block = tokens // 2
    fixed = [pl.BlockSpec(w.shape, lambda i, _: (0, 0)) for w in (a_all, *pieces)]
    return pl.pallas_call(
        project_kernel,
        out_shape=jax.ShapeDtypeStruct((tokens, columns), jnp.float32),
        grid_spec=pltpu.PrefetchScalarGridSpec(
            num_scalar_prefetch=1,
            grid=(tokens // block,),
            in_specs=[
                pl.BlockSpec((depth, block), lambda i, _: (0, i)),
                pl.BlockSpec((4, depth // 4, block), lambda i, _: (0, 0, i)),
                *fixed,
            ],
            out_specs=pl.BlockSpec((block, columns), lambda i, _: (i, 0)),
        ),
        compiler_params=pltpu.CompilerParams(vmem_limit_bytes=40 << 20),
        cost_estimate=pl.CostEstimate(
            flops=2 * depth * tokens * columns,
            bytes_accessed=4 * tokens * columns + 2 * depth * (2 * tokens + columns),
            transcendentals=0,
        ),
        name="project",
    )(y.reshape(1).astype(jnp.int32), whole, part, a_all, *pieces)


def attend_kernel(raw_ref, add_ref, allowed_ref, live_ref, member_ref, cos_ref, sin_ref, out_ref):
    width = HEAD_WIDTH
    cosine, sine = cos_ref[...], sin_ref[...]
    members = member_ref[...]
    heads = raw_ref.shape[1] // width - 2
    texts = members.shape[0] // heads

    def rotate(x):
        return (x * cosine + pltpu.roll(x, width // 2, 1) * sine).astype(jnp.bfloat16)

    for block in range(raw_ref.shape[0] // BLOCK):
        rows = slice(block * BLOCK, (block + 1) * BLOCK)

        def column(index):
            lanes = slice(index * width, (index + 1) * width)
            return raw_ref[rows, lanes] + add_ref[rows, lanes]

        allowed = jnp.concatenate([allowed_ref[rows, :]] * heads, axis=0)
        live = jnp.concatenate([live_ref[rows, :]] * heads, axis=0)
        keys = rotate(column(0))
        values = column(1).astype(jnp.bfloat16)
        rotated = jnp.concatenate([rotate(column(h + 2)) for h in range(heads)], axis=0)
        scores = lax.dot_general(
            rotated, keys, (((1,), (1,)), ((), ())), preferred_element_type=jnp.float32
        ) * (1.0 / math.sqrt(width))
        weights = jnp.where(allowed > 0.0, jnp.exp(scores), 0.0)
        total = jnp.sum(weights, axis=1, keepdims=True)
        probs = (weights * (live / total)).astype(jnp.bfloat16)
        shares = jnp.dot(members, probs, preferred_element_type=jnp.float32)
        high = shares.astype(jnp.bfloat16)
        low = (shares - high.astype(jnp.float32)).astype(jnp.bfloat16)
        pooled = jnp.dot(high, values, preferred_element_type=jnp.float32) + jnp.dot(
            low, values, preferred_element_type=jnp.float32
        )
        for head in range(heads):
            out_ref[block * texts : (block + 1) * texts, head * width : (head + 1) * width] = pooled[
                head * texts : (head + 1) * texts
            ]


def attend_tables(text_ids):
    texts, length = text_ids.shape
    per = BLOCK // length
    live = (text_ids != 0).reshape(texts // per, BLOCK)
    place = np.arange(BLOCK)
    shape = (place[:, None] // length == place[None, :] // length) & (
        place[:, None] >= place[None, :]
    )
    allowed = (jnp.asarray(shape)[None] & live[:, None, :]).astype(jnp.float32)
    return allowed.reshape(-1, BLOCK), (text_ids != 0).astype(jnp.float32).reshape(-1, 1)


def attend_pooled(raw, add, allowed, live, length):
    tokens, columns = raw.shape
    texts = tokens // length
    per = BLOCK // length
    heads = columns // HEAD_WIDTH - 2
    owner = (np.arange(per)[:, None] == np.arange(BLOCK)[None, :] // length).astype(np.float32)
    members = jnp.asarray(np.kron(np.eye(heads), owner), jnp.bfloat16)
    cosine, sine = rotary_tables(length)
    step = 2 * BLOCK
    return pl.pallas_call(
        attend_kernel,
        out_shape=jax.ShapeDtypeStruct((texts, heads * HEAD_WIDTH), jnp.float32),
        grid=(tokens // step,),
        in_specs=[
            pl.BlockSpec((step, columns), lambda i: (i, 0)),
            pl.BlockSpec((step, columns), lambda i: (i, 0)),
            pl.BlockSpec((step, BLOCK), lambda i: (i, 0)),
            pl.BlockSpec((step, 1), lambda i: (i, 0)),
            pl.BlockSpec(members.shape, lambda i: (0, 0)),
            pl.BlockSpec((BLOCK, HEAD_WIDTH), lambda i: (0, 0)),
            pl.BlockSpec((BLOCK, HEAD_WIDTH), lambda i: (0, 0)),
        ],
        out_specs=pl.BlockSpec((2 * per, heads * HEAD_WIDTH), lambda i: (i, 0)),
        compiler_params=pltpu.CompilerParams(vmem_limit_bytes=32 << 20),
        cost_estimate=pl.CostEstimate(
            flops=4 * tokens * BLOCK * heads * HEAD_WIDTH,
            bytes_accessed=raw.size * 8,
            transcendentals=tokens * BLOCK * heads,
        ),
        name="attend",
    )(
        raw,
        add,
        allowed,
        live,
        members,
        cosine,
        sine,
    )


def shift(x, axis, size, by):
    return lax.ppermute(x, axis, [(i, (i + by) % size) for i in range(size)])


def ring_pieces(own):
    up, down = shift(own, "y", 4, -1), shift(own, "y", 4, 1)
    half = own.shape[0] // 2
    return own, up, shift(up[:half], "y", 4, -1), shift(down[half:], "y", 4, 1), down


def in_order(parts, index):
    n = len(parts)
    out = jnp.zeros((n,) + parts[0].shape, parts[0].dtype)
    for d, part in enumerate(parts):
        out = lax.dynamic_update_slice_in_dim(out, part[None], (index + d) % n, 0)
    return out


def spread(x, axes, size):
    return lax.all_to_all(jnp.broadcast_to(x[None], (size,) + x.shape), axes, 0, 0, tiled=True)


def focal(margin):
    missed = jax.nn.sigmoid(-margin)
    softened = jnp.maximum(-margin, 0.0) + jnp.log1p(jnp.exp(-jnp.abs(margin)))
    return missed * missed * softened, -(missed * missed) * (
        2.0 * jax.nn.sigmoid(margin) * softened + missed
    )


def tail_kernel(core_ref, sums_ref, new_ref, queries_ref, kept_ref, signs_ref, balance_ref, mine_ref, theirs_ref, slopes_ref):
    batch, width = queries_ref.shape
    rows = new_ref[...]
    logits = lax.dot_general(
        queries_ref[...], rows, (((1,), (1,)), ((), ())), preferred_element_type=jnp.float32
    ) / math.sqrt(width)
    signs = signs_ref[...]
    balance = balance_ref[...]
    terms, slope = focal(signs * logits)
    losses = jnp.sum(balance * terms, axis=1, keepdims=True) + sums_ref[0] / batch
    slopes = (balance * signs * slope).astype(jnp.bfloat16)
    slopes_ref[...] = slopes.astype(jnp.float32)
    left = kept_ref[:, :HALF] + jnp.dot(slopes, rows[:, :HALF], preferred_element_type=jnp.float32)
    right = kept_ref[:, HALF:] + jnp.dot(slopes, rows[:, HALF:], preferred_element_type=jnp.float32)
    rest = width - HALF
    lanes = (2 * HALF - width) // 2
    loss_lanes = jnp.broadcast_to(losses, (batch, lanes))
    class_lanes = jnp.full((batch, lanes), sums_ref[1] / batch, jnp.float32)

    def write(first, second):
        first[...] = left
        second[:, :rest] = right
        second[:, rest : rest + lanes] = loss_lanes
        second[:, rest + lanes :] = class_lanes

    @pl.when(core_ref[0] == 0)
    def _():
        write(mine_ref, theirs_ref)

    @pl.when(core_ref[0] != 0)
    def _():
        write(theirs_ref, mine_ref)


def tail(core, sums, rows, queries, kept, signs, balance):
    batch, width = queries.shape
    smem = pl.BlockSpec(memory_space=pltpu.SMEM)
    vmem = pl.BlockSpec(memory_space=pltpu.VMEM)
    half = jax.ShapeDtypeStruct((batch, HALF), jnp.float32)
    return pl.pallas_call(
        tail_kernel,
        out_shape=(half, half, jax.ShapeDtypeStruct((batch, rows.shape[0]), jnp.float32)),
        in_specs=[smem, smem, vmem, vmem, vmem, vmem, vmem],
        out_specs=(vmem, vmem, vmem),
        compiler_params=pltpu.CompilerParams(vmem_limit_bytes=24 << 20),
        cost_estimate=pl.CostEstimate(
            flops=4 * batch * width * rows.shape[0],
            bytes_accessed=10 * batch * width,
            transcendentals=8 * batch,
        ),
        name="tail",
    )(core.reshape(1).astype(jnp.int32), sums, rows, queries, kept, signs, balance)


def shards(
    hidden_states,
    token_ids,
    norm_gain,
    q_weight,
    key_matrix,
    value_matrix,
    out_weight,
    label_table,
    refresh_rows,
    label_counts,
    queries,
    positives,
):
    f32, bf16 = jnp.float32, jnp.bfloat16
    width = hidden_states.shape[1]
    group_tokens = hidden_states.shape[0]
    texts, length = token_ids.shape
    xh, core = lax.axis_index("xh"), lax.axis_index("c")
    member = lax.axis_index(MP)
    ndp, nmp = 64, 4
    rows = q_weight.shape[0]

    packed = jnp.concatenate([key_matrix, value_matrix, q_weight, out_weight], axis=1)
    moved = lax.ppermute(
        packed,
        ("xh", "xl", "c"),
        [(4 * h + 2 * l + k, 4 * l + 2 * k + h) for h in (0, 1) for l in (0, 1) for k in (0, 1)],
    )
    cut = packed.shape[1] - out_weight.shape[1]
    y = lax.axis_index("y")
    far_z = lax.all_gather(moved[:, CUT:], "z", axis=0, tiled=True)
    part_a = moved[:, :CUT]
    a_y = in_order([part_a] + [shift(part_a, "y", 4, -d) for d in (1, 2, 3)], y)
    a_all = lax.all_gather(a_y.reshape(-1, CUT), "z", axis=0, tiled=True)
    pieces = ring_pieces(far_z[:, : cut - CUT])
    out_pieces = ring_pieces(far_z[:, cut - CUT :])

    balance = (1.0 - focal_beta) / -jnp.expm1(
        label_counts.astype(f32) * math.log(focal_beta)
    )
    owned = label_table.shape[0]
    root = math.sqrt(width)
    first_label = (lax.axis_index(DP) * nmp + member) * owned
    own_rows = jnp.arange(owned, dtype=jnp.int32)
    chosen = refresh_rows[:, None] == own_rows[None, :]
    kept = ~jnp.any(chosen, axis=0)
    kept_balance = jnp.where(kept, balance, 0.0)
    matched = jnp.any(positives[:, :, None] == (first_label + own_rows)[None, None, :], axis=1)
    signs = jnp.where(matched, 1.0, -1.0)
    logits = (
        lax.dot_general(
            queries, label_table, (((1,), (1,)), ((), ())), preferred_element_type=f32
        )
        / root
    )
    terms, slope = focal(signs * logits)
    kept_loss = jnp.sum(kept_balance[None, :] * terms)
    kept_slopes = (kept_balance[None, :] * signs * slope).astype(bf16)
    kept_query = jnp.dot(kept_slopes, label_table, preferred_element_type=f32)
    new_balance = jnp.sum(jnp.where(chosen, balance[None, :], 0.0), axis=1)
    new_signs = jnp.where(
        jnp.any(positives[:, :, None] == (first_label + refresh_rows)[None, None, :], axis=1),
        1.0,
        -1.0,
    )

    states = hidden_states.astype(f32)
    scaled = lax.rsqrt(jnp.mean(states * states, axis=1, keepdims=True) + norm_eps)
    normed = (states * scaled * norm_gain).astype(bf16)
    live = (token_ids != 0).astype(f32)
    share = texts // nmp
    live_own = lax.dynamic_slice_in_dim(live, member * share, share, 0)
    states_own = lax.dynamic_slice_in_dim(
        hidden_states, member * share * length, share * length, 0
    ).reshape(share, length, width)
    counted = jnp.sum(live_own, axis=1, keepdims=True)
    states_sum = jnp.sum(states_own.astype(f32) * live_own[:, :, None], axis=1)

    half = normed.T.reshape(ndp // 2, 2, rows, group_tokens)
    half = lax.dynamic_index_in_dim(half, core, 1, keepdims=False).reshape(-1, group_tokens)
    facing = [(i, 3 - i) for i in range(4)]
    half_other = lax.ppermute(half, RING_X, facing)
    ids_other = lax.ppermute(token_ids, RING_X, facing)
    keeps = xh == core
    give = jnp.where(keeps, half_other, half)
    keep = jnp.where(keeps, half, half_other)
    ids = jnp.where(keeps, token_ids, ids_other)

    def by_y(block):
        return block.reshape(8, 4, rows, -1).transpose(1, 0, 2, 3).reshape(4, 8 * rows, -1)

    allowed, live_rows = attend_tables(ids)
    sums = jnp.stack([kept_loss, jnp.sum(balance)])
    early = (kept_query, kept_slopes, sums, new_balance, new_signs, chosen, states_sum, counted)
    early = early + (allowed, live_rows, give, keep, by_y(give), by_y(keep))
    (a_all, pieces, early) = lax.optimization_barrier((a_all, pieces, early))
    kept_query, kept_slopes, sums, new_balance, new_signs, chosen, states_sum, counted = early[:8]
    allowed, live_rows, give, keep, give_y, keep_y = early[8:]
    taken = shift(project(y, give, give_y, a_all, pieces), "c", 2, 1)
    raw = project(y, keep, keep_y, a_all, pieces)
    pooled = attend_pooled(raw, taken, allowed, live_rows, length).astype(bf16)

    pooled_other = shift(pooled, "c", 2, 1)
    both = jnp.concatenate(
        [jnp.where(core == 0, pooled, pooled_other), jnp.where(core == 0, pooled_other, pooled)],
        axis=0,
    )
    out_all = jnp.concatenate(out_pieces, axis=0)
    head_terms = lax.dot_general(
        both, out_all, (((1,), (1,)), ((), ())), preferred_element_type=f32
    )
    exchanged = lax.all_to_all(
        head_terms.reshape(8, share, -1), ("xh", "xl", "c"), 0, 0, tiled=True
    )
    summed = jnp.sum(exchanged.reshape(nmp, 2, share, -1), axis=0)
    blocks = summed.reshape(2, share, 4, 8 * rows)
    turned = lax.dynamic_slice_in_dim(jnp.concatenate([blocks, blocks], axis=2), 4 - y, 4, 2)
    output_own = (
        turned.reshape(2, share, 4, 8, rows).transpose(1, 3, 2, 0, 4).reshape(share, width)
    )
    refreshed = ((states_sum + output_own) / counted).astype(bf16)

    mine, theirs, new_slopes = tail(
        core, sums, refreshed, queries, kept_query, new_signs, new_balance[None, :]
    )
    slopes = kept_slopes + jnp.dot(
        new_slopes.astype(bf16), chosen.astype(bf16), preferred_element_type=f32
    ).astype(bf16)
    label_part = lax.dot_general(
        slopes, queries, (((0,), (0,)), ((), ())), preferred_element_type=f32
    )

    batch = queries.shape[0]
    near = ("y", "xh", "xl")
    part = mine + shift(theirs, "c", 2, 1)
    part = jnp.sum(
        lax.all_to_all(part.reshape(16, batch // 16, HALF), near, 0, 0, tiled=True), axis=0
    )
    part = jnp.sum(spread(part, "z", 8), axis=0)
    part = spread(part, near, 16).reshape(batch, HALF)
    back = shift(part, "c", 2, 1)
    left = jnp.where(core == 0, part, back)
    right = jnp.where(core == 0, back, part)
    rest = width - HALF
    lanes = (2 * HALF - width) // 2
    total_labels = owned * ndp * nmp
    factor = total_labels / jnp.sum(right[:, rest + lanes])
    scale = factor / root
    loss = factor * jnp.sum(right[:, rest]) / (batch * total_labels)
    query_grad = scale * jnp.concatenate([left, right[:, :rest]], axis=1)
    return (scale * label_part, query_grad, loss)


def solution(mesh):
    grid = Mesh(mesh.devices.reshape(SIZES), AXES)
    in_specs = (
        P(DP, None),
        P(DP, None),
        P(),
        P(DP, MP),
        P(DP, MP),
        P(DP, MP),
        P(DP, MP),
        P(AXES, None),
        P(AXES),
        P(AXES),
        P(),
        P(),
    )
    out_specs = (P(AXES, None), P(), P())
    return jax.shard_map(shards, mesh=grid, in_specs=in_specs, out_specs=out_specs, check_vma=False)
```

```python
import functools
import math

import jax
import jax.numpy as jnp
import numpy as np
from jax import lax
from jax.experimental import pallas as pl
from jax.experimental.pallas import tpu as pltpu
from jax.sharding import Mesh, PartitionSpec as P

HEAD_WIDTH = 128

rope_theta = 1000000.0
norm_eps = 1e-06
focal_beta = 0.9999

AXES = ("z", "y", "xh", "xl", "c")
SIZES = (8, 4, 2, 2, 2)
DP = ("z", "y", "xh")
MP = ("xl", "c")
RING_X = ("xh", "xl")


BLOCK = 128
CUT = 384
HALF = 1920


def rotary_tables(length):
    half = HEAD_WIDTH // 2
    frequency = rope_theta ** (-2.0 * np.arange(half) / HEAD_WIDTH)
    angles = np.arange(length)[:, None] * frequency[None, :]
    cosine = np.concatenate([np.cos(angles), np.cos(angles)], axis=1)
    sine = np.concatenate([-np.sin(angles), np.sin(angles)], axis=1)
    repeat = BLOCK // length
    return (
        jnp.asarray(np.tile(cosine, (repeat, 1)), jnp.float32),
        jnp.asarray(np.tile(sine, (repeat, 1)), jnp.float32),
    )


def project_kernel(place_ref, whole_ref, part_ref, a_ref, b0_ref, b1_ref, b2a_ref, b2b_ref, b3_ref, out_ref):
    contract = (((0,), (0,)), ((), ()))

    def dot(x, w):
        return lax.dot_general(x, w, contract, preferred_element_type=jnp.float32)

    y = place_ref[0]
    cut = a_ref.shape[1]
    half = b2a_ref.shape[0]
    out_ref[:, :cut] = dot(whole_ref[...], a_ref[...])
    far = part_ref[(y + 2) % 4]
    out_ref[:, cut:] = (
        dot(part_ref[y], b0_ref[...])
        + dot(part_ref[(y + 1) % 4], b1_ref[...])
        + dot(part_ref[(y + 3) % 4], b3_ref[...])
        + dot(far[:half], b2a_ref[...])
        + dot(far[half:], b2b_ref[...])
    )


def project(y, whole, part, a_all, pieces):
    depth, tokens = whole.shape
    columns = a_all.shape[1] + pieces[0].shape[1]
    block = tokens // 2
    fixed = [pl.BlockSpec(w.shape, lambda i, _: (0, 0)) for w in (a_all, *pieces)]
    return pl.pallas_call(
        project_kernel,
        out_shape=jax.ShapeDtypeStruct((tokens, columns), jnp.float32),
        grid_spec=pltpu.PrefetchScalarGridSpec(
            num_scalar_prefetch=1,
            grid=(tokens // block,),
            in_specs=[
                pl.BlockSpec((depth, block), lambda i, _: (0, i)),
                pl.BlockSpec((4, depth // 4, block), lambda i, _: (0, 0, i)),
                *fixed,
            ],
            out_specs=pl.BlockSpec((block, columns), lambda i, _: (i, 0)),
        ),
        compiler_params=pltpu.CompilerParams(vmem_limit_bytes=56 << 20),
        cost_estimate=pl.CostEstimate(
            flops=2 * depth * tokens * columns,
            bytes_accessed=4 * tokens * columns + 2 * depth * (2 * tokens + columns),
            transcendentals=0,
        ),
        name="project",
    )(y.reshape(1).astype(jnp.int32), whole, part, a_all, *pieces)


def attend_kernel(raw_ref, add_ref, allowed_ref, live_ref, member_ref, cos_ref, sin_ref, out_ref):
    width = HEAD_WIDTH
    cosine, sine = cos_ref[...], sin_ref[...]
    members = member_ref[...]
    heads = raw_ref.shape[1] // width - 2
    texts = members.shape[0] // heads

    def rotate(x):
        return (x * cosine + pltpu.roll(x, width // 2, 1) * sine).astype(jnp.bfloat16)

    for block in range(raw_ref.shape[0] // BLOCK):
        rows = slice(block * BLOCK, (block + 1) * BLOCK)

        def column(index):
            lanes = slice(index * width, (index + 1) * width)
            return raw_ref[rows, lanes] + add_ref[rows, lanes]

        allowed = jnp.concatenate([allowed_ref[rows, :]] * heads, axis=0)
        live = jnp.concatenate([live_ref[rows, :]] * heads, axis=0)
        keys = rotate(column(0))
        values = column(1).astype(jnp.bfloat16)
        rotated = jnp.concatenate([rotate(column(h + 2)) for h in range(heads)], axis=0)
        scores = lax.dot_general(
            rotated, keys, (((1,), (1,)), ((), ())), preferred_element_type=jnp.float32
        ) * (1.0 / math.sqrt(width))
        weights = jnp.where(allowed > 0.0, jnp.exp(scores), 0.0)
        total = jnp.sum(weights, axis=1, keepdims=True)
        probs = (weights * (live / total)).astype(jnp.bfloat16)
        shares = jnp.dot(members, probs, preferred_element_type=jnp.float32)
        high = shares.astype(jnp.bfloat16)
        low = (shares - high.astype(jnp.float32)).astype(jnp.bfloat16)
        pooled = jnp.dot(high, values, preferred_element_type=jnp.float32) + jnp.dot(
            low, values, preferred_element_type=jnp.float32
        )
        for head in range(heads):
            out_ref[block * texts : (block + 1) * texts, head * width : (head + 1) * width] = pooled[
                head * texts : (head + 1) * texts
            ]


def attend_tables(text_ids):
    texts, length = text_ids.shape
    per = BLOCK // length
    live = (text_ids != 0).reshape(texts // per, BLOCK)
    place = np.arange(BLOCK)
    shape = (place[:, None] // length == place[None, :] // length) & (
        place[:, None] >= place[None, :]
    )
    allowed = (jnp.asarray(shape)[None] & live[:, None, :]).astype(jnp.float32)
    return allowed.reshape(-1, BLOCK), (text_ids != 0).astype(jnp.float32).reshape(-1, 1)


def attend_pooled(raw, add, allowed, live, length):
    tokens, columns = raw.shape
    texts = tokens // length
    per = BLOCK // length
    heads = columns // HEAD_WIDTH - 2
    owner = (np.arange(per)[:, None] == np.arange(BLOCK)[None, :] // length).astype(np.float32)
    members = jnp.asarray(np.kron(np.eye(heads), owner), jnp.bfloat16)
    cosine, sine = rotary_tables(length)
    step = 2 * BLOCK
    return pl.pallas_call(
        attend_kernel,
        out_shape=jax.ShapeDtypeStruct((texts, heads * HEAD_WIDTH), jnp.float32),
        grid=(tokens // step,),
        in_specs=[
            pl.BlockSpec((step, columns), lambda i: (i, 0)),
            pl.BlockSpec((step, columns), lambda i: (i, 0)),
            pl.BlockSpec((step, BLOCK), lambda i: (i, 0)),
            pl.BlockSpec((step, 1), lambda i: (i, 0)),
            pl.BlockSpec(members.shape, lambda i: (0, 0)),
            pl.BlockSpec((BLOCK, HEAD_WIDTH), lambda i: (0, 0)),
            pl.BlockSpec((BLOCK, HEAD_WIDTH), lambda i: (0, 0)),
        ],
        out_specs=pl.BlockSpec((2 * per, heads * HEAD_WIDTH), lambda i: (i, 0)),
        compiler_params=pltpu.CompilerParams(vmem_limit_bytes=56 << 20),
        cost_estimate=pl.CostEstimate(
            flops=4 * tokens * BLOCK * heads * HEAD_WIDTH,
            bytes_accessed=raw.size * 8,
            transcendentals=tokens * BLOCK * heads,
        ),
        name="attend",
    )(
        raw,
        add,
        allowed,
        live,
        members,
        cosine,
        sine,
    )


def shift(x, axis, size, by):
    return lax.ppermute(x, axis, [(i, (i + by) % size) for i in range(size)])


def ring_near(own):
    return shift(own, "y", 4, -1), shift(own, "y", 4, 1)


def ring_far(up, down):
    half = up.shape[0] // 2
    return shift(up[:half], "y", 4, -1), shift(down[half:], "y", 4, 1)


def in_order(parts, index):
    n = len(parts)
    out = jnp.zeros((n,) + parts[0].shape, parts[0].dtype)
    for d, part in enumerate(parts):
        out = lax.dynamic_update_slice_in_dim(out, part[None], (index + d) % n, 0)
    return out


def spread(x, axes, size):
    return lax.all_to_all(jnp.broadcast_to(x[None], (size,) + x.shape), axes, 0, 0, tiled=True)


def focal(margin):
    missed = jax.nn.sigmoid(-margin)
    softened = jnp.maximum(-margin, 0.0) + jnp.log1p(jnp.exp(-jnp.abs(margin)))
    return missed * missed * softened, -(missed * missed) * (
        2.0 * jax.nn.sigmoid(margin) * softened + missed
    )


def tail_kernel(core_ref, sums_ref, new_ref, queries_ref, kept_ref, signs_ref, balance_ref, mine_ref, theirs_ref, slopes_ref):
    batch, width = queries_ref.shape
    rows = new_ref[...]
    logits = lax.dot_general(
        queries_ref[...], rows, (((1,), (1,)), ((), ())), preferred_element_type=jnp.float32
    ) / math.sqrt(width)
    signs = signs_ref[...]
    balance = balance_ref[...]
    terms, slope = focal(signs * logits)
    losses = jnp.sum(balance * terms, axis=1, keepdims=True) + sums_ref[0] / batch
    slopes = (balance * signs * slope).astype(jnp.bfloat16)
    slopes_ref[...] = slopes.astype(jnp.float32)
    left = kept_ref[:, :HALF] + jnp.dot(slopes, rows[:, :HALF], preferred_element_type=jnp.float32)
    right = kept_ref[:, HALF:] + jnp.dot(slopes, rows[:, HALF:], preferred_element_type=jnp.float32)
    rest = width - HALF
    lanes = (2 * HALF - width) // 2
    loss_lanes = jnp.broadcast_to(losses, (batch, lanes))
    class_lanes = jnp.full((batch, lanes), sums_ref[1] / batch, jnp.float32)

    def write(first, second):
        first[...] = left
        second[:, :rest] = right
        second[:, rest : rest + lanes] = loss_lanes
        second[:, rest + lanes :] = class_lanes

    @pl.when(core_ref[0] == 0)
    def _():
        write(mine_ref, theirs_ref)

    @pl.when(core_ref[0] != 0)
    def _():
        write(theirs_ref, mine_ref)


def tail(core, sums, rows, queries, kept, signs, balance):
    batch, width = queries.shape
    smem = pl.BlockSpec(memory_space=pltpu.SMEM)
    vmem = pl.BlockSpec(memory_space=pltpu.VMEM)
    half = jax.ShapeDtypeStruct((batch, HALF), jnp.float32)
    return pl.pallas_call(
        tail_kernel,
        out_shape=(half, half, jax.ShapeDtypeStruct((batch, rows.shape[0]), jnp.float32)),
        in_specs=[smem, smem, vmem, vmem, vmem, vmem, vmem],
        out_specs=(vmem, vmem, vmem),
        compiler_params=pltpu.CompilerParams(vmem_limit_bytes=24 << 20),
        cost_estimate=pl.CostEstimate(
            flops=4 * batch * width * rows.shape[0],
            bytes_accessed=10 * batch * width,
            transcendentals=8 * batch,
        ),
        name="tail",
    )(core.reshape(1).astype(jnp.int32), sums, rows, queries, kept, signs, balance)


def final_kernel(core_ref, part_ref, back_ref, slopes_ref, queries_ref, label_ref, query_ref, loss_ref, *, labels):
    batch, width = queries_ref.shape
    rest = width - HALF
    lanes = (2 * HALF - width) // 2
    first = core_ref[0] == 0
    step = pl.program_id(0)
    rows = pl.ds(pl.multiple_of(step * query_ref.shape[0], 8), query_ref.shape[0])

    def side(left_ref, right_ref):
        losses = jnp.sum(right_ref[:, rest : rest + lanes]) / lanes
        weights = jnp.sum(right_ref[:, rest + lanes :]) / lanes
        factor = labels / weights
        scale = factor / math.sqrt(width)
        loss_ref[...] = jnp.full(loss_ref.shape, factor * losses / (batch * labels), jnp.float32)
        query_ref[:, :HALF] = scale * left_ref[rows, :]
        query_ref[:, HALF:] = scale * right_ref[rows, :rest]
        label_ref[...] = scale * lax.dot_general(
            slopes_ref[...],
            queries_ref[...],
            (((1,), (0,)), ((), ())),
            preferred_element_type=jnp.float32,
        )

    @pl.when(first)
    def _():
        side(part_ref, back_ref)

    @pl.when(jnp.logical_not(first))
    def _():
        side(back_ref, part_ref)


def final(core, part, back, slopes, queries, labels):
    batch, width = queries.shape
    owned = slopes.shape[0]
    steps = 4
    whole = lambda x: pl.BlockSpec(x.shape, lambda i, _: (0, 0))
    return pl.pallas_call(
        functools.partial(final_kernel, labels=labels),
        out_shape=(
            jax.ShapeDtypeStruct((owned, width), jnp.float32),
            jax.ShapeDtypeStruct((batch, width), jnp.float32),
            jax.ShapeDtypeStruct((8, 128), jnp.float32),
        ),
        grid_spec=pltpu.PrefetchScalarGridSpec(
            num_scalar_prefetch=1,
            grid=(steps,),
            in_specs=[
                whole(part),
                whole(back),
                pl.BlockSpec((owned // steps, batch), lambda i, _: (i, 0)),
                whole(queries),
            ],
            out_specs=(
                pl.BlockSpec((owned // steps, width), lambda i, _: (i, 0)),
                pl.BlockSpec((batch // steps, width), lambda i, _: (i, 0)),
                pl.BlockSpec((8, 128), lambda i, _: (0, 0)),
            ),
        ),
        compiler_params=pltpu.CompilerParams(vmem_limit_bytes=32 << 20),
        name="final",
    )(core.reshape(1).astype(jnp.int32), part, back, slopes, queries)


def shards(
    hidden_states,
    token_ids,
    norm_gain,
    q_weight,
    key_matrix,
    value_matrix,
    out_weight,
    label_table,
    refresh_rows,
    label_counts,
    queries,
    positives,
):
    f32, bf16 = jnp.float32, jnp.bfloat16
    width = hidden_states.shape[1]
    group_tokens = hidden_states.shape[0]
    texts, length = token_ids.shape
    xh, core = lax.axis_index("xh"), lax.axis_index("c")
    member = lax.axis_index(MP)
    ndp, nmp = 64, 4
    rows = q_weight.shape[0]

    packed = jnp.concatenate([key_matrix, value_matrix, q_weight, out_weight], axis=1)
    moved = lax.ppermute(
        packed,
        ("xh", "xl", "c"),
        [(4 * h + 2 * l + k, 4 * l + 2 * k + h) for h in (0, 1) for l in (0, 1) for k in (0, 1)],
    )
    cut = packed.shape[1] - out_weight.shape[1]
    moved, hidden_states = lax.optimization_barrier((moved, hidden_states))
    y = lax.axis_index("y")
    far_z = lax.all_gather(moved[:, CUT:], "z", axis=0, tiled=True)
    part_a = moved[:, :CUT]
    a_y = in_order([part_a] + [shift(part_a, "y", 4, -d) for d in (1, 2, 3)], y)
    a_all = lax.all_gather(a_y.reshape(-1, CUT), "z", axis=0, tiled=True)
    own = far_z[:, : cut - CUT]
    up, down = ring_near(own)
    pieces = (own, up, *ring_far(up, down), down)
    far_z, pieces = lax.optimization_barrier((far_z, pieces))
    out_own = far_z[:, cut - CUT :]
    out_up, out_down = ring_near(out_own)

    balance = (1.0 - focal_beta) / -jnp.expm1(
        label_counts.astype(f32) * math.log(focal_beta)
    )
    owned = label_table.shape[0]
    root = math.sqrt(width)
    first_label = (lax.axis_index(DP) * nmp + member) * owned
    own_rows = jnp.arange(owned, dtype=jnp.int32)
    chosen = refresh_rows[:, None] == own_rows[None, :]
    kept = ~jnp.any(chosen, axis=0)
    kept_balance = jnp.where(kept, balance, 0.0)
    matched = jnp.any(positives[:, :, None] == (first_label + own_rows)[None, None, :], axis=1)
    signs = jnp.where(matched, 1.0, -1.0)
    logits = (
        lax.dot_general(
            queries, label_table, (((1,), (1,)), ((), ())), preferred_element_type=f32
        )
        / root
    )
    terms, slope = focal(signs * logits)
    kept_loss = jnp.sum(kept_balance[None, :] * terms)
    kept_slopes = (kept_balance[None, :] * signs * slope).astype(bf16)
    kept_query = jnp.dot(kept_slopes, label_table, preferred_element_type=f32)
    new_balance = jnp.sum(jnp.where(chosen, balance[None, :], 0.0), axis=1)
    new_signs = jnp.where(
        jnp.any(positives[:, :, None] == (first_label + refresh_rows)[None, None, :], axis=1),
        1.0,
        -1.0,
    )

    states = hidden_states.astype(f32)
    scaled = lax.rsqrt(jnp.mean(states * states, axis=1, keepdims=True) + norm_eps)
    normed = (states * scaled * norm_gain).astype(bf16)
    live = (token_ids != 0).astype(f32)
    share = texts // nmp
    live_own = lax.dynamic_slice_in_dim(live, member * share, share, 0)
    states_own = lax.dynamic_slice_in_dim(
        hidden_states, member * share * length, share * length, 0
    ).reshape(share, length, width)
    counted = jnp.sum(live_own, axis=1, keepdims=True)
    states_sum = jnp.sum(states_own.astype(f32) * live_own[:, :, None], axis=1)

    half = normed.T.reshape(ndp // 2, 2, rows, group_tokens)
    half = lax.dynamic_index_in_dim(half, core, 1, keepdims=False).reshape(-1, group_tokens)
    facing = [(i, 3 - i) for i in range(4)]
    half_other = lax.ppermute(half, RING_X, facing)
    ids_other = lax.ppermute(token_ids, RING_X, facing)
    keeps = xh == core
    give = jnp.where(keeps, half_other, half)
    keep = jnp.where(keeps, half, half_other)
    ids = jnp.where(keeps, token_ids, ids_other)

    def by_y(block):
        return block.reshape(8, 4, rows, -1).transpose(1, 0, 2, 3).reshape(4, 8 * rows, -1)

    allowed, live_rows = attend_tables(ids)
    sums = jnp.stack([kept_loss, jnp.sum(balance)])
    early = (kept_query, kept_slopes, sums, new_balance, new_signs, chosen, states_sum, counted)
    early = early + (allowed, live_rows, give, keep, by_y(give), by_y(keep))
    (a_all, pieces, early) = lax.optimization_barrier((a_all, pieces, early))
    kept_query, kept_slopes, sums, new_balance, new_signs, chosen, states_sum, counted = early[:8]
    allowed, live_rows, give, keep, give_y, keep_y = early[8:]
    taken = shift(project(y, give, give_y, a_all, pieces), "c", 2, 1)
    raw = project(y, keep, keep_y, a_all, pieces)
    raw, out_up, out_down = lax.optimization_barrier((raw, out_up, out_down))
    out_far = ring_far(out_up, out_down)
    pooled = attend_pooled(raw, taken, allowed, live_rows, length).astype(bf16)

    pooled_other = shift(pooled, "c", 2, 1)
    both = jnp.concatenate(
        [jnp.where(core == 0, pooled, pooled_other), jnp.where(core == 0, pooled_other, pooled)],
        axis=0,
    )
    out_all = jnp.concatenate([out_own, out_up, *out_far, out_down], axis=0)
    head_terms = lax.dot_general(
        both, out_all, (((1,), (1,)), ((), ())), preferred_element_type=f32
    )
    exchanged = lax.all_to_all(
        head_terms.reshape(8, share, -1), ("xh", "xl", "c"), 0, 0, tiled=True
    )
    summed = jnp.sum(exchanged.reshape(nmp, 2, share, -1), axis=0)
    blocks = summed.reshape(2, share, 4, 8 * rows)
    turned = lax.dynamic_slice_in_dim(jnp.concatenate([blocks, blocks], axis=2), 4 - y, 4, 2)
    output_own = (
        turned.reshape(2, share, 4, 8, rows).transpose(1, 3, 2, 0, 4).reshape(share, width)
    )
    refreshed = ((states_sum + output_own) / counted).astype(bf16)

    mine, theirs, new_slopes = tail(
        core, sums, refreshed, queries, kept_query, new_signs, new_balance[None, :]
    )
    slopes = kept_slopes.T + lax.dot_general(
        chosen.astype(bf16),
        new_slopes.astype(bf16),
        (((0,), (1,)), ((), ())),
        preferred_element_type=f32,
    ).astype(bf16)

    batch = queries.shape[0]
    near = ("y", "xh", "xl")
    part = mine + shift(theirs, "c", 2, 1)
    part = jnp.sum(
        lax.all_to_all(part.reshape(16, batch // 16, HALF), near, 0, 0, tiled=True), axis=0
    )
    part = jnp.sum(spread(part, "z", 8), axis=0)
    part = spread(part, near, 16).reshape(batch, HALF)
    back = shift(part, "c", 2, 1)
    label_grad, query_grad, loss = final(core, part, back, slopes, queries, owned * ndp * nmp)
    return (label_grad, query_grad, loss[0, 0])


def solution(mesh):
    grid = Mesh(mesh.devices.reshape(SIZES), AXES)
    in_specs = (
        P(DP, None),
        P(DP, None),
        P(),
        P(DP, MP),
        P(DP, MP),
        P(DP, MP),
        P(DP, MP),
        P(AXES, None),
        P(AXES),
        P(AXES),
        P(),
        P(),
    )
    out_specs = (P(AXES, None), P(), P())
    return jax.shard_map(shards, mesh=grid, in_specs=in_specs, out_specs=out_specs, check_vma=False)
```

```python
import functools
import math

import jax
import jax.numpy as jnp
import numpy as np
from jax import lax
from jax.experimental import pallas as pl
from jax.experimental.pallas import tpu as pltpu
from jax.sharding import Mesh, PartitionSpec as P

HEAD_WIDTH = 128

rope_theta = 1000000.0
norm_eps = 1e-06
focal_beta = 0.9999

AXES = ("z", "y", "xh", "xl", "c")
SIZES = (8, 4, 2, 2, 2)
DP = ("z", "y", "xh")
MP = ("xl", "c")
RING_X = ("xh", "xl")


BLOCK = 128
SENT = 1280
HALF = 1920


def rotary_tables(length):
    half = HEAD_WIDTH // 2
    frequency = rope_theta ** (-2.0 * np.arange(half) / HEAD_WIDTH)
    angles = np.arange(length)[:, None] * frequency[None, :]
    cosine = np.concatenate([np.cos(angles), np.cos(angles)], axis=1)
    sine = np.concatenate([-np.sin(angles), np.sin(angles)], axis=1)
    repeat = BLOCK // length
    return (
        jnp.asarray(np.tile(cosine, (repeat, 1)), jnp.float32),
        jnp.asarray(np.tile(sine, (repeat, 1)), jnp.float32),
    )


def project_kernel(place_ref, x_ref, w0_ref, w1_ref, w2a_ref, w2b_ref, w3_ref, out_ref):
    def dot(x, w):
        return lax.dot_general(
            x, w, (((0,), (0,)), ((), ())), preferred_element_type=jnp.float32
        )

    y = place_ref[0]
    half = w2a_ref.shape[0]
    far = x_ref[(y + 2) % 4]
    out_ref[...] = (
        dot(x_ref[y], w0_ref[...])
        + dot(x_ref[(y + 1) % 4], w1_ref[...])
        + dot(x_ref[(y + 3) % 4], w3_ref[...])
        + dot(far[:half], w2a_ref[...])
        + dot(far[half:], w2b_ref[...])
    )


def project(y, x, pieces):
    _, depth, tokens = x.shape
    columns = pieces[0].shape[1]
    block = tokens // 2
    return pl.pallas_call(
        project_kernel,
        out_shape=jax.ShapeDtypeStruct((tokens, columns), jnp.float32),
        grid_spec=pltpu.PrefetchScalarGridSpec(
            num_scalar_prefetch=1,
            grid=(tokens // block,),
            in_specs=[
                pl.BlockSpec((4, depth, block), lambda i, _: (0, 0, i)),
                *[pl.BlockSpec(w.shape, lambda i, _: (0, 0)) for w in pieces],
            ],
            out_specs=pl.BlockSpec((block, columns), lambda i, _: (i, 0)),
        ),
        compiler_params=pltpu.CompilerParams(vmem_limit_bytes=56 << 20),
        cost_estimate=pl.CostEstimate(
            flops=8 * depth * tokens * columns,
            bytes_accessed=4 * tokens * columns + 8 * depth * (tokens + columns),
            transcendentals=0,
        ),
        name="project",
    )(y.reshape(1).astype(jnp.int32), x, *pieces)


def attend_kernel(raw_ref, add_ref, allowed_ref, live_ref, member_ref, cos_ref, sin_ref, out_ref):
    width = HEAD_WIDTH
    cosine, sine = cos_ref[...], sin_ref[...]
    members = member_ref[...]
    heads = raw_ref.shape[1] // width - 2
    texts = members.shape[0] // heads

    def rotate(x):
        return (x * cosine + pltpu.roll(x, width // 2, 1) * sine).astype(jnp.bfloat16)

    for block in range(raw_ref.shape[0] // BLOCK):
        rows = slice(block * BLOCK, (block + 1) * BLOCK)

        def column(index):
            lanes = slice(index * width, (index + 1) * width)
            return raw_ref[rows, lanes] + add_ref[rows, lanes]

        allowed = jnp.concatenate([allowed_ref[rows, :]] * heads, axis=0)
        live = jnp.concatenate([live_ref[rows, :]] * heads, axis=0)
        keys = rotate(column(0))
        values = column(1).astype(jnp.bfloat16)
        rotated = jnp.concatenate([rotate(column(h + 2)) for h in range(heads)], axis=0)
        scores = lax.dot_general(
            rotated, keys, (((1,), (1,)), ((), ())), preferred_element_type=jnp.float32
        ) * (1.0 / math.sqrt(width))
        weights = jnp.where(allowed > 0.0, jnp.exp(scores), 0.0)
        total = jnp.sum(weights, axis=1, keepdims=True)
        probs = (weights * (live / total)).astype(jnp.bfloat16)
        shares = jnp.dot(members, probs, preferred_element_type=jnp.float32)
        high = shares.astype(jnp.bfloat16)
        low = (shares - high.astype(jnp.float32)).astype(jnp.bfloat16)
        pooled = jnp.dot(high, values, preferred_element_type=jnp.float32) + jnp.dot(
            low, values, preferred_element_type=jnp.float32
        )
        for head in range(heads):
            out_ref[block * texts : (block + 1) * texts, head * width : (head + 1) * width] = pooled[
                head * texts : (head + 1) * texts
            ]


def attend_tables(text_ids):
    texts, length = text_ids.shape
    per = BLOCK // length
    live = (text_ids != 0).reshape(texts // per, BLOCK)
    place = np.arange(BLOCK)
    shape = (place[:, None] // length == place[None, :] // length) & (
        place[:, None] >= place[None, :]
    )
    allowed = (jnp.asarray(shape)[None] & live[:, None, :]).astype(jnp.float32)
    return allowed.reshape(-1, BLOCK), (text_ids != 0).astype(jnp.float32).reshape(-1, 1)


def attend_pooled(raw, add, allowed, live, length):
    tokens, columns = raw.shape
    texts = tokens // length
    per = BLOCK // length
    heads = columns // HEAD_WIDTH - 2
    owner = (np.arange(per)[:, None] == np.arange(BLOCK)[None, :] // length).astype(np.float32)
    members = jnp.asarray(np.kron(np.eye(heads), owner), jnp.bfloat16)
    cosine, sine = rotary_tables(length)
    step = 2 * BLOCK
    return pl.pallas_call(
        attend_kernel,
        out_shape=jax.ShapeDtypeStruct((texts, heads * HEAD_WIDTH), jnp.float32),
        grid=(tokens // step,),
        in_specs=[
            pl.BlockSpec((step, columns), lambda i: (i, 0)),
            pl.BlockSpec((step, columns), lambda i: (i, 0)),
            pl.BlockSpec((step, BLOCK), lambda i: (i, 0)),
            pl.BlockSpec((step, 1), lambda i: (i, 0)),
            pl.BlockSpec(members.shape, lambda i: (0, 0)),
            pl.BlockSpec((BLOCK, HEAD_WIDTH), lambda i: (0, 0)),
            pl.BlockSpec((BLOCK, HEAD_WIDTH), lambda i: (0, 0)),
        ],
        out_specs=pl.BlockSpec((2 * per, heads * HEAD_WIDTH), lambda i: (i, 0)),
        compiler_params=pltpu.CompilerParams(vmem_limit_bytes=56 << 20),
        cost_estimate=pl.CostEstimate(
            flops=4 * tokens * BLOCK * heads * HEAD_WIDTH,
            bytes_accessed=raw.size * 8,
            transcendentals=tokens * BLOCK * heads,
        ),
        name="attend",
    )(
        raw,
        add,
        allowed,
        live,
        members,
        cosine,
        sine,
    )


def shift(x, axis, size, by):
    return lax.ppermute(x, axis, [(i, (i + by) % size) for i in range(size)])


def ring_near(own):
    return shift(own, "y", 4, -1), shift(own, "y", 4, 1)


def ring_far(up, down):
    half = up.shape[0] // 2
    return shift(up[:half], "y", 4, -1), shift(down[half:], "y", 4, 1)


def in_order(parts, index):
    n = len(parts)
    out = jnp.zeros((n,) + parts[0].shape, parts[0].dtype)
    for d, part in enumerate(parts):
        out = lax.dynamic_update_slice_in_dim(out, part[None], (index + d) % n, 0)
    return out


def spread(x, axes, size):
    return lax.all_to_all(jnp.broadcast_to(x[None], (size,) + x.shape), axes, 0, 0, tiled=True)


def focal(margin):
    missed = jax.nn.sigmoid(-margin)
    softened = jnp.maximum(-margin, 0.0) + jnp.log1p(jnp.exp(-jnp.abs(margin)))
    return missed * missed * softened, -(missed * missed) * (
        2.0 * jax.nn.sigmoid(margin) * softened + missed
    )


def tail_kernel(core_ref, sums_ref, new_ref, queries_ref, kept_ref, signs_ref, balance_ref, mine_ref, theirs_ref, slopes_ref):
    batch, width = queries_ref.shape
    rows = new_ref[...]
    logits = lax.dot_general(
        queries_ref[...], rows, (((1,), (1,)), ((), ())), preferred_element_type=jnp.float32
    ) / math.sqrt(width)
    signs = signs_ref[...]
    balance = balance_ref[...]
    terms, slope = focal(signs * logits)
    losses = jnp.sum(balance * terms, axis=1, keepdims=True) + sums_ref[0] / batch
    slopes = (balance * signs * slope).astype(jnp.bfloat16)
    slopes_ref[...] = slopes.astype(jnp.float32)
    left = kept_ref[:, :HALF] + jnp.dot(slopes, rows[:, :HALF], preferred_element_type=jnp.float32)
    right = kept_ref[:, HALF:] + jnp.dot(slopes, rows[:, HALF:], preferred_element_type=jnp.float32)
    rest = width - HALF
    lanes = (2 * HALF - width) // 2
    loss_lanes = jnp.broadcast_to(losses, (batch, lanes))
    class_lanes = jnp.full((batch, lanes), sums_ref[1] / batch, jnp.float32)

    def write(first, second):
        first[...] = left
        second[:, :rest] = right
        second[:, rest : rest + lanes] = loss_lanes
        second[:, rest + lanes :] = class_lanes

    @pl.when(core_ref[0] == 0)
    def _():
        write(mine_ref, theirs_ref)

    @pl.when(core_ref[0] != 0)
    def _():
        write(theirs_ref, mine_ref)


def tail(core, sums, rows, queries, kept, signs, balance):
    batch, width = queries.shape
    smem = pl.BlockSpec(memory_space=pltpu.SMEM)
    vmem = pl.BlockSpec(memory_space=pltpu.VMEM)
    half = jax.ShapeDtypeStruct((batch, HALF), jnp.float32)
    return pl.pallas_call(
        tail_kernel,
        out_shape=(half, half, jax.ShapeDtypeStruct((batch, rows.shape[0]), jnp.float32)),
        in_specs=[smem, smem, vmem, vmem, vmem, vmem, vmem],
        out_specs=(vmem, vmem, vmem),
        compiler_params=pltpu.CompilerParams(vmem_limit_bytes=24 << 20),
        cost_estimate=pl.CostEstimate(
            flops=4 * batch * width * rows.shape[0],
            bytes_accessed=10 * batch * width,
            transcendentals=8 * batch,
        ),
        name="tail",
    )(core.reshape(1).astype(jnp.int32), sums, rows, queries, kept, signs, balance)


def final_kernel(core_ref, part_ref, back_ref, slopes_ref, queries_ref, label_ref, query_ref, loss_ref, *, labels):
    batch, width = queries_ref.shape
    rest = width - HALF
    lanes = (2 * HALF - width) // 2
    first = core_ref[0] == 0
    step = pl.program_id(0)
    rows = pl.ds(pl.multiple_of(step * query_ref.shape[0], 8), query_ref.shape[0])

    def side(left_ref, right_ref):
        losses = jnp.sum(right_ref[:, rest : rest + lanes]) / lanes
        weights = jnp.sum(right_ref[:, rest + lanes :]) / lanes
        factor = labels / weights
        scale = factor / math.sqrt(width)
        loss_ref[...] = jnp.full(loss_ref.shape, factor * losses / (batch * labels), jnp.float32)
        query_ref[:, :HALF] = scale * left_ref[rows, :]
        query_ref[:, HALF:] = scale * right_ref[rows, :rest]
        label_ref[...] = scale * lax.dot_general(
            slopes_ref[...],
            queries_ref[...],
            (((1,), (0,)), ((), ())),
            preferred_element_type=jnp.float32,
        )

    @pl.when(first)
    def _():
        side(part_ref, back_ref)

    @pl.when(jnp.logical_not(first))
    def _():
        side(back_ref, part_ref)


def final(core, part, back, slopes, queries, labels):
    batch, width = queries.shape
    owned = slopes.shape[0]
    steps = 4
    whole = lambda x: pl.BlockSpec(x.shape, lambda i, _: (0, 0))
    return pl.pallas_call(
        functools.partial(final_kernel, labels=labels),
        out_shape=(
            jax.ShapeDtypeStruct((owned, width), jnp.float32),
            jax.ShapeDtypeStruct((batch, width), jnp.float32),
            jax.ShapeDtypeStruct((8, 128), jnp.float32),
        ),
        grid_spec=pltpu.PrefetchScalarGridSpec(
            num_scalar_prefetch=1,
            grid=(steps,),
            in_specs=[
                whole(part),
                whole(back),
                pl.BlockSpec((owned // steps, batch), lambda i, _: (i, 0)),
                whole(queries),
            ],
            out_specs=(
                pl.BlockSpec((owned // steps, width), lambda i, _: (i, 0)),
                pl.BlockSpec((batch // steps, width), lambda i, _: (i, 0)),
                pl.BlockSpec((8, 128), lambda i, _: (0, 0)),
            ),
        ),
        compiler_params=pltpu.CompilerParams(vmem_limit_bytes=32 << 20),
        name="final",
    )(core.reshape(1).astype(jnp.int32), part, back, slopes, queries)


def shards(
    hidden_states,
    token_ids,
    norm_gain,
    q_weight,
    key_matrix,
    value_matrix,
    out_weight,
    label_table,
    refresh_rows,
    label_counts,
    queries,
    positives,
):
    f32, bf16 = jnp.float32, jnp.bfloat16
    width = hidden_states.shape[1]
    group_tokens = hidden_states.shape[0]
    texts, length = token_ids.shape
    xh, core = lax.axis_index("xh"), lax.axis_index("c")
    member = lax.axis_index(MP)
    ndp, nmp = 64, 4
    rows = q_weight.shape[0]

    packed = jnp.concatenate([key_matrix, value_matrix, q_weight, out_weight], axis=1)
    moved = lax.ppermute(
        packed,
        ("xh", "xl", "c"),
        [(4 * h + 2 * l + k, 4 * l + 2 * k + h) for h in (0, 1) for l in (0, 1) for k in (0, 1)],
    )
    cut = packed.shape[1] - out_weight.shape[1]
    y = lax.axis_index("y")
    in_z = lax.all_gather(moved[:, :SENT], "z", axis=0, tiled=True)
    out_part = moved[:, cut:]
    out_y = in_order([out_part] + [shift(out_part, "y", 4, -d) for d in (1, 2, 3)], y)
    out_y, hidden_states = lax.optimization_barrier((out_y, hidden_states))
    out_all = lax.all_gather(out_y.reshape(4 * rows, -1), "z", axis=0, tiled=True)
    own = in_z[:, :cut]
    up, down = ring_near(own)
    pieces = (own, up, *ring_far(up, down), down)

    balance = (1.0 - focal_beta) / -jnp.expm1(
        label_counts.astype(f32) * math.log(focal_beta)
    )
    owned = label_table.shape[0]
    root = math.sqrt(width)
    first_label = (lax.axis_index(DP) * nmp + member) * owned
    own_rows = jnp.arange(owned, dtype=jnp.int32)
    chosen = refresh_rows[:, None] == own_rows[None, :]
    kept = ~jnp.any(chosen, axis=0)
    kept_balance = jnp.where(kept, balance, 0.0)
    matched = jnp.any(positives[:, :, None] == (first_label + own_rows)[None, None, :], axis=1)
    signs = jnp.where(matched, 1.0, -1.0)
    logits = (
        lax.dot_general(
            queries, label_table, (((1,), (1,)), ((), ())), preferred_element_type=f32
        )
        / root
    )
    terms, slope = focal(signs * logits)
    kept_loss = jnp.sum(kept_balance[None, :] * terms)
    kept_slopes = (kept_balance[None, :] * signs * slope).astype(bf16)
    kept_query = jnp.dot(kept_slopes, label_table, preferred_element_type=f32)
    new_balance = jnp.sum(jnp.where(chosen, balance[None, :], 0.0), axis=1)
    new_signs = jnp.where(
        jnp.any(positives[:, :, None] == (first_label + refresh_rows)[None, None, :], axis=1),
        1.0,
        -1.0,
    )

    states = hidden_states.astype(f32)
    scaled = lax.rsqrt(jnp.mean(states * states, axis=1, keepdims=True) + norm_eps)
    normed = (states * scaled * norm_gain).astype(bf16)
    live = (token_ids != 0).astype(f32)
    share = texts // nmp
    live_own = lax.dynamic_slice_in_dim(live, member * share, share, 0)
    states_own = lax.dynamic_slice_in_dim(
        hidden_states, member * share * length, share * length, 0
    ).reshape(share, length, width)
    counted = jnp.sum(live_own, axis=1, keepdims=True)
    states_sum = jnp.sum(states_own.astype(f32) * live_own[:, :, None], axis=1)

    half = normed.T.reshape(ndp // 2, 2, rows, group_tokens)
    half = lax.dynamic_index_in_dim(half, core, 1, keepdims=False).reshape(-1, group_tokens)
    facing = [(i, 3 - i) for i in range(4)]
    half_other = lax.ppermute(half, RING_X, facing)
    ids_other = lax.ppermute(token_ids, RING_X, facing)
    keeps = xh == core
    give = jnp.where(keeps, half_other, half)
    keep = jnp.where(keeps, half, half_other)
    ids = jnp.where(keeps, token_ids, ids_other)

    def by_y(block):
        return block.reshape(8, 4, rows, -1).transpose(1, 0, 2, 3).reshape(4, 8 * rows, -1)

    allowed, live_rows = attend_tables(ids)
    sums = jnp.stack([kept_loss, jnp.sum(balance)])
    early = (kept_query, kept_slopes, sums, new_balance, new_signs, chosen, states_sum, counted)
    early = early + (allowed, live_rows, by_y(give), by_y(keep))
    pieces, early = lax.optimization_barrier((pieces, early))
    kept_query, kept_slopes, sums, new_balance, new_signs, chosen, states_sum, counted = early[:8]
    allowed, live_rows, give, keep = early[8:]
    taken = shift(project(y, give, pieces), "c", 2, 1)
    raw = project(y, keep, pieces)
    pooled = attend_pooled(raw, taken, allowed, live_rows, length).astype(bf16)

    pooled_other = shift(pooled, "c", 2, 1)
    both = jnp.concatenate(
        [jnp.where(core == 0, pooled, pooled_other), jnp.where(core == 0, pooled_other, pooled)],
        axis=0,
    )
    head_terms = lax.dot_general(
        both, out_all, (((1,), (1,)), ((), ())), preferred_element_type=f32
    )
    exchanged = lax.all_to_all(
        head_terms.reshape(8, share, -1), ("xh", "xl", "c"), 0, 0, tiled=True
    )
    summed = jnp.sum(exchanged.reshape(nmp, 2, share, -1), axis=0)
    output_own = (
        summed.reshape(2, share, ndp // 2, rows).transpose(1, 2, 0, 3).reshape(share, width)
    )
    refreshed = ((states_sum + output_own) / counted).astype(bf16)

    mine, theirs, new_slopes = tail(
        core, sums, refreshed, queries, kept_query, new_signs, new_balance[None, :]
    )
    slopes = kept_slopes.T + lax.dot_general(
        chosen.astype(bf16),
        new_slopes.astype(bf16),
        (((0,), (1,)), ((), ())),
        preferred_element_type=f32,
    ).astype(bf16)

    batch = queries.shape[0]
    near = ("y", "xh", "xl")
    part = mine + shift(theirs, "c", 2, 1)
    part = jnp.sum(
        lax.all_to_all(part.reshape(16, batch // 16, HALF), near, 0, 0, tiled=True), axis=0
    )
    part = jnp.sum(spread(part, "z", 8), axis=0)
    part = spread(part, near, 16).reshape(batch, HALF)
    back = shift(part, "c", 2, 1)
    label_grad, query_grad, loss = final(core, part, back, slopes, queries, owned * ndp * nmp)
    return (label_grad, query_grad, loss[0, 0])


def solution(mesh):
    grid = Mesh(mesh.devices.reshape(SIZES), AXES)
    in_specs = (
        P(DP, None),
        P(DP, None),
        P(),
        P(DP, MP),
        P(DP, MP),
        P(DP, MP),
        P(DP, MP),
        P(AXES, None),
        P(AXES),
        P(AXES),
        P(),
        P(),
    )
    out_specs = (P(AXES, None), P(), P())
    return jax.shard_map(shards, mesh=grid, in_specs=in_specs, out_specs=out_specs, check_vma=False)
```

```python
import functools
import math

import jax
import jax.numpy as jnp
import numpy as np
from jax import lax
from jax.experimental import pallas as pl
from jax.experimental.pallas import tpu as pltpu
from jax.sharding import Mesh, PartitionSpec as P

HEAD_WIDTH = 128

rope_theta = 1000000.0
norm_eps = 1e-06
focal_beta = 0.9999

AXES = ("z", "y", "xh", "xl", "c")
SIZES = (8, 4, 2, 2, 2)
DP = ("z", "y", "xh")
MP = ("xl", "c")
RING_X = ("xh", "xl")


BLOCK = 128
HALF = 1920


def rotary_tables(length):
    half = HEAD_WIDTH // 2
    frequency = rope_theta ** (-2.0 * np.arange(half) / HEAD_WIDTH)
    angles = np.arange(length)[:, None] * frequency[None, :]
    cosine = np.concatenate([np.cos(angles), np.cos(angles)], axis=1)
    sine = np.concatenate([-np.sin(angles), np.sin(angles)], axis=1)
    repeat = BLOCK // length
    return (
        jnp.asarray(np.tile(cosine, (repeat, 1)), jnp.float32),
        jnp.asarray(np.tile(sine, (repeat, 1)), jnp.float32),
    )


def norm_kernel(core_ref, states_ref, gain_ref, out_ref, turned_ref):
    states = states_ref[...].astype(jnp.float32)
    scaled = lax.rsqrt(jnp.mean(states * states, axis=1, keepdims=True) + norm_eps)
    turned_ref[...] = (states * scaled * gain_ref[...]).T
    rows = out_ref.shape[1] // 8

    def block(z, y):
        first = pl.multiple_of(((z * 4 + y) * 2 + core_ref[0]) * rows, 8)
        return turned_ref[pl.ds(first, rows), :]

    for y in range(4):
        for pair in range(4):
            out_ref[y, 2 * pair * rows : 2 * (pair + 1) * rows, :] = jnp.concatenate(
                [block(2 * pair, y), block(2 * pair + 1, y)], axis=0
            ).astype(jnp.bfloat16)


def norm_half(core, states, gain):
    tokens, width = states.shape
    block = 128
    return pl.pallas_call(
        norm_kernel,
        out_shape=jax.ShapeDtypeStruct((4, width // 8, tokens), jnp.bfloat16),
        grid_spec=pltpu.PrefetchScalarGridSpec(
            num_scalar_prefetch=1,
            grid=(tokens // block,),
            in_specs=[
                pl.BlockSpec((block, width), lambda i, _: (i, 0)),
                pl.BlockSpec((1, width), lambda i, _: (0, 0)),
            ],
            out_specs=pl.BlockSpec((4, width // 8, block), lambda i, _: (0, 0, i)),
            scratch_shapes=[pltpu.VMEM((width, block), jnp.float32)],
        ),
        compiler_params=pltpu.CompilerParams(vmem_limit_bytes=32 << 20),
        cost_estimate=pl.CostEstimate(
            flops=4 * tokens * width, bytes_accessed=3 * tokens * width, transcendentals=tokens
        ),
        name="norm",
    )(core.reshape(1).astype(jnp.int32), states, gain.reshape(1, width))


def near_kernel(place_ref, x_ref, w0_ref, w1_ref, w3_ref, out_ref):
    def dot(x, w):
        return lax.dot_general(
            x, w, (((0,), (0,)), ((), ())), preferred_element_type=jnp.float32
        )

    y = place_ref[0]
    out_ref[...] = (
        dot(x_ref[y], w0_ref[...])
        + dot(x_ref[(y + 1) % 4], w1_ref[...])
        + dot(x_ref[(y + 3) % 4], w3_ref[...])
    )


def far_kernel(place_ref, x_ref, near_ref, w2a_ref, w2b_ref, out_ref):
    def dot(x, w):
        return lax.dot_general(
            x, w, (((0,), (0,)), ((), ())), preferred_element_type=jnp.float32
        )

    half = w2a_ref.shape[0]
    far = x_ref[0]
    out_ref[...] = (
        near_ref[...] + dot(far[:half], w2a_ref[...]) + dot(far[half:], w2b_ref[...])
    ).astype(out_ref.dtype)


def project(y, x, pieces, near=None, dtype=jnp.float32):
    _, depth, tokens = x.shape
    columns = pieces[0].shape[1]
    block = tokens // 2
    fixed = [pl.BlockSpec(w.shape, lambda i, _: (0, 0)) for w in pieces]
    tile = pl.BlockSpec((block, columns), lambda i, _: (i, 0))
    if near is None:
        kernel, extra = near_kernel, ()
        x_spec = pl.BlockSpec((4, depth, block), lambda i, _: (0, 0, i))
    else:
        kernel, extra = far_kernel, (near,)
        x_spec = pl.BlockSpec((1, depth, block), lambda i, p: ((p[0] + 2) % 4, 0, i))
    used = sum(w.shape[0] for w in pieces)
    return pl.pallas_call(
        kernel,
        out_shape=jax.ShapeDtypeStruct((tokens, columns), dtype),
        grid_spec=pltpu.PrefetchScalarGridSpec(
            num_scalar_prefetch=1,
            grid=(tokens // block,),
            in_specs=[x_spec, *[tile for _ in extra], *fixed],
            out_specs=tile,
        ),
        compiler_params=pltpu.CompilerParams(vmem_limit_bytes=56 << 20),
        cost_estimate=pl.CostEstimate(
            flops=2 * used * tokens * columns,
            bytes_accessed=6 * tokens * columns + 2 * used * (tokens + columns),
            transcendentals=0,
        ),
        name="near" if near is None else "far",
    )(y.reshape(1).astype(jnp.int32), x, *extra, *pieces)


def attend_kernel(raw_ref, add_ref, allowed_ref, live_ref, member_ref, cos_ref, sin_ref, out_ref):
    width = HEAD_WIDTH
    cosine, sine = cos_ref[...], sin_ref[...]
    members = member_ref[...]
    heads = raw_ref.shape[1] // width - 2
    texts = members.shape[0] // heads

    def rotate(x):
        return (x * cosine + pltpu.roll(x, width // 2, 1) * sine).astype(jnp.bfloat16)

    for block in range(raw_ref.shape[0] // BLOCK):
        rows = slice(block * BLOCK, (block + 1) * BLOCK)

        def column(index):
            lanes = slice(index * width, (index + 1) * width)
            return raw_ref[rows, lanes] + add_ref[rows, lanes].astype(jnp.float32)

        allowed = jnp.concatenate([allowed_ref[rows, :]] * heads, axis=0)
        live = jnp.concatenate([live_ref[rows, :]] * heads, axis=0)
        keys = rotate(column(0))
        values = column(1).astype(jnp.bfloat16)
        rotated = jnp.concatenate([rotate(column(h + 2)) for h in range(heads)], axis=0)
        scores = lax.dot_general(
            rotated, keys, (((1,), (1,)), ((), ())), preferred_element_type=jnp.float32
        ) * (1.0 / math.sqrt(width))
        weights = jnp.where(allowed > 0.0, jnp.exp(scores), 0.0)
        total = jnp.sum(weights, axis=1, keepdims=True)
        probs = (weights * (live / total)).astype(jnp.bfloat16)
        shares = jnp.dot(members, probs, preferred_element_type=jnp.float32)
        high = shares.astype(jnp.bfloat16)
        low = (shares - high.astype(jnp.float32)).astype(jnp.bfloat16)
        pooled = jnp.dot(high, values, preferred_element_type=jnp.float32) + jnp.dot(
            low, values, preferred_element_type=jnp.float32
        )
        for head in range(heads):
            columns = slice(head * width, (head + 1) * width)
            out_ref[block * texts : (block + 1) * texts, columns] = pooled[
                head * texts : (head + 1) * texts
            ].astype(out_ref.dtype)


def attend_tables(text_ids):
    texts, length = text_ids.shape
    per = BLOCK // length
    live = (text_ids != 0).reshape(texts // per, BLOCK)
    place = np.arange(BLOCK)
    shape = (place[:, None] // length == place[None, :] // length) & (
        place[:, None] >= place[None, :]
    )
    allowed = (jnp.asarray(shape)[None] & live[:, None, :]).astype(jnp.float32)
    return allowed.reshape(-1, BLOCK), (text_ids != 0).astype(jnp.float32).reshape(-1, 1)


def attend_pooled(raw, add, allowed, live, length):
    tokens, columns = raw.shape
    texts = tokens // length
    per = BLOCK // length
    heads = columns // HEAD_WIDTH - 2
    owner = (np.arange(per)[:, None] == np.arange(BLOCK)[None, :] // length).astype(np.float32)
    members = jnp.asarray(np.kron(np.eye(heads), owner), jnp.bfloat16)
    cosine, sine = rotary_tables(length)
    step = 2 * BLOCK
    return pl.pallas_call(
        attend_kernel,
        out_shape=jax.ShapeDtypeStruct((texts, heads * HEAD_WIDTH), jnp.bfloat16),
        grid=(tokens // step,),
        in_specs=[
            pl.BlockSpec((step, columns), lambda i: (i, 0)),
            pl.BlockSpec((step, columns), lambda i: (i, 0)),
            pl.BlockSpec((step, BLOCK), lambda i: (i, 0)),
            pl.BlockSpec((step, 1), lambda i: (i, 0)),
            pl.BlockSpec(members.shape, lambda i: (0, 0)),
            pl.BlockSpec((BLOCK, HEAD_WIDTH), lambda i: (0, 0)),
            pl.BlockSpec((BLOCK, HEAD_WIDTH), lambda i: (0, 0)),
        ],
        out_specs=pl.BlockSpec((2 * per, heads * HEAD_WIDTH), lambda i: (i, 0)),
        compiler_params=pltpu.CompilerParams(vmem_limit_bytes=56 << 20),
        cost_estimate=pl.CostEstimate(
            flops=4 * tokens * BLOCK * heads * HEAD_WIDTH,
            bytes_accessed=raw.size * 8,
            transcendentals=tokens * BLOCK * heads,
        ),
        name="attend",
    )(
        raw,
        add,
        allowed,
        live,
        members,
        cosine,
        sine,
    )


def shift(x, axis, size, by):
    return lax.ppermute(x, axis, [(i, (i + by) % size) for i in range(size)])


def ring_near(own):
    return shift(own, "y", 4, -1), shift(own, "y", 4, 1)


def ring_far(up, down):
    half = up.shape[0] // 2
    return shift(up[:half], "y", 4, -1), shift(down[half:], "y", 4, 1)


def in_order(parts, index):
    n = len(parts)
    out = jnp.zeros((n,) + parts[0].shape, parts[0].dtype)
    for d, part in enumerate(parts):
        out = lax.dynamic_update_slice_in_dim(out, part[None], (index + d) % n, 0)
    return out


def spread(x, axes, size):
    return lax.all_to_all(jnp.broadcast_to(x[None], (size,) + x.shape), axes, 0, 0, tiled=True)


def focal(margin):
    missed = jax.nn.sigmoid(-margin)
    softened = jnp.maximum(-margin, 0.0) + jnp.log1p(jnp.exp(-jnp.abs(margin)))
    return missed * missed * softened, -(missed * missed) * (
        2.0 * jax.nn.sigmoid(margin) * softened + missed
    )


def tail_kernel(core_ref, sums_ref, new_ref, queries_ref, kept_ref, signs_ref, balance_ref, mine_ref, theirs_ref, slopes_ref):
    batch, width = queries_ref.shape
    rows = new_ref[...]
    logits = lax.dot_general(
        queries_ref[...], rows, (((1,), (1,)), ((), ())), preferred_element_type=jnp.float32
    ) / math.sqrt(width)
    signs = signs_ref[...]
    balance = balance_ref[...]
    terms, slope = focal(signs * logits)
    losses = jnp.sum(balance * terms, axis=1, keepdims=True) + sums_ref[0] / batch
    slopes = (balance * signs * slope).astype(jnp.bfloat16)
    slopes_ref[...] = slopes.astype(jnp.float32)
    left = kept_ref[:, :HALF] + jnp.dot(slopes, rows[:, :HALF], preferred_element_type=jnp.float32)
    right = kept_ref[:, HALF:] + jnp.dot(slopes, rows[:, HALF:], preferred_element_type=jnp.float32)
    rest = width - HALF
    lanes = (2 * HALF - width) // 2
    loss_lanes = jnp.broadcast_to(losses, (batch, lanes))
    class_lanes = jnp.full((batch, lanes), sums_ref[1] / batch, jnp.float32)

    def write(first, second):
        first[...] = left
        second[:, :rest] = right
        second[:, rest : rest + lanes] = loss_lanes
        second[:, rest + lanes :] = class_lanes

    @pl.when(core_ref[0] == 0)
    def _():
        write(mine_ref, theirs_ref)

    @pl.when(core_ref[0] != 0)
    def _():
        write(theirs_ref, mine_ref)


def tail(core, sums, rows, queries, kept, signs, balance):
    batch, width = queries.shape
    smem = pl.BlockSpec(memory_space=pltpu.SMEM)
    vmem = pl.BlockSpec(memory_space=pltpu.VMEM)
    half = jax.ShapeDtypeStruct((batch, HALF), jnp.float32)
    return pl.pallas_call(
        tail_kernel,
        out_shape=(half, half, jax.ShapeDtypeStruct((batch, rows.shape[0]), jnp.float32)),
        in_specs=[smem, smem, vmem, vmem, vmem, vmem, vmem],
        out_specs=(vmem, vmem, vmem),
        compiler_params=pltpu.CompilerParams(vmem_limit_bytes=24 << 20),
        cost_estimate=pl.CostEstimate(
            flops=4 * batch * width * rows.shape[0],
            bytes_accessed=10 * batch * width,
            transcendentals=8 * batch,
        ),
        name="tail",
    )(core.reshape(1).astype(jnp.int32), sums, rows, queries, kept, signs, balance)


def final_kernel(core_ref, part_ref, back_ref, slopes_ref, queries_ref, label_ref, query_ref, loss_ref, *, labels):
    batch, width = queries_ref.shape
    rest = width - HALF
    lanes = (2 * HALF - width) // 2
    first = core_ref[0] == 0
    step = pl.program_id(0)
    rows = pl.ds(pl.multiple_of(step * query_ref.shape[0], 8), query_ref.shape[0])

    def side(left_ref, right_ref):
        losses = jnp.sum(right_ref[:, rest : rest + lanes]) / lanes
        weights = jnp.sum(right_ref[:, rest + lanes :]) / lanes
        factor = labels / weights
        scale = factor / math.sqrt(width)
        loss_ref[...] = jnp.full(loss_ref.shape, factor * losses / (batch * labels), jnp.float32)
        query_ref[:, :HALF] = scale * left_ref[rows, :]
        query_ref[:, HALF:] = scale * right_ref[rows, :rest]
        label_ref[...] = scale * lax.dot_general(
            slopes_ref[...],
            queries_ref[...],
            (((1,), (0,)), ((), ())),
            preferred_element_type=jnp.float32,
        )

    @pl.when(first)
    def _():
        side(part_ref, back_ref)

    @pl.when(jnp.logical_not(first))
    def _():
        side(back_ref, part_ref)


def final(core, part, back, slopes, queries, labels):
    batch, width = queries.shape
    owned = slopes.shape[0]
    steps = 4
    whole = lambda x: pl.BlockSpec(x.shape, lambda i, _: (0, 0))
    return pl.pallas_call(
        functools.partial(final_kernel, labels=labels),
        out_shape=(
            jax.ShapeDtypeStruct((owned, width), jnp.float32),
            jax.ShapeDtypeStruct((batch, width), jnp.float32),
            jax.ShapeDtypeStruct((8, 128), jnp.float32),
        ),
        grid_spec=pltpu.PrefetchScalarGridSpec(
            num_scalar_prefetch=1,
            grid=(steps,),
            in_specs=[
                whole(part),
                whole(back),
                pl.BlockSpec((owned // steps, batch), lambda i, _: (i, 0)),
                whole(queries),
            ],
            out_specs=(
                pl.BlockSpec((owned // steps, width), lambda i, _: (i, 0)),
                pl.BlockSpec((batch // steps, width), lambda i, _: (i, 0)),
                pl.BlockSpec((8, 128), lambda i, _: (0, 0)),
            ),
        ),
        compiler_params=pltpu.CompilerParams(vmem_limit_bytes=32 << 20),
        name="final",
    )(core.reshape(1).astype(jnp.int32), part, back, slopes, queries)


def shards(
    hidden_states,
    token_ids,
    norm_gain,
    q_weight,
    key_matrix,
    value_matrix,
    out_weight,
    label_table,
    refresh_rows,
    label_counts,
    queries,
    positives,
):
    f32, bf16 = jnp.float32, jnp.bfloat16
    width = hidden_states.shape[1]
    texts, length = token_ids.shape
    xh, core = lax.axis_index("xh"), lax.axis_index("c")
    member = lax.axis_index(MP)
    ndp, nmp = 64, 4
    rows = q_weight.shape[0]

    def to_group(block, by):
        return lax.ppermute(
            block,
            ("y", "xh", "xl", "c"),
            [
                (8 * v + 4 * h + 2 * l + k, 8 * ((v - by) % 4) + 4 * l + 2 * k + h)
                for v in range(4)
                for h in (0, 1)
                for l in (0, 1)
                for k in (0, 1)
            ],
        )

    y = lax.axis_index("y")
    moved = to_group(jnp.concatenate([key_matrix, value_matrix, q_weight], axis=1), 0)
    out_y = in_order([to_group(out_weight, d) for d in range(4)], y)
    half = norm_half(core, hidden_states, norm_gain)
    facing = [(i, 3 - i) for i in range(4)]
    half_other = lax.ppermute(half, RING_X, facing)
    ids_other = lax.ppermute(token_ids, RING_X, facing)
    moved, half = lax.optimization_barrier((moved, half))
    own = lax.all_gather(moved, "z", axis=0, tiled=True)
    own, out_y = lax.optimization_barrier((own, out_y))
    out_all = lax.all_gather(out_y.reshape(4 * rows, -1), "z", axis=0, tiled=True)
    up, down = ring_near(own)
    far_a, far_b = ring_far(up, down)
    rest = (positives, label_counts, refresh_rows, queries, token_ids)
    half_other, rest = lax.optimization_barrier((half_other, rest))
    positives, label_counts, refresh_rows, queries, token_ids = rest

    balance = (1.0 - focal_beta) / -jnp.expm1(
        label_counts.astype(f32) * math.log(focal_beta)
    )
    owned = label_table.shape[0]
    root = math.sqrt(width)
    first_label = (lax.axis_index(DP) * nmp + member) * owned
    own_rows = jnp.arange(owned, dtype=jnp.int32)
    chosen = refresh_rows[:, None] == own_rows[None, :]
    kept = ~jnp.any(chosen, axis=0)
    kept_balance = jnp.where(kept, balance, 0.0)
    matched = jnp.any(positives[:, :, None] == (first_label + own_rows)[None, None, :], axis=1)
    signs = jnp.where(matched, 1.0, -1.0)
    logits = (
        lax.dot_general(
            queries, label_table, (((1,), (1,)), ((), ())), preferred_element_type=f32
        )
        / root
    )
    terms, slope = focal(signs * logits)
    kept_loss = jnp.sum(kept_balance[None, :] * terms)
    kept_slopes = (kept_balance[None, :] * signs * slope).astype(bf16)
    kept_query = jnp.dot(kept_slopes, label_table, preferred_element_type=f32)
    new_balance = jnp.sum(jnp.where(chosen, balance[None, :], 0.0), axis=1)
    new_signs = jnp.where(
        jnp.any(positives[:, :, None] == (first_label + refresh_rows)[None, None, :], axis=1),
        1.0,
        -1.0,
    )

    live = (token_ids != 0).astype(f32)
    share = texts // nmp
    live_own = lax.dynamic_slice_in_dim(live, member * share, share, 0)
    states_own = lax.dynamic_slice_in_dim(
        hidden_states, member * share * length, share * length, 0
    ).reshape(share, length, width)
    counted = jnp.sum(live_own, axis=1, keepdims=True)
    states_sum = jnp.sum(states_own.astype(f32) * live_own[:, :, None], axis=1)

    keeps = xh == core
    give = jnp.where(keeps, half_other, half)
    keep = jnp.where(keeps, half, half_other)
    ids = jnp.where(keeps, token_ids, ids_other)

    allowed, live_rows = attend_tables(ids)
    sums = jnp.stack([kept_loss, jnp.sum(balance)])
    early = (kept_query, kept_slopes, sums, new_balance, new_signs, chosen, states_sum, counted)
    near = (own, up, down)
    give_near, keep_near = project(y, give, near), project(y, keep, near)
    early = early + (allowed, live_rows, give_near, keep_near)
    far, early = lax.optimization_barrier(((far_a, far_b), early))
    kept_query, kept_slopes, sums, new_balance, new_signs, chosen, states_sum, counted = early[:8]
    allowed, live_rows, give_near, keep_near = early[8:]
    taken = shift(project(y, give, far, give_near, bf16), "c", 2, 1)
    raw = project(y, keep, far, keep_near)
    pooled = attend_pooled(raw, taken, allowed, live_rows, length)

    pooled_other = shift(pooled, "c", 2, 1)
    both = jnp.concatenate(
        [jnp.where(core == 0, pooled, pooled_other), jnp.where(core == 0, pooled_other, pooled)],
        axis=0,
    )
    head_terms = lax.dot_general(
        both, out_all, (((1,), (1,)), ((), ())), preferred_element_type=f32
    )
    exchanged = lax.all_to_all(
        head_terms.astype(bf16).reshape(8, share, -1), ("xh", "xl", "c"), 0, 0, tiled=True
    )
    summed = jnp.sum(exchanged.astype(f32).reshape(nmp, 2, share, -1), axis=0)
    output_own = (
        summed.reshape(2, share, ndp // 2, rows).transpose(1, 2, 0, 3).reshape(share, width)
    )
    refreshed = ((states_sum + output_own) / counted).astype(bf16)

    mine, theirs, new_slopes = tail(
        core, sums, refreshed, queries, kept_query, new_signs, new_balance[None, :]
    )
    slopes = kept_slopes.T + lax.dot_general(
        chosen.astype(bf16),
        new_slopes.astype(bf16),
        (((0,), (1,)), ((), ())),
        preferred_element_type=f32,
    ).astype(bf16)

    batch = queries.shape[0]
    near = ("y", "xh", "xl")
    part = mine + shift(theirs, "c", 2, 1)
    part = jnp.sum(
        lax.all_to_all(part.reshape(16, batch // 16, HALF), near, 0, 0, tiled=True), axis=0
    )
    part = jnp.sum(spread(part, "z", 8), axis=0)
    part = spread(part, near, 16).reshape(batch, HALF)
    back = shift(part, "c", 2, 1)
    label_grad, query_grad, loss = final(core, part, back, slopes, queries, owned * ndp * nmp)
    return (label_grad, query_grad, loss[0, 0])


def solution(mesh):
    grid = Mesh(mesh.devices.reshape(SIZES), AXES)
    in_specs = (
        P(DP, None),
        P(DP, None),
        P(),
        P(DP, MP),
        P(DP, MP),
        P(DP, MP),
        P(DP, MP),
        P(AXES, None),
        P(AXES),
        P(AXES),
        P(),
        P(),
    )
    out_specs = (P(AXES, None), P(), P())
    return jax.shard_map(shards, mesh=grid, in_specs=in_specs, out_specs=out_specs, check_vma=False)
```

```python
import functools
import math

import jax
import jax.numpy as jnp
import numpy as np
from jax import lax
from jax.experimental import pallas as pl
from jax.experimental.pallas import tpu as pltpu
from jax.sharding import Mesh, PartitionSpec as P

HEAD_WIDTH = 128

rope_theta = 1000000.0
norm_eps = 1e-06
focal_beta = 0.9999

AXES = ("z", "y", "xh", "xl", "c")
SIZES = (8, 4, 2, 2, 2)
DP = ("z", "y", "xh")
MP = ("xl", "c")
RING_X = ("xh", "xl")


BLOCK = 128
HALF = 1920
SENT = 1280


def rotary_tables(length):
    half = HEAD_WIDTH // 2
    frequency = rope_theta ** (-2.0 * np.arange(half) / HEAD_WIDTH)
    angles = np.arange(length)[:, None] * frequency[None, :]
    cosine = np.concatenate([np.cos(angles), np.cos(angles)], axis=1)
    sine = np.concatenate([-np.sin(angles), np.sin(angles)], axis=1)
    repeat = BLOCK // length
    return (
        jnp.asarray(np.tile(cosine, (repeat, 1)), jnp.float32),
        jnp.asarray(np.tile(sine, (repeat, 1)), jnp.float32),
    )


def norm_kernel(core_ref, states_ref, gain_ref, out_ref, turned_ref):
    states = states_ref[...].astype(jnp.float32)
    scaled = lax.rsqrt(jnp.mean(states * states, axis=1, keepdims=True) + norm_eps)
    turned_ref[...] = (states * scaled * gain_ref[...]).T
    rows = out_ref.shape[1] // 8

    def block(z, y):
        first = pl.multiple_of(((z * 4 + y) * 2 + core_ref[0]) * rows, 8)
        return turned_ref[pl.ds(first, rows), :]

    for y in range(4):
        for pair in range(4):
            out_ref[y, 2 * pair * rows : 2 * (pair + 1) * rows, :] = jnp.concatenate(
                [block(2 * pair, y), block(2 * pair + 1, y)], axis=0
            ).astype(jnp.bfloat16)


def norm_half(core, states, gain):
    tokens, width = states.shape
    block = 128
    return pl.pallas_call(
        norm_kernel,
        out_shape=jax.ShapeDtypeStruct((4, width // 8, tokens), jnp.bfloat16),
        grid_spec=pltpu.PrefetchScalarGridSpec(
            num_scalar_prefetch=1,
            grid=(tokens // block,),
            in_specs=[
                pl.BlockSpec((block, width), lambda i, _: (i, 0)),
                pl.BlockSpec((1, width), lambda i, _: (0, 0)),
            ],
            out_specs=pl.BlockSpec((4, width // 8, block), lambda i, _: (0, 0, i)),
            scratch_shapes=[pltpu.VMEM((width, block), jnp.float32)],
        ),
        compiler_params=pltpu.CompilerParams(vmem_limit_bytes=32 << 20),
        cost_estimate=pl.CostEstimate(
            flops=4 * tokens * width, bytes_accessed=3 * tokens * width, transcendentals=tokens
        ),
        name="norm",
    )(core.reshape(1).astype(jnp.int32), states, gain.reshape(1, width))


def near_kernel(place_ref, x_ref, w0_ref, w1_ref, w3_ref, out_ref):
    def dot(x, w):
        return lax.dot_general(
            x, w, (((0,), (0,)), ((), ())), preferred_element_type=jnp.float32
        )

    y = place_ref[0]
    out_ref[...] = (
        dot(x_ref[y], w0_ref[...])
        + dot(x_ref[(y + 1) % 4], w1_ref[...])
        + dot(x_ref[(y + 3) % 4], w3_ref[...])
    )


def far_kernel(place_ref, x_ref, near_ref, w2a_ref, w2b_ref, out_ref):
    def dot(x, w):
        return lax.dot_general(
            x, w, (((0,), (0,)), ((), ())), preferred_element_type=jnp.float32
        )

    half = w2a_ref.shape[0]
    far = x_ref[0]
    out_ref[...] = (
        near_ref[...] + dot(far[:half], w2a_ref[...]) + dot(far[half:], w2b_ref[...])
    ).astype(out_ref.dtype)


def project(y, x, pieces, near=None, dtype=jnp.float32):
    _, depth, tokens = x.shape
    columns = pieces[0].shape[1]
    block = tokens // 2
    fixed = [pl.BlockSpec(w.shape, lambda i, _: (0, 0)) for w in pieces]
    tile = pl.BlockSpec((block, columns), lambda i, _: (i, 0))
    if near is None:
        kernel, extra = near_kernel, ()
        x_spec = pl.BlockSpec((4, depth, block), lambda i, _: (0, 0, i))
    else:
        kernel, extra = far_kernel, (near,)
        x_spec = pl.BlockSpec((1, depth, block), lambda i, p: ((p[0] + 2) % 4, 0, i))
    used = sum(w.shape[0] for w in pieces)
    return pl.pallas_call(
        kernel,
        out_shape=jax.ShapeDtypeStruct((tokens, columns), dtype),
        grid_spec=pltpu.PrefetchScalarGridSpec(
            num_scalar_prefetch=1,
            grid=(tokens // block,),
            in_specs=[x_spec, *[tile for _ in extra], *fixed],
            out_specs=tile,
        ),
        compiler_params=pltpu.CompilerParams(vmem_limit_bytes=56 << 20),
        cost_estimate=pl.CostEstimate(
            flops=2 * used * tokens * columns,
            bytes_accessed=6 * tokens * columns + 2 * used * (tokens + columns),
            transcendentals=0,
        ),
        name="near" if near is None else "far",
    )(y.reshape(1).astype(jnp.int32), x, *extra, *pieces)


def attend_kernel(raw_ref, add_ref, allowed_ref, live_ref, member_ref, cos_ref, sin_ref, out_ref):
    width = HEAD_WIDTH
    cosine, sine = cos_ref[...], sin_ref[...]
    members = member_ref[...]
    heads = raw_ref.shape[1] // width - 2
    texts = members.shape[0] // heads

    def rotate(x):
        return (x * cosine + pltpu.roll(x, width // 2, 1) * sine).astype(jnp.bfloat16)

    for block in range(raw_ref.shape[0] // BLOCK):
        rows = slice(block * BLOCK, (block + 1) * BLOCK)

        def column(index):
            lanes = slice(index * width, (index + 1) * width)
            return raw_ref[rows, lanes] + add_ref[rows, lanes].astype(jnp.float32)

        allowed = jnp.concatenate([allowed_ref[rows, :]] * heads, axis=0)
        live = jnp.concatenate([live_ref[rows, :]] * heads, axis=0)
        keys = rotate(column(0))
        values = column(1).astype(jnp.bfloat16)
        rotated = jnp.concatenate([rotate(column(h + 2)) for h in range(heads)], axis=0)
        scores = lax.dot_general(
            rotated, keys, (((1,), (1,)), ((), ())), preferred_element_type=jnp.float32
        ) * (1.0 / math.sqrt(width))
        weights = jnp.where(allowed > 0.0, jnp.exp(scores), 0.0)
        total = jnp.sum(weights, axis=1, keepdims=True)
        probs = (weights * (live / total)).astype(jnp.bfloat16)
        shares = jnp.dot(members, probs, preferred_element_type=jnp.float32)
        high = shares.astype(jnp.bfloat16)
        low = (shares - high.astype(jnp.float32)).astype(jnp.bfloat16)
        pooled = jnp.dot(high, values, preferred_element_type=jnp.float32) + jnp.dot(
            low, values, preferred_element_type=jnp.float32
        )
        for head in range(heads):
            columns = slice(head * width, (head + 1) * width)
            out_ref[block * texts : (block + 1) * texts, columns] = pooled[
                head * texts : (head + 1) * texts
            ].astype(out_ref.dtype)


def attend_tables(text_ids):
    texts, length = text_ids.shape
    per = BLOCK // length
    live = (text_ids != 0).reshape(texts // per, BLOCK)
    place = np.arange(BLOCK)
    shape = (place[:, None] // length == place[None, :] // length) & (
        place[:, None] >= place[None, :]
    )
    allowed = (jnp.asarray(shape)[None] & live[:, None, :]).astype(jnp.float32)
    return allowed.reshape(-1, BLOCK), (text_ids != 0).astype(jnp.float32).reshape(-1, 1)


def attend_pooled(raw, add, allowed, live, length):
    tokens, columns = raw.shape
    texts = tokens // length
    per = BLOCK // length
    heads = columns // HEAD_WIDTH - 2
    owner = (np.arange(per)[:, None] == np.arange(BLOCK)[None, :] // length).astype(np.float32)
    members = jnp.asarray(np.kron(np.eye(heads), owner), jnp.bfloat16)
    cosine, sine = rotary_tables(length)
    step = 2 * BLOCK
    return pl.pallas_call(
        attend_kernel,
        out_shape=jax.ShapeDtypeStruct((texts, heads * HEAD_WIDTH), jnp.bfloat16),
        grid=(tokens // step,),
        in_specs=[
            pl.BlockSpec((step, columns), lambda i: (i, 0)),
            pl.BlockSpec((step, columns), lambda i: (i, 0)),
            pl.BlockSpec((step, BLOCK), lambda i: (i, 0)),
            pl.BlockSpec((step, 1), lambda i: (i, 0)),
            pl.BlockSpec(members.shape, lambda i: (0, 0)),
            pl.BlockSpec((BLOCK, HEAD_WIDTH), lambda i: (0, 0)),
            pl.BlockSpec((BLOCK, HEAD_WIDTH), lambda i: (0, 0)),
        ],
        out_specs=pl.BlockSpec((2 * per, heads * HEAD_WIDTH), lambda i: (i, 0)),
        compiler_params=pltpu.CompilerParams(vmem_limit_bytes=56 << 20),
        cost_estimate=pl.CostEstimate(
            flops=4 * tokens * BLOCK * heads * HEAD_WIDTH,
            bytes_accessed=raw.size * 8,
            transcendentals=tokens * BLOCK * heads,
        ),
        name="attend",
    )(
        raw,
        add,
        allowed,
        live,
        members,
        cosine,
        sine,
    )


def shift(x, axis, size, by):
    return lax.ppermute(x, axis, [(i, (i + by) % size) for i in range(size)])


def ring_near(own):
    return shift(own, "y", 4, -1), shift(own, "y", 4, 1)


def ring_far(up, down):
    half = up.shape[0] // 2
    return shift(up[:half], "y", 4, -1), shift(down[half:], "y", 4, 1)


def in_order(parts, index):
    n = len(parts)
    out = jnp.zeros((n,) + parts[0].shape, parts[0].dtype)
    for d, part in enumerate(parts):
        out = lax.dynamic_update_slice_in_dim(out, part[None], (index + d) % n, 0)
    return out


def spread(x, axes, size):
    return lax.all_to_all(jnp.broadcast_to(x[None], (size,) + x.shape), axes, 0, 0, tiled=True)


def focal(margin):
    missed = jax.nn.sigmoid(-margin)
    softened = jnp.maximum(-margin, 0.0) + jnp.log1p(jnp.exp(-jnp.abs(margin)))
    return missed * missed * softened, -(missed * missed) * (
        2.0 * jax.nn.sigmoid(margin) * softened + missed
    )


def tail_kernel(core_ref, sums_ref, new_ref, queries_ref, kept_ref, signs_ref, balance_ref, mine_ref, theirs_ref, slopes_ref):
    batch, width = queries_ref.shape
    rows = new_ref[...]
    logits = lax.dot_general(
        queries_ref[...], rows, (((1,), (1,)), ((), ())), preferred_element_type=jnp.float32
    ) / math.sqrt(width)
    signs = signs_ref[...]
    balance = balance_ref[...]
    terms, slope = focal(signs * logits)
    losses = jnp.sum(balance * terms, axis=1, keepdims=True) + sums_ref[0] / batch
    slopes = (balance * signs * slope).astype(jnp.bfloat16)
    slopes_ref[...] = slopes.astype(jnp.float32)
    left = kept_ref[:, :HALF] + jnp.dot(slopes, rows[:, :HALF], preferred_element_type=jnp.float32)
    right = kept_ref[:, HALF:] + jnp.dot(slopes, rows[:, HALF:], preferred_element_type=jnp.float32)
    rest = width - HALF
    lanes = (2 * HALF - width) // 2
    loss_lanes = jnp.broadcast_to(losses, (batch, lanes))
    class_lanes = jnp.full((batch, lanes), sums_ref[1] / batch, jnp.float32)

    def write(first, second):
        first[...] = left
        second[:, :rest] = right
        second[:, rest : rest + lanes] = loss_lanes
        second[:, rest + lanes :] = class_lanes

    @pl.when(core_ref[0] == 0)
    def _():
        write(mine_ref, theirs_ref)

    @pl.when(core_ref[0] != 0)
    def _():
        write(theirs_ref, mine_ref)


def tail(core, sums, rows, queries, kept, signs, balance):
    batch, width = queries.shape
    smem = pl.BlockSpec(memory_space=pltpu.SMEM)
    vmem = pl.BlockSpec(memory_space=pltpu.VMEM)
    half = jax.ShapeDtypeStruct((batch, HALF), jnp.float32)
    return pl.pallas_call(
        tail_kernel,
        out_shape=(half, half, jax.ShapeDtypeStruct((batch, rows.shape[0]), jnp.float32)),
        in_specs=[smem, smem, vmem, vmem, vmem, vmem, vmem],
        out_specs=(vmem, vmem, vmem),
        compiler_params=pltpu.CompilerParams(vmem_limit_bytes=24 << 20),
        cost_estimate=pl.CostEstimate(
            flops=4 * batch * width * rows.shape[0],
            bytes_accessed=10 * batch * width,
            transcendentals=8 * batch,
        ),
        name="tail",
    )(core.reshape(1).astype(jnp.int32), sums, rows, queries, kept, signs, balance)


def final_kernel(core_ref, part_ref, back_ref, slopes_ref, queries_ref, label_ref, query_ref, loss_ref, *, labels):
    batch, width = queries_ref.shape
    rest = width - HALF
    lanes = (2 * HALF - width) // 2
    first = core_ref[0] == 0
    step = pl.program_id(0)
    rows = pl.ds(pl.multiple_of(step * query_ref.shape[0], 16), query_ref.shape[0])

    def side(left_ref, right_ref):
        extra = jnp.sum(right_ref[:, rest:].astype(jnp.float32), axis=0, keepdims=True)
        losses = jnp.sum(extra[:, :lanes]) / (lanes // 2)
        weights = jnp.sum(extra[:, lanes:]) / (lanes // 2)
        factor = labels / weights
        scale = factor / math.sqrt(width)
        loss_ref[...] = jnp.full(loss_ref.shape, factor * losses / (batch * labels), jnp.float32)
        query_ref[:, :HALF] = scale * left_ref[rows, :].astype(jnp.float32)
        query_ref[:, HALF:] = scale * right_ref[rows, :rest].astype(jnp.float32)
        label_ref[...] = scale * lax.dot_general(
            slopes_ref[...],
            queries_ref[...],
            (((1,), (0,)), ((), ())),
            preferred_element_type=jnp.float32,
        )

    @pl.when(first)
    def _():
        side(part_ref, back_ref)

    @pl.when(jnp.logical_not(first))
    def _():
        side(back_ref, part_ref)


def final(core, part, back, slopes, queries, labels):
    batch, width = queries.shape
    owned = slopes.shape[0]
    steps = 4
    whole = lambda x: pl.BlockSpec(x.shape, lambda i, _: (0, 0))
    return pl.pallas_call(
        functools.partial(final_kernel, labels=labels),
        out_shape=(
            jax.ShapeDtypeStruct((owned, width), jnp.float32),
            jax.ShapeDtypeStruct((batch, width), jnp.float32),
            jax.ShapeDtypeStruct((8, 128), jnp.float32),
        ),
        grid_spec=pltpu.PrefetchScalarGridSpec(
            num_scalar_prefetch=1,
            grid=(steps,),
            in_specs=[
                whole(part),
                whole(back),
                pl.BlockSpec((owned // steps, batch), lambda i, _: (i, 0)),
                whole(queries),
            ],
            out_specs=(
                pl.BlockSpec((owned // steps, width), lambda i, _: (i, 0)),
                pl.BlockSpec((batch // steps, width), lambda i, _: (i, 0)),
                pl.BlockSpec((8, 128), lambda i, _: (0, 0)),
            ),
        ),
        compiler_params=pltpu.CompilerParams(vmem_limit_bytes=32 << 20),
        name="final",
    )(core.reshape(1).astype(jnp.int32), part, back, slopes, queries)


def shards(
    hidden_states,
    token_ids,
    norm_gain,
    q_weight,
    key_matrix,
    value_matrix,
    out_weight,
    label_table,
    refresh_rows,
    label_counts,
    queries,
    positives,
):
    f32, bf16 = jnp.float32, jnp.bfloat16
    width = hidden_states.shape[1]
    texts, length = token_ids.shape
    xh, core = lax.axis_index("xh"), lax.axis_index("c")
    member = lax.axis_index(MP)
    ndp, nmp = 64, 4
    rows = q_weight.shape[0]

    def to_group(block, by):
        return lax.ppermute(
            block,
            ("y", "xh", "xl", "c"),
            [
                (8 * v + 4 * h + 2 * l + k, 8 * ((v - by) % 4) + 4 * l + 2 * k + h)
                for v in range(4)
                for h in (0, 1)
                for l in (0, 1)
                for k in (0, 1)
            ],
        )

    y = lax.axis_index("y")
    packed = jnp.concatenate([key_matrix, value_matrix, q_weight], axis=1)
    cut = packed.shape[1]
    moved = to_group(jnp.concatenate([packed, out_weight[:, : SENT - cut]], axis=1), 0)
    half = norm_half(core, hidden_states, norm_gain)
    moved, half, out_weight = lax.optimization_barrier((moved, half, out_weight))
    in_z = lax.all_gather(moved, "z", axis=0, tiled=True)
    out_y = in_order([to_group(out_weight, d) for d in range(4)], y)
    out_all = lax.all_gather(out_y.reshape(4 * rows, -1), "z", axis=0, tiled=True)
    facing = [(i, 3 - i) for i in range(4)]
    half_other = lax.ppermute(half, RING_X, facing)
    ids_other = lax.ppermute(token_ids, RING_X, facing)

    balance = (1.0 - focal_beta) / -jnp.expm1(
        label_counts.astype(f32) * math.log(focal_beta)
    )
    owned = label_table.shape[0]
    root = math.sqrt(width)
    first_label = (lax.axis_index(DP) * nmp + member) * owned
    own_rows = jnp.arange(owned, dtype=jnp.int32)
    chosen = refresh_rows[:, None] == own_rows[None, :]
    kept = ~jnp.any(chosen, axis=0)
    kept_balance = jnp.where(kept, balance, 0.0)
    matched = jnp.any(positives[:, :, None] == (first_label + own_rows)[None, None, :], axis=1)
    signs = jnp.where(matched, 1.0, -1.0)
    logits = (
        lax.dot_general(
            queries, label_table, (((1,), (1,)), ((), ())), preferred_element_type=f32
        )
        / root
    )
    terms, slope = focal(signs * logits)
    kept_loss = jnp.sum(kept_balance[None, :] * terms)
    kept_slopes = (kept_balance[None, :] * signs * slope).astype(bf16)
    kept_query = jnp.dot(kept_slopes, label_table, preferred_element_type=f32)
    new_balance = jnp.sum(jnp.where(chosen, balance[None, :], 0.0), axis=1)
    new_signs = jnp.where(
        jnp.any(positives[:, :, None] == (first_label + refresh_rows)[None, None, :], axis=1),
        1.0,
        -1.0,
    )

    live = (token_ids != 0).astype(f32)
    share = texts // nmp
    live_own = lax.dynamic_slice_in_dim(live, member * share, share, 0)
    states_own = lax.dynamic_slice_in_dim(
        hidden_states, member * share * length, share * length, 0
    ).reshape(share, length, width)
    counted = jnp.sum(live_own, axis=1, keepdims=True)
    states_sum = jnp.sum(states_own.astype(f32) * live_own[:, :, None], axis=1)

    keeps = xh == core
    give = jnp.where(keeps, half_other, half)
    keep = jnp.where(keeps, half, half_other)
    ids = jnp.where(keeps, token_ids, ids_other)

    allowed, live_rows = attend_tables(ids)
    early = (kept_slopes, kept_loss, new_balance, new_signs, chosen, allowed, live_rows)
    in_z, early = lax.optimization_barrier((in_z, early))
    kept_slopes, kept_loss, new_balance, new_signs, chosen, allowed, live_rows = early
    sums = jnp.stack([kept_loss, jnp.sum(balance)])

    own = in_z[:, :cut]
    up, down = ring_near(own)
    far = ring_far(up, down)
    near = (own, up, down)
    give_near, keep_near = project(y, give, near), project(y, keep, near)
    early = (kept_query, sums, states_sum, counted, give_near, keep_near)
    far, early = lax.optimization_barrier((far, early))
    kept_query, sums, states_sum, counted, give_near, keep_near = early
    taken = shift(project(y, give, far, give_near, bf16), "c", 2, 1)
    raw = project(y, keep, far, keep_near)
    pooled = attend_pooled(raw, taken, allowed, live_rows, length)

    pooled_other = shift(pooled, "c", 2, 1)
    both = jnp.concatenate(
        [jnp.where(core == 0, pooled, pooled_other), jnp.where(core == 0, pooled_other, pooled)],
        axis=0,
    )
    head_terms = lax.dot_general(
        both, out_all, (((1,), (1,)), ((), ())), preferred_element_type=f32
    )
    exchanged = lax.all_to_all(
        head_terms.astype(bf16).reshape(8, share, -1), ("xh", "xl", "c"), 0, 0, tiled=True
    )
    summed = jnp.sum(exchanged.astype(f32).reshape(nmp, 2, share, -1), axis=0)
    output_own = (
        summed.reshape(2, share, ndp // 2, rows).transpose(1, 2, 0, 3).reshape(share, width)
    )
    refreshed = ((states_sum + output_own) / counted).astype(bf16)

    mine, theirs, new_slopes = tail(
        core, sums, refreshed, queries, kept_query, new_signs, new_balance[None, :]
    )
    slopes = kept_slopes.T + lax.dot_general(
        chosen.astype(bf16),
        new_slopes.astype(bf16),
        (((0,), (1,)), ((), ())),
        preferred_element_type=f32,
    ).astype(bf16)

    batch = queries.shape[0]
    plane = ("y", "xh", "xl")
    part = mine + shift(theirs, "c", 2, 1)
    part = jnp.sum(
        lax.all_to_all(part.reshape(16, batch // 16, HALF), plane, 0, 0, tiled=True), axis=0
    )
    part = jnp.sum(spread(part, "z", 8), axis=0)
    lane = lax.broadcasted_iota(jnp.int32, part.shape, 1)
    spare = (lane >= width - HALF) & (lane % 128 >= 64) & (core == 1)
    low = part - lax.reduce_precision(part, 8, 7)
    part = jnp.where(spare, low, part).astype(bf16)
    part = spread(part, plane, 16).reshape(batch, HALF)
    back = shift(part, "c", 2, 1)
    label_grad, query_grad, loss = final(core, part, back, slopes, queries, owned * ndp * nmp)
    return (label_grad, query_grad, loss[0, 0])


def solution(mesh):
    grid = Mesh(mesh.devices.reshape(SIZES), AXES)
    in_specs = (
        P(DP, None),
        P(DP, None),
        P(),
        P(DP, MP),
        P(DP, MP),
        P(DP, MP),
        P(DP, MP),
        P(AXES, None),
        P(AXES),
        P(AXES),
        P(),
        P(),
    )
    out_specs = (P(AXES, None), P(), P())
    return jax.shard_map(shards, mesh=grid, in_specs=in_specs, out_specs=out_specs, check_vma=False)
```

```python
import functools
import math

import jax
import jax.numpy as jnp
import numpy as np
from jax import lax
from jax.experimental import pallas as pl
from jax.experimental.pallas import tpu as pltpu
from jax.sharding import Mesh, PartitionSpec as P

HEAD_WIDTH = 128

rope_theta = 1000000.0
norm_eps = 1e-06
focal_beta = 0.9999

AXES = ("z", "y", "xh", "xl", "c")
SIZES = (8, 4, 2, 2, 2)
DP = ("z", "y", "xh")
MP = ("xl", "c")
RING_X = ("xh", "xl")


BLOCK = 128
HALF = 1920
SENT = 1280


def rotary_tables(length):
    half = HEAD_WIDTH // 2
    frequency = rope_theta ** (-2.0 * np.arange(half) / HEAD_WIDTH)
    angles = np.arange(length)[:, None] * frequency[None, :]
    cosine = np.concatenate([np.cos(angles), np.cos(angles)], axis=1)
    sine = np.concatenate([-np.sin(angles), np.sin(angles)], axis=1)
    repeat = BLOCK // length
    return (
        jnp.asarray(np.tile(cosine, (repeat, 1)), jnp.float32),
        jnp.asarray(np.tile(sine, (repeat, 1)), jnp.float32),
    )


def norm_kernel(core_ref, states_ref, gain_ref, out_ref, turned_ref):
    states = states_ref[...].astype(jnp.float32)
    scaled = lax.rsqrt(jnp.mean(states * states, axis=1, keepdims=True) + norm_eps)
    turned_ref[...] = (states * scaled * gain_ref[...]).T
    rows = out_ref.shape[1] // 8

    def block(z, y):
        first = pl.multiple_of(((z * 4 + y) * 2 + core_ref[0]) * rows, 8)
        return turned_ref[pl.ds(first, rows), :]

    for y in range(4):
        for pair in range(4):
            out_ref[y, 2 * pair * rows : 2 * (pair + 1) * rows, :] = jnp.concatenate(
                [block(2 * pair, y), block(2 * pair + 1, y)], axis=0
            ).astype(jnp.bfloat16)


def norm_half(core, states, gain):
    tokens, width = states.shape
    block = 128
    return pl.pallas_call(
        norm_kernel,
        out_shape=jax.ShapeDtypeStruct((4, width // 8, tokens), jnp.bfloat16),
        grid_spec=pltpu.PrefetchScalarGridSpec(
            num_scalar_prefetch=1,
            grid=(tokens // block,),
            in_specs=[
                pl.BlockSpec((block, width), lambda i, _: (i, 0)),
                pl.BlockSpec((1, width), lambda i, _: (0, 0)),
            ],
            out_specs=pl.BlockSpec((4, width // 8, block), lambda i, _: (0, 0, i)),
            scratch_shapes=[pltpu.VMEM((width, block), jnp.float32)],
        ),
        compiler_params=pltpu.CompilerParams(vmem_limit_bytes=32 << 20),
        cost_estimate=pl.CostEstimate(
            flops=4 * tokens * width, bytes_accessed=3 * tokens * width, transcendentals=tokens
        ),
        name="norm",
    )(core.reshape(1).astype(jnp.int32), states, gain.reshape(1, width))


def project_kernel(place_ref, *refs, pieces, seeded):
    out_ref = refs[-1]
    total = refs[3 * pieces][...] if seeded else None
    first = place_ref[1] != 0
    for index in range(pieces):
        x = jnp.where(first, refs[index][0], refs[pieces + index][0])
        w = refs[2 * pieces + index][...]
        term = lax.dot_general(
            x, w, (((0,), (0,)), ((), ())), preferred_element_type=jnp.float32
        )
        total = term if total is None else total + term
    out_ref[...] = total.astype(out_ref.dtype)


def project(y, first, x, pieces, near=None, dtype=jnp.float32):
    _, depth, tokens = x[0].shape
    columns = pieces[0][2].shape[1]
    block = tokens // 2
    extra = () if near is None else (near,)
    tile = pl.BlockSpec((block, columns), lambda i, _: (i, 0))

    def x_spec(distance, part, w):
        return pl.BlockSpec(
            (1, w.shape[0], block), lambda i, p: ((p[0] + distance) % 4, part, i)
        )

    weights = [w for _, _, w in pieces]
    used = sum(w.shape[0] for w in weights)
    return pl.pallas_call(
        functools.partial(project_kernel, pieces=len(pieces), seeded=near is not None),
        out_shape=jax.ShapeDtypeStruct((tokens, columns), dtype),
        grid_spec=pltpu.PrefetchScalarGridSpec(
            num_scalar_prefetch=1,
            grid=(tokens // block,),
            in_specs=[
                *[x_spec(*piece) for piece in pieces],
                *[x_spec(*piece) for piece in pieces],
                *[pl.BlockSpec(w.shape, lambda i, _: (0, 0)) for w in weights],
                *[tile for _ in extra],
            ],
            out_specs=tile,
        ),
        compiler_params=pltpu.CompilerParams(vmem_limit_bytes=56 << 20),
        cost_estimate=pl.CostEstimate(
            flops=2 * used * tokens * columns,
            bytes_accessed=6 * tokens * columns + 2 * used * (tokens + columns),
            transcendentals=0,
        ),
        name="project",
    )(
        jnp.stack([y, first]).astype(jnp.int32),
        *[x[0] for _ in pieces],
        *[x[1] for _ in pieces],
        *weights,
        *extra,
    )


def attend_kernel(raw_ref, add_ref, allowed_ref, live_ref, member_ref, cos_ref, sin_ref, out_ref):
    width = HEAD_WIDTH
    cosine, sine = cos_ref[...], sin_ref[...]
    members = member_ref[...]
    heads = raw_ref.shape[1] // width - 2
    texts = members.shape[0] // heads

    def rotate(x):
        return (x * cosine + pltpu.roll(x, width // 2, 1) * sine).astype(jnp.bfloat16)

    for block in range(raw_ref.shape[0] // BLOCK):
        rows = slice(block * BLOCK, (block + 1) * BLOCK)

        def column(index):
            lanes = slice(index * width, (index + 1) * width)
            return raw_ref[rows, lanes] + add_ref[rows, lanes].astype(jnp.float32)

        allowed = jnp.concatenate([allowed_ref[rows, :]] * heads, axis=0)
        live = jnp.concatenate([live_ref[rows, :]] * heads, axis=0)
        keys = rotate(column(0))
        values = column(1).astype(jnp.bfloat16)
        rotated = jnp.concatenate([rotate(column(h + 2)) for h in range(heads)], axis=0)
        scores = lax.dot_general(
            rotated, keys, (((1,), (1,)), ((), ())), preferred_element_type=jnp.float32
        ) * (1.0 / math.sqrt(width))
        weights = jnp.where(allowed > 0.0, jnp.exp(scores), 0.0)
        total = jnp.sum(weights, axis=1, keepdims=True)
        probs = (weights * (live / total)).astype(jnp.bfloat16)
        shares = jnp.dot(members, probs, preferred_element_type=jnp.float32)
        high = shares.astype(jnp.bfloat16)
        low = (shares - high.astype(jnp.float32)).astype(jnp.bfloat16)
        pooled = jnp.dot(high, values, preferred_element_type=jnp.float32) + jnp.dot(
            low, values, preferred_element_type=jnp.float32
        )
        for head in range(heads):
            columns = slice(head * width, (head + 1) * width)
            out_ref[block * texts : (block + 1) * texts, columns] = pooled[
                head * texts : (head + 1) * texts
            ].astype(out_ref.dtype)


def attend_tables(text_ids):
    texts, length = text_ids.shape
    per = BLOCK // length
    live = (text_ids != 0).reshape(texts // per, BLOCK)
    place = np.arange(BLOCK)
    shape = (place[:, None] // length == place[None, :] // length) & (
        place[:, None] >= place[None, :]
    )
    allowed = (jnp.asarray(shape)[None] & live[:, None, :]).astype(jnp.float32)
    return allowed.reshape(-1, BLOCK), (text_ids != 0).astype(jnp.float32).reshape(-1, 1)


def attend_pooled(raw, add, allowed, live, length):
    tokens, columns = raw.shape
    texts = tokens // length
    per = BLOCK // length
    heads = columns // HEAD_WIDTH - 2
    owner = (np.arange(per)[:, None] == np.arange(BLOCK)[None, :] // length).astype(np.float32)
    members = jnp.asarray(np.kron(np.eye(heads), owner), jnp.bfloat16)
    cosine, sine = rotary_tables(length)
    step = 2 * BLOCK
    return pl.pallas_call(
        attend_kernel,
        out_shape=jax.ShapeDtypeStruct((texts, heads * HEAD_WIDTH), jnp.bfloat16),
        grid=(tokens // step,),
        in_specs=[
            pl.BlockSpec((step, columns), lambda i: (i, 0)),
            pl.BlockSpec((step, columns), lambda i: (i, 0)),
            pl.BlockSpec((step, BLOCK), lambda i: (i, 0)),
            pl.BlockSpec((step, 1), lambda i: (i, 0)),
            pl.BlockSpec(members.shape, lambda i: (0, 0)),
            pl.BlockSpec((BLOCK, HEAD_WIDTH), lambda i: (0, 0)),
            pl.BlockSpec((BLOCK, HEAD_WIDTH), lambda i: (0, 0)),
        ],
        out_specs=pl.BlockSpec((2 * per, heads * HEAD_WIDTH), lambda i: (i, 0)),
        compiler_params=pltpu.CompilerParams(vmem_limit_bytes=56 << 20),
        cost_estimate=pl.CostEstimate(
            flops=4 * tokens * BLOCK * heads * HEAD_WIDTH,
            bytes_accessed=raw.size * 8,
            transcendentals=tokens * BLOCK * heads,
        ),
        name="attend",
    )(
        raw,
        add,
        allowed,
        live,
        members,
        cosine,
        sine,
    )


def shift(x, axis, size, by):
    return lax.ppermute(x, axis, [(i, (i + by) % size) for i in range(size)])


def ring_near(own):
    return shift(own, "y", 4, -1), shift(own, "y", 4, 1)


def ring_far(up, down):
    half = up.shape[0] // 2
    return shift(up[:half], "y", 4, -1), shift(down[half:], "y", 4, 1)


def in_order(parts, index):
    n = len(parts)
    out = jnp.zeros((n,) + parts[0].shape, parts[0].dtype)
    for d, part in enumerate(parts):
        out = lax.dynamic_update_slice_in_dim(out, part[None], (index + d) % n, 0)
    return out


def spread(x, axes, size):
    return lax.all_to_all(jnp.broadcast_to(x[None], (size,) + x.shape), axes, 0, 0, tiled=True)


def focal(margin):
    missed = jax.nn.sigmoid(-margin)
    softened = jnp.maximum(-margin, 0.0) + jnp.log1p(jnp.exp(-jnp.abs(margin)))
    return missed * missed * softened, -(missed * missed) * (
        2.0 * jax.nn.sigmoid(margin) * softened + missed
    )


def tail_kernel(core_ref, sums_ref, new_ref, queries_ref, kept_ref, signs_ref, balance_ref, mine_ref, theirs_ref, slopes_ref):
    batch, width = queries_ref.shape
    rows = new_ref[...]
    logits = lax.dot_general(
        queries_ref[...], rows, (((1,), (1,)), ((), ())), preferred_element_type=jnp.float32
    ) / math.sqrt(width)
    signs = signs_ref[...]
    balance = balance_ref[...]
    terms, slope = focal(signs * logits)
    losses = jnp.sum(balance * terms, axis=1, keepdims=True) + sums_ref[0] / batch
    slopes = (balance * signs * slope).astype(jnp.bfloat16)
    slopes_ref[...] = slopes.astype(jnp.float32)
    left = kept_ref[:, :HALF] + jnp.dot(slopes, rows[:, :HALF], preferred_element_type=jnp.float32)
    right = kept_ref[:, HALF:] + jnp.dot(slopes, rows[:, HALF:], preferred_element_type=jnp.float32)
    rest = width - HALF
    lanes = (2 * HALF - width) // 2
    loss_lanes = jnp.broadcast_to(losses, (batch, lanes))
    class_lanes = jnp.full((batch, lanes), sums_ref[1] / batch, jnp.float32)

    def write(first, second):
        first[...] = left
        second[:, :rest] = right
        second[:, rest : rest + lanes] = loss_lanes
        second[:, rest + lanes :] = class_lanes

    @pl.when(core_ref[0] == 0)
    def _():
        write(mine_ref, theirs_ref)

    @pl.when(core_ref[0] != 0)
    def _():
        write(theirs_ref, mine_ref)


def tail(core, sums, rows, queries, kept, signs, balance):
    batch, width = queries.shape
    smem = pl.BlockSpec(memory_space=pltpu.SMEM)
    vmem = pl.BlockSpec(memory_space=pltpu.VMEM)
    half = jax.ShapeDtypeStruct((batch, HALF), jnp.float32)
    return pl.pallas_call(
        tail_kernel,
        out_shape=(half, half, jax.ShapeDtypeStruct((batch, rows.shape[0]), jnp.float32)),
        in_specs=[smem, smem, vmem, vmem, vmem, vmem, vmem],
        out_specs=(vmem, vmem, vmem),
        compiler_params=pltpu.CompilerParams(vmem_limit_bytes=24 << 20),
        cost_estimate=pl.CostEstimate(
            flops=4 * batch * width * rows.shape[0],
            bytes_accessed=10 * batch * width,
            transcendentals=8 * batch,
        ),
        name="tail",
    )(core.reshape(1).astype(jnp.int32), sums, rows, queries, kept, signs, balance)


def final_kernel(core_ref, part_ref, back_ref, slopes_ref, queries_ref, label_ref, query_ref, loss_ref, *, labels):
    batch, width = queries_ref.shape
    rest = width - HALF
    lanes = (2 * HALF - width) // 2
    first = core_ref[0] == 0
    step = pl.program_id(0)
    rows = pl.ds(pl.multiple_of(step * query_ref.shape[0], 16), query_ref.shape[0])

    def side(left_ref, right_ref):
        extra = jnp.sum(right_ref[:, rest:].astype(jnp.float32), axis=0, keepdims=True)
        losses = jnp.sum(extra[:, :lanes]) / (lanes // 2)
        weights = jnp.sum(extra[:, lanes:]) / (lanes // 2)
        factor = labels / weights
        scale = factor / math.sqrt(width)
        loss_ref[...] = jnp.full(loss_ref.shape, factor * losses / (batch * labels), jnp.float32)
        query_ref[:, :HALF] = scale * left_ref[rows, :].astype(jnp.float32)
        query_ref[:, HALF:] = scale * right_ref[rows, :rest].astype(jnp.float32)
        label_ref[...] = scale * lax.dot_general(
            slopes_ref[...],
            queries_ref[...],
            (((1,), (0,)), ((), ())),
            preferred_element_type=jnp.float32,
        )

    @pl.when(first)
    def _():
        side(part_ref, back_ref)

    @pl.when(jnp.logical_not(first))
    def _():
        side(back_ref, part_ref)


def final(core, part, back, slopes, queries, labels):
    batch, width = queries.shape
    owned = slopes.shape[0]
    steps = 4
    whole = lambda x: pl.BlockSpec(x.shape, lambda i, _: (0, 0))
    return pl.pallas_call(
        functools.partial(final_kernel, labels=labels),
        out_shape=(
            jax.ShapeDtypeStruct((owned, width), jnp.float32),
            jax.ShapeDtypeStruct((batch, width), jnp.float32),
            jax.ShapeDtypeStruct((8, 128), jnp.float32),
        ),
        grid_spec=pltpu.PrefetchScalarGridSpec(
            num_scalar_prefetch=1,
            grid=(steps,),
            in_specs=[
                whole(part),
                whole(back),
                pl.BlockSpec((owned // steps, batch), lambda i, _: (i, 0)),
                whole(queries),
            ],
            out_specs=(
                pl.BlockSpec((owned // steps, width), lambda i, _: (i, 0)),
                pl.BlockSpec((batch // steps, width), lambda i, _: (i, 0)),
                pl.BlockSpec((8, 128), lambda i, _: (0, 0)),
            ),
        ),
        compiler_params=pltpu.CompilerParams(vmem_limit_bytes=32 << 20),
        name="final",
    )(core.reshape(1).astype(jnp.int32), part, back, slopes, queries)


def shards(
    hidden_states,
    token_ids,
    norm_gain,
    q_weight,
    key_matrix,
    value_matrix,
    out_weight,
    label_table,
    refresh_rows,
    label_counts,
    queries,
    positives,
):
    f32, bf16 = jnp.float32, jnp.bfloat16
    width = hidden_states.shape[1]
    texts, length = token_ids.shape
    xh, core = lax.axis_index("xh"), lax.axis_index("c")
    member = lax.axis_index(MP)
    ndp, nmp = 64, 4
    rows = q_weight.shape[0]

    def to_group(block, by):
        return lax.ppermute(
            block,
            ("y", "xh", "xl", "c"),
            [
                (8 * v + 4 * h + 2 * l + k, 8 * ((v - by) % 4) + 4 * l + 2 * k + h)
                for v in range(4)
                for h in (0, 1)
                for l in (0, 1)
                for k in (0, 1)
            ],
        )

    y = lax.axis_index("y")
    packed = jnp.concatenate([key_matrix, value_matrix, q_weight], axis=1)
    cut = packed.shape[1]
    moved = to_group(jnp.concatenate([packed, out_weight[:, : SENT - cut]], axis=1), 0)
    half = norm_half(core, hidden_states, norm_gain)
    moved, half, out_weight = lax.optimization_barrier((moved, half, out_weight))
    in_z = lax.all_gather(moved, "z", axis=0, tiled=True)
    out_y = in_order([to_group(out_weight, d) for d in range(4)], y)
    out_all = lax.all_gather(out_y.reshape(4 * rows, -1), "z", axis=0, tiled=True)
    facing = [(i, 3 - i) for i in range(4)]
    half_other = lax.ppermute(half, RING_X, facing)
    ids_other = lax.ppermute(token_ids, RING_X, facing)

    balance = (1.0 - focal_beta) / -jnp.expm1(
        label_counts.astype(f32) * math.log(focal_beta)
    )
    owned = label_table.shape[0]
    root = math.sqrt(width)
    first_label = (lax.axis_index(DP) * nmp + member) * owned
    own_rows = jnp.arange(owned, dtype=jnp.int32)
    chosen = refresh_rows[:, None] == own_rows[None, :]
    kept = ~jnp.any(chosen, axis=0)
    kept_balance = jnp.where(kept, balance, 0.0)
    matched = jnp.any(positives[:, :, None] == (first_label + own_rows)[None, None, :], axis=1)
    signs = jnp.where(matched, 1.0, -1.0)
    logits = (
        lax.dot_general(
            queries, label_table, (((1,), (1,)), ((), ())), preferred_element_type=f32
        )
        / root
    )
    terms, slope = focal(signs * logits)
    kept_loss = jnp.sum(kept_balance[None, :] * terms)
    kept_slopes = (kept_balance[None, :] * signs * slope).astype(bf16)
    kept_query = jnp.dot(kept_slopes, label_table, preferred_element_type=f32)
    new_balance = jnp.sum(jnp.where(chosen, balance[None, :], 0.0), axis=1)
    new_signs = jnp.where(
        jnp.any(positives[:, :, None] == (first_label + refresh_rows)[None, None, :], axis=1),
        1.0,
        -1.0,
    )

    live = (token_ids != 0).astype(f32)
    share = texts // nmp
    live_own = lax.dynamic_slice_in_dim(live, member * share, share, 0)
    states_own = lax.dynamic_slice_in_dim(
        hidden_states, member * share * length, share * length, 0
    ).reshape(share, length, width)
    counted = jnp.sum(live_own, axis=1, keepdims=True)
    states_sum = jnp.sum(states_own.astype(f32) * live_own[:, :, None], axis=1)

    keeps = xh == core
    sides = (half, half_other)
    keep, give = keeps.astype(jnp.int32), 1 - keeps.astype(jnp.int32)
    ids = jnp.where(keeps, token_ids, ids_other)

    allowed, live_rows = attend_tables(ids)
    early = (kept_slopes, kept_loss, new_balance, new_signs, chosen, allowed, live_rows)
    in_z, early = lax.optimization_barrier((in_z, early))
    kept_slopes, kept_loss, new_balance, new_signs, chosen, allowed, live_rows = early
    sums = jnp.stack([kept_loss, jnp.sum(balance)])

    own = in_z[:, :cut]
    up, down = ring_near(own)
    give_own = project(y, give, sides, [(0, 0, own)])
    keep_own = project(y, keep, sides, [(0, 0, own)])
    up, down, give_own, keep_own = lax.optimization_barrier((up, down, give_own, keep_own))
    far = ring_far(up, down)
    near = [(1, 0, up), (3, 0, down)]
    give_near = project(y, give, sides, near, give_own)
    keep_near = project(y, keep, sides, near, keep_own)
    early = (kept_query, sums, states_sum, counted, give_near, keep_near)
    weights, early = lax.optimization_barrier((far, early))
    far = [(2, part, w) for part, w in enumerate(weights)]
    kept_query, sums, states_sum, counted, give_near, keep_near = early
    taken = shift(project(y, give, sides, far, give_near, bf16), "c", 2, 1)
    raw = project(y, keep, sides, far, keep_near)
    pooled = attend_pooled(raw, taken, allowed, live_rows, length)

    pooled_other = shift(pooled, "c", 2, 1)
    both = jnp.concatenate(
        [jnp.where(core == 0, pooled, pooled_other), jnp.where(core == 0, pooled_other, pooled)],
        axis=0,
    )
    head_terms = lax.dot_general(
        both, out_all, (((1,), (1,)), ((), ())), preferred_element_type=f32
    )
    exchanged = lax.all_to_all(
        head_terms.astype(bf16).reshape(8, share, -1), ("xh", "xl", "c"), 0, 0, tiled=True
    )
    summed = jnp.sum(exchanged.astype(f32).reshape(nmp, 2, share, -1), axis=0)
    output_own = (
        summed.reshape(2, share, ndp // 2, rows).transpose(1, 2, 0, 3).reshape(share, width)
    )
    refreshed = ((states_sum + output_own) / counted).astype(bf16)

    mine, theirs, new_slopes = tail(
        core, sums, refreshed, queries, kept_query, new_signs, new_balance[None, :]
    )
    slopes = kept_slopes.T + lax.dot_general(
        chosen.astype(bf16),
        new_slopes.astype(bf16),
        (((0,), (1,)), ((), ())),
        preferred_element_type=f32,
    ).astype(bf16)

    batch = queries.shape[0]
    plane = ("y", "xh", "xl")
    part = mine + shift(theirs, "c", 2, 1)
    part = jnp.sum(
        lax.all_to_all(part.reshape(16, batch // 16, HALF), plane, 0, 0, tiled=True), axis=0
    )
    part = jnp.sum(spread(part, "z", 8), axis=0)
    lane = lax.broadcasted_iota(jnp.int32, part.shape, 1)
    spare = (lane >= width - HALF) & (lane % 128 >= 64) & (core == 1)
    low = part - lax.reduce_precision(part, 8, 7)
    part = jnp.where(spare, low, part).astype(bf16)
    part = spread(part, plane, 16).reshape(batch, HALF)
    back = shift(part, "c", 2, 1)
    label_grad, query_grad, loss = final(core, part, back, slopes, queries, owned * ndp * nmp)
    return (label_grad, query_grad, loss[0, 0])


def solution(mesh):
    grid = Mesh(mesh.devices.reshape(SIZES), AXES)
    in_specs = (
        P(DP, None),
        P(DP, None),
        P(),
        P(DP, MP),
        P(DP, MP),
        P(DP, MP),
        P(DP, MP),
        P(AXES, None),
        P(AXES),
        P(AXES),
        P(),
        P(),
    )
    out_specs = (P(AXES, None), P(), P())
    return jax.shard_map(shards, mesh=grid, in_specs=in_specs, out_specs=out_specs, check_vma=False)
```

```python
import functools
import math

import jax
import jax.numpy as jnp
import numpy as np
from jax import lax
from jax.experimental import pallas as pl
from jax.experimental.pallas import tpu as pltpu
from jax.sharding import Mesh, PartitionSpec as P

HEAD_WIDTH = 128

rope_theta = 1000000.0
norm_eps = 1e-06
focal_beta = 0.9999

AXES = ("z", "y", "xh", "xl", "c")
SIZES = (8, 4, 2, 2, 2)
DP = ("z", "y", "xh")
MP = ("xl", "c")
RING_X = ("xh", "xl")


BLOCK = 128
HALF = 1920
SENT = 1280


def rotary_tables(length):
    half = HEAD_WIDTH // 2
    frequency = rope_theta ** (-2.0 * np.arange(half) / HEAD_WIDTH)
    angles = np.arange(length)[:, None] * frequency[None, :]
    cosine = np.concatenate([np.cos(angles), np.cos(angles)], axis=1)
    sine = np.concatenate([-np.sin(angles), np.sin(angles)], axis=1)
    repeat = BLOCK // length
    return (
        jnp.asarray(np.tile(cosine, (repeat, 1)), jnp.float32),
        jnp.asarray(np.tile(sine, (repeat, 1)), jnp.float32),
    )


def norm_kernel(core_ref, states_ref, gain_ref, out_ref, turned_ref):
    states = states_ref[...].astype(jnp.float32)
    scaled = lax.rsqrt(jnp.mean(states * states, axis=1, keepdims=True) + norm_eps)
    turned_ref[...] = (states * scaled * gain_ref[...]).T
    rows = out_ref.shape[1] // 8

    def block(z, y):
        first = pl.multiple_of(((z * 4 + y) * 2 + core_ref[0]) * rows, 8)
        return turned_ref[pl.ds(first, rows), :]

    for y in range(4):
        for pair in range(4):
            out_ref[y, 2 * pair * rows : 2 * (pair + 1) * rows, :] = jnp.concatenate(
                [block(2 * pair, y), block(2 * pair + 1, y)], axis=0
            ).astype(jnp.bfloat16)


def norm_half(core, states, gain):
    tokens, width = states.shape
    block = 128
    return pl.pallas_call(
        norm_kernel,
        out_shape=jax.ShapeDtypeStruct((4, width // 8, tokens), jnp.bfloat16),
        grid_spec=pltpu.PrefetchScalarGridSpec(
            num_scalar_prefetch=1,
            grid=(tokens // block,),
            in_specs=[
                pl.BlockSpec((block, width), lambda i, _: (i, 0)),
                pl.BlockSpec((1, width), lambda i, _: (0, 0)),
            ],
            out_specs=pl.BlockSpec((4, width // 8, block), lambda i, _: (0, 0, i)),
            scratch_shapes=[pltpu.VMEM((width, block), jnp.float32)],
        ),
        compiler_params=pltpu.CompilerParams(vmem_limit_bytes=32 << 20),
        cost_estimate=pl.CostEstimate(
            flops=4 * tokens * width, bytes_accessed=3 * tokens * width, transcendentals=tokens
        ),
        name="norm",
    )(core.reshape(1).astype(jnp.int32), states, gain.reshape(1, width))


def near_kernel(place_ref, x_ref, w0_ref, w1_ref, w3_ref, out_ref):
    def dot(x, w):
        return lax.dot_general(
            x, w, (((0,), (0,)), ((), ())), preferred_element_type=jnp.float32
        )

    y = place_ref[0]
    out_ref[...] = (
        dot(x_ref[y], w0_ref[...])
        + dot(x_ref[(y + 1) % 4], w1_ref[...])
        + dot(x_ref[(y + 3) % 4], w3_ref[...])
    )


def far_kernel(place_ref, x_ref, near_ref, w2a_ref, w2b_ref, out_ref):
    def dot(x, w):
        return lax.dot_general(
            x, w, (((0,), (0,)), ((), ())), preferred_element_type=jnp.float32
        )

    half = w2a_ref.shape[0]
    far = x_ref[0]
    out_ref[...] = (
        near_ref[...] + dot(far[:half], w2a_ref[...]) + dot(far[half:], w2b_ref[...])
    ).astype(out_ref.dtype)


def whole_kernel(place_ref, x_ref, w0_ref, w1_ref, w3_ref, w2a_ref, w2b_ref, out_ref):
    def dot(x, w):
        return lax.dot_general(
            x, w, (((0,), (0,)), ((), ())), preferred_element_type=jnp.float32
        )

    y = place_ref[0]
    half = w2a_ref.shape[0]
    far = x_ref[(y + 2) % 4]
    out_ref[...] = (
        dot(x_ref[y], w0_ref[...])
        + dot(x_ref[(y + 1) % 4], w1_ref[...])
        + dot(x_ref[(y + 3) % 4], w3_ref[...])
        + dot(far[:half], w2a_ref[...])
        + dot(far[half:], w2b_ref[...])
    )


def project(y, x, pieces, near=None, dtype=jnp.float32):
    _, depth, tokens = x.shape
    columns = pieces[0].shape[1]
    block = tokens // 2
    fixed = [pl.BlockSpec(w.shape, lambda i, _: (0, 0)) for w in pieces]
    tile = pl.BlockSpec((block, columns), lambda i, _: (i, 0))
    if near is None:
        kernel, extra = near_kernel if len(pieces) == 3 else whole_kernel, ()
        x_spec = pl.BlockSpec((4, depth, block), lambda i, _: (0, 0, i))
    else:
        kernel, extra = far_kernel, (near,)
        x_spec = pl.BlockSpec((1, depth, block), lambda i, p: ((p[0] + 2) % 4, 0, i))
    used = sum(w.shape[0] for w in pieces)
    return pl.pallas_call(
        kernel,
        out_shape=jax.ShapeDtypeStruct((tokens, columns), dtype),
        grid_spec=pltpu.PrefetchScalarGridSpec(
            num_scalar_prefetch=1,
            grid=(tokens // block,),
            in_specs=[x_spec, *[tile for _ in extra], *fixed],
            out_specs=tile,
        ),
        compiler_params=pltpu.CompilerParams(vmem_limit_bytes=56 << 20),
        cost_estimate=pl.CostEstimate(
            flops=2 * used * tokens * columns,
            bytes_accessed=6 * tokens * columns + 2 * used * (tokens + columns),
            transcendentals=0,
        ),
        name="far" if near is not None else "near" if len(pieces) == 3 else "whole",
    )(y.reshape(1).astype(jnp.int32), x, *extra, *pieces)


def attend_kernel(raw_ref, add_ref, allowed_ref, live_ref, member_ref, cos_ref, sin_ref, out_ref):
    width = HEAD_WIDTH
    cosine, sine = cos_ref[...], sin_ref[...]
    members = member_ref[...]
    heads = raw_ref.shape[1] // width - 2
    texts = members.shape[0] // heads

    def rotate(x):
        return (x * cosine + pltpu.roll(x, width // 2, 1) * sine).astype(jnp.bfloat16)

    for block in range(raw_ref.shape[0] // BLOCK):
        rows = slice(block * BLOCK, (block + 1) * BLOCK)

        def column(index):
            lanes = slice(index * width, (index + 1) * width)
            return raw_ref[rows, lanes] + add_ref[rows, lanes].astype(jnp.float32)

        allowed = jnp.concatenate([allowed_ref[rows, :]] * heads, axis=0)
        live = jnp.concatenate([live_ref[rows, :]] * heads, axis=0)
        keys = rotate(column(0))
        values = column(1).astype(jnp.bfloat16)
        rotated = jnp.concatenate([rotate(column(h + 2)) for h in range(heads)], axis=0)
        scores = lax.dot_general(
            rotated, keys, (((1,), (1,)), ((), ())), preferred_element_type=jnp.float32
        ) * (1.0 / math.sqrt(width))
        weights = jnp.where(allowed > 0.0, jnp.exp(scores), 0.0)
        total = jnp.sum(weights, axis=1, keepdims=True)
        probs = (weights * (live / total)).astype(jnp.bfloat16)
        shares = jnp.dot(members, probs, preferred_element_type=jnp.float32)
        high = shares.astype(jnp.bfloat16)
        low = (shares - high.astype(jnp.float32)).astype(jnp.bfloat16)
        pooled = jnp.dot(high, values, preferred_element_type=jnp.float32) + jnp.dot(
            low, values, preferred_element_type=jnp.float32
        )
        for head in range(heads):
            columns = slice(head * width, (head + 1) * width)
            out_ref[block * texts : (block + 1) * texts, columns] = pooled[
                head * texts : (head + 1) * texts
            ].astype(out_ref.dtype)


def attend_tables(text_ids):
    texts, length = text_ids.shape
    per = BLOCK // length
    live = (text_ids != 0).reshape(texts // per, BLOCK)
    place = np.arange(BLOCK)
    shape = (place[:, None] // length == place[None, :] // length) & (
        place[:, None] >= place[None, :]
    )
    allowed = (jnp.asarray(shape)[None] & live[:, None, :]).astype(jnp.float32)
    return allowed.reshape(-1, BLOCK), (text_ids != 0).astype(jnp.float32).reshape(-1, 1)


def attend_pooled(raw, add, allowed, live, length):
    tokens, columns = raw.shape
    texts = tokens // length
    per = BLOCK // length
    heads = columns // HEAD_WIDTH - 2
    owner = (np.arange(per)[:, None] == np.arange(BLOCK)[None, :] // length).astype(np.float32)
    members = jnp.asarray(np.kron(np.eye(heads), owner), jnp.bfloat16)
    cosine, sine = rotary_tables(length)
    step = 2 * BLOCK
    return pl.pallas_call(
        attend_kernel,
        out_shape=jax.ShapeDtypeStruct((texts, heads * HEAD_WIDTH), jnp.bfloat16),
        grid=(tokens // step,),
        in_specs=[
            pl.BlockSpec((step, columns), lambda i: (i, 0)),
            pl.BlockSpec((step, columns), lambda i: (i, 0)),
            pl.BlockSpec((step, BLOCK), lambda i: (i, 0)),
            pl.BlockSpec((step, 1), lambda i: (i, 0)),
            pl.BlockSpec(members.shape, lambda i: (0, 0)),
            pl.BlockSpec((BLOCK, HEAD_WIDTH), lambda i: (0, 0)),
            pl.BlockSpec((BLOCK, HEAD_WIDTH), lambda i: (0, 0)),
        ],
        out_specs=pl.BlockSpec((2 * per, heads * HEAD_WIDTH), lambda i: (i, 0)),
        compiler_params=pltpu.CompilerParams(vmem_limit_bytes=56 << 20),
        cost_estimate=pl.CostEstimate(
            flops=4 * tokens * BLOCK * heads * HEAD_WIDTH,
            bytes_accessed=raw.size * 8,
            transcendentals=tokens * BLOCK * heads,
        ),
        name="attend",
    )(
        raw,
        add,
        allowed,
        live,
        members,
        cosine,
        sine,
    )


def shift(x, axis, size, by):
    return lax.ppermute(x, axis, [(i, (i + by) % size) for i in range(size)])


def ring_near(own):
    return shift(own, "y", 4, -1), shift(own, "y", 4, 1)


def ring_far(up, down):
    half = up.shape[0] // 2
    return shift(up[:half], "y", 4, -1), shift(down[half:], "y", 4, 1)


def in_order(parts, index):
    n = len(parts)
    out = jnp.zeros((n,) + parts[0].shape, parts[0].dtype)
    for d, part in enumerate(parts):
        out = lax.dynamic_update_slice_in_dim(out, part[None], (index + d) % n, 0)
    return out


def spread(x, axes, size):
    return lax.all_to_all(jnp.broadcast_to(x[None], (size,) + x.shape), axes, 0, 0, tiled=True)


def focal(margin):
    missed = jax.nn.sigmoid(-margin)
    softened = jnp.maximum(-margin, 0.0) + jnp.log1p(jnp.exp(-jnp.abs(margin)))
    return missed * missed * softened, -(missed * missed) * (
        2.0 * jax.nn.sigmoid(margin) * softened + missed
    )


def tail_kernel(core_ref, sums_ref, new_ref, queries_ref, kept_ref, signs_ref, balance_ref, mine_ref, theirs_ref, slopes_ref):
    batch, width = queries_ref.shape
    rows = new_ref[...]
    logits = lax.dot_general(
        queries_ref[...], rows, (((1,), (1,)), ((), ())), preferred_element_type=jnp.float32
    ) / math.sqrt(width)
    signs = signs_ref[...]
    balance = balance_ref[...]
    terms, slope = focal(signs * logits)
    losses = jnp.sum(balance * terms, axis=1, keepdims=True) + sums_ref[0] / batch
    slopes = (balance * signs * slope).astype(jnp.bfloat16)
    slopes_ref[...] = slopes.astype(jnp.float32)
    left = kept_ref[:, :HALF] + jnp.dot(slopes, rows[:, :HALF], preferred_element_type=jnp.float32)
    right = kept_ref[:, HALF:] + jnp.dot(slopes, rows[:, HALF:], preferred_element_type=jnp.float32)
    rest = width - HALF
    lanes = (2 * HALF - width) // 2
    loss_lanes = jnp.broadcast_to(losses, (batch, lanes))
    class_lanes = jnp.full((batch, lanes), sums_ref[1] / batch, jnp.float32)

    def write(first, second):
        first[...] = left
        second[:, :rest] = right
        second[:, rest : rest + lanes] = loss_lanes
        second[:, rest + lanes :] = class_lanes

    @pl.when(core_ref[0] == 0)
    def _():
        write(mine_ref, theirs_ref)

    @pl.when(core_ref[0] != 0)
    def _():
        write(theirs_ref, mine_ref)


def tail(core, sums, rows, queries, kept, signs, balance):
    batch, width = queries.shape
    smem = pl.BlockSpec(memory_space=pltpu.SMEM)
    vmem = pl.BlockSpec(memory_space=pltpu.VMEM)
    half = jax.ShapeDtypeStruct((batch, HALF), jnp.float32)
    return pl.pallas_call(
        tail_kernel,
        out_shape=(half, half, jax.ShapeDtypeStruct((batch, rows.shape[0]), jnp.float32)),
        in_specs=[smem, smem, vmem, vmem, vmem, vmem, vmem],
        out_specs=(vmem, vmem, vmem),
        compiler_params=pltpu.CompilerParams(vmem_limit_bytes=24 << 20),
        cost_estimate=pl.CostEstimate(
            flops=4 * batch * width * rows.shape[0],
            bytes_accessed=10 * batch * width,
            transcendentals=8 * batch,
        ),
        name="tail",
    )(core.reshape(1).astype(jnp.int32), sums, rows, queries, kept, signs, balance)


def final_kernel(core_ref, part_ref, back_ref, slopes_ref, queries_ref, label_ref, query_ref, loss_ref, *, labels):
    batch, width = queries_ref.shape
    rest = width - HALF
    lanes = (2 * HALF - width) // 2
    first = core_ref[0] == 0
    step = pl.program_id(0)
    rows = pl.ds(pl.multiple_of(step * query_ref.shape[0], 16), query_ref.shape[0])

    def side(left_ref, right_ref):
        extra = jnp.sum(right_ref[:, rest:].astype(jnp.float32), axis=0, keepdims=True)
        losses = jnp.sum(extra[:, :lanes]) / (lanes // 2)
        weights = jnp.sum(extra[:, lanes:]) / (lanes // 2)
        factor = labels / weights
        scale = factor / math.sqrt(width)
        loss_ref[...] = jnp.full(loss_ref.shape, factor * losses / (batch * labels), jnp.float32)
        query_ref[:, :HALF] = scale * left_ref[rows, :].astype(jnp.float32)
        query_ref[:, HALF:] = scale * right_ref[rows, :rest].astype(jnp.float32)
        label_ref[...] = scale * lax.dot_general(
            slopes_ref[...],
            queries_ref[...],
            (((1,), (0,)), ((), ())),
            preferred_element_type=jnp.float32,
        )

    @pl.when(first)
    def _():
        side(part_ref, back_ref)

    @pl.when(jnp.logical_not(first))
    def _():
        side(back_ref, part_ref)


def final(core, part, back, slopes, queries, labels):
    batch, width = queries.shape
    owned = slopes.shape[0]
    steps = 4
    whole = lambda x: pl.BlockSpec(x.shape, lambda i, _: (0, 0))
    return pl.pallas_call(
        functools.partial(final_kernel, labels=labels),
        out_shape=(
            jax.ShapeDtypeStruct((owned, width), jnp.float32),
            jax.ShapeDtypeStruct((batch, width), jnp.float32),
            jax.ShapeDtypeStruct((8, 128), jnp.float32),
        ),
        grid_spec=pltpu.PrefetchScalarGridSpec(
            num_scalar_prefetch=1,
            grid=(steps,),
            in_specs=[
                whole(part),
                whole(back),
                pl.BlockSpec((owned // steps, batch), lambda i, _: (i, 0)),
                whole(queries),
            ],
            out_specs=(
                pl.BlockSpec((owned // steps, width), lambda i, _: (i, 0)),
                pl.BlockSpec((batch // steps, width), lambda i, _: (i, 0)),
                pl.BlockSpec((8, 128), lambda i, _: (0, 0)),
            ),
        ),
        compiler_params=pltpu.CompilerParams(vmem_limit_bytes=32 << 20),
        name="final",
    )(core.reshape(1).astype(jnp.int32), part, back, slopes, queries)


def shards(
    hidden_states,
    token_ids,
    norm_gain,
    q_weight,
    key_matrix,
    value_matrix,
    out_weight,
    label_table,
    refresh_rows,
    label_counts,
    queries,
    positives,
):
    f32, bf16 = jnp.float32, jnp.bfloat16
    width = hidden_states.shape[1]
    texts, length = token_ids.shape
    xh, core = lax.axis_index("xh"), lax.axis_index("c")
    member = lax.axis_index(MP)
    ndp, nmp = 64, 4
    rows = q_weight.shape[0]

    def to_group(block, by):
        return lax.ppermute(
            block,
            ("y", "xh", "xl", "c"),
            [
                (8 * v + 4 * h + 2 * l + k, 8 * ((v - by) % 4) + 4 * l + 2 * k + h)
                for v in range(4)
                for h in (0, 1)
                for l in (0, 1)
                for k in (0, 1)
            ],
        )

    y = lax.axis_index("y")
    packed = jnp.concatenate([key_matrix, value_matrix, q_weight], axis=1)
    cut = packed.shape[1]
    moved = to_group(jnp.concatenate([packed, out_weight[:, : SENT - cut]], axis=1), 0)
    half = norm_half(core, hidden_states, norm_gain)
    moved, half, out_weight = lax.optimization_barrier((moved, half, out_weight))
    in_z = lax.all_gather(moved, "z", axis=0, tiled=True)
    out_y = in_order([to_group(out_weight, d) for d in range(4)], y)
    out_all = lax.all_gather(out_y.reshape(4 * rows, -1), "z", axis=0, tiled=True)
    facing = [(i, 3 - i) for i in range(4)]
    half_other = lax.ppermute(half, RING_X, facing)
    ids_other = lax.ppermute(token_ids, RING_X, facing)

    balance = (1.0 - focal_beta) / -jnp.expm1(
        label_counts.astype(f32) * math.log(focal_beta)
    )
    owned = label_table.shape[0]
    root = math.sqrt(width)
    first_label = (lax.axis_index(DP) * nmp + member) * owned
    own_rows = jnp.arange(owned, dtype=jnp.int32)
    chosen = refresh_rows[:, None] == own_rows[None, :]
    kept = ~jnp.any(chosen, axis=0)
    kept_balance = jnp.where(kept, balance, 0.0)
    matched = jnp.any(positives[:, :, None] == (first_label + own_rows)[None, None, :], axis=1)
    signs = jnp.where(matched, 1.0, -1.0)
    logits = (
        lax.dot_general(
            queries, label_table, (((1,), (1,)), ((), ())), preferred_element_type=f32
        )
        / root
    )
    terms, slope = focal(signs * logits)
    kept_loss = jnp.sum(kept_balance[None, :] * terms)
    kept_slopes = (kept_balance[None, :] * signs * slope).astype(bf16)
    kept_query = jnp.dot(kept_slopes, label_table, preferred_element_type=f32)
    new_balance = jnp.sum(jnp.where(chosen, balance[None, :], 0.0), axis=1)
    new_signs = jnp.where(
        jnp.any(positives[:, :, None] == (first_label + refresh_rows)[None, None, :], axis=1),
        1.0,
        -1.0,
    )

    live = (token_ids != 0).astype(f32)
    share = texts // nmp
    live_own = lax.dynamic_slice_in_dim(live, member * share, share, 0)
    states_own = lax.dynamic_slice_in_dim(
        hidden_states, member * share * length, share * length, 0
    ).reshape(share, length, width)
    counted = jnp.sum(live_own, axis=1, keepdims=True)
    states_sum = jnp.sum(states_own.astype(f32) * live_own[:, :, None], axis=1)

    keeps = xh == core
    give = jnp.where(keeps, half_other, half)
    keep = jnp.where(keeps, half, half_other)
    ids = jnp.where(keeps, token_ids, ids_other)

    allowed, live_rows = attend_tables(ids)
    early = (kept_slopes, kept_loss, new_balance, new_signs, chosen, allowed, live_rows)
    in_z, early = lax.optimization_barrier((in_z, early))
    kept_slopes, kept_loss, new_balance, new_signs, chosen, allowed, live_rows = early
    sums = jnp.stack([kept_loss, jnp.sum(balance)])

    own = in_z[:, :cut]
    up, down = ring_near(own)
    far = ring_far(up, down)
    near = (own, up, down)
    give_near = project(y, give, near)
    early = (kept_query, sums, states_sum, counted, give_near)
    far, early = lax.optimization_barrier((far, early))
    kept_query, sums, states_sum, counted, give_near = early
    given = project(y, give, far, give_near, bf16)
    given, keep = lax.optimization_barrier((given, keep))
    taken = shift(given, "c", 2, 1)
    raw = project(y, keep, (*near, *far))
    pooled = attend_pooled(raw, taken, allowed, live_rows, length)

    pooled_other = shift(pooled, "c", 2, 1)
    both = jnp.concatenate(
        [jnp.where(core == 0, pooled, pooled_other), jnp.where(core == 0, pooled_other, pooled)],
        axis=0,
    )
    head_terms = lax.dot_general(
        both, out_all, (((1,), (1,)), ((), ())), preferred_element_type=f32
    )
    exchanged = lax.all_to_all(
        head_terms.astype(bf16).reshape(8, share, -1), ("xh", "xl", "c"), 0, 0, tiled=True
    )
    summed = jnp.sum(exchanged.astype(f32).reshape(nmp, 2, share, -1), axis=0)
    output_own = (
        summed.reshape(2, share, ndp // 2, rows).transpose(1, 2, 0, 3).reshape(share, width)
    )
    refreshed = ((states_sum + output_own) / counted).astype(bf16)

    mine, theirs, new_slopes = tail(
        core, sums, refreshed, queries, kept_query, new_signs, new_balance[None, :]
    )
    slopes = kept_slopes.T + lax.dot_general(
        chosen.astype(bf16),
        new_slopes.astype(bf16),
        (((0,), (1,)), ((), ())),
        preferred_element_type=f32,
    ).astype(bf16)

    batch = queries.shape[0]
    plane = ("y", "xh", "xl")
    part = mine + shift(theirs, "c", 2, 1)
    part = jnp.sum(
        lax.all_to_all(part.reshape(16, batch // 16, HALF), plane, 0, 0, tiled=True), axis=0
    )
    part = jnp.sum(spread(part, "z", 8), axis=0)
    lane = lax.broadcasted_iota(jnp.int32, part.shape, 1)
    spare = (lane >= width - HALF) & (lane % 128 >= 64) & (core == 1)
    low = part - lax.reduce_precision(part, 8, 7)
    part = jnp.where(spare, low, part).astype(bf16)
    part = spread(part, plane, 16).reshape(batch, HALF)
    back = shift(part, "c", 2, 1)
    label_grad, query_grad, loss = final(core, part, back, slopes, queries, owned * ndp * nmp)
    return (label_grad, query_grad, loss[0, 0])


def solution(mesh):
    grid = Mesh(mesh.devices.reshape(SIZES), AXES)
    in_specs = (
        P(DP, None),
        P(DP, None),
        P(),
        P(DP, MP),
        P(DP, MP),
        P(DP, MP),
        P(DP, MP),
        P(AXES, None),
        P(AXES),
        P(AXES),
        P(),
        P(),
    )
    out_specs = (P(AXES, None), P(), P())
    return jax.shard_map(shards, mesh=grid, in_specs=in_specs, out_specs=out_specs, check_vma=False)
```

```python
import functools
import math

import jax
import jax.numpy as jnp
import numpy as np
from jax import lax
from jax.experimental import pallas as pl
from jax.experimental.pallas import tpu as pltpu
from jax.sharding import Mesh, PartitionSpec as P

HEAD_WIDTH = 128

rope_theta = 1000000.0
norm_eps = 1e-06
focal_beta = 0.9999

AXES = ("z", "y", "xh", "xl", "c")
SIZES = (8, 4, 2, 2, 2)
DP = ("z", "y", "xh")
MP = ("xl", "c")
RING_X = ("xh", "xl")


BLOCK = 128
HALF = 1920
SENT = 1280


def rotary_tables(length):
    half = HEAD_WIDTH // 2
    frequency = rope_theta ** (-2.0 * np.arange(half) / HEAD_WIDTH)
    angles = np.arange(length)[:, None] * frequency[None, :]
    cosine = np.concatenate([np.cos(angles), np.cos(angles)], axis=1)
    sine = np.concatenate([-np.sin(angles), np.sin(angles)], axis=1)
    repeat = BLOCK // length
    return (
        jnp.asarray(np.tile(cosine, (repeat, 1)), jnp.float32),
        jnp.asarray(np.tile(sine, (repeat, 1)), jnp.float32),
    )


def norm_kernel(core_ref, states_ref, gain_ref, out_ref, turned_ref):
    states = states_ref[...].astype(jnp.float32)
    scaled = lax.rsqrt(jnp.mean(states * states, axis=1, keepdims=True) + norm_eps)
    turned_ref[...] = (states * scaled * gain_ref[...]).T
    rows = out_ref.shape[1] // 8

    def block(z, y):
        first = pl.multiple_of(((z * 4 + y) * 2 + core_ref[0]) * rows, 8)
        return turned_ref[pl.ds(first, rows), :]

    for y in range(4):
        for pair in range(4):
            out_ref[y, 2 * pair * rows : 2 * (pair + 1) * rows, :] = jnp.concatenate(
                [block(2 * pair, y), block(2 * pair + 1, y)], axis=0
            ).astype(jnp.bfloat16)


def norm_half(core, states, gain):
    tokens, width = states.shape
    block = 128
    return pl.pallas_call(
        norm_kernel,
        out_shape=jax.ShapeDtypeStruct((4, width // 8, tokens), jnp.bfloat16),
        grid_spec=pltpu.PrefetchScalarGridSpec(
            num_scalar_prefetch=1,
            grid=(tokens // block,),
            in_specs=[
                pl.BlockSpec((block, width), lambda i, _: (i, 0)),
                pl.BlockSpec((1, width), lambda i, _: (0, 0)),
            ],
            out_specs=pl.BlockSpec((4, width // 8, block), lambda i, _: (0, 0, i)),
            scratch_shapes=[pltpu.VMEM((width, block), jnp.float32)],
        ),
        compiler_params=pltpu.CompilerParams(vmem_limit_bytes=32 << 20),
        cost_estimate=pl.CostEstimate(
            flops=4 * tokens * width, bytes_accessed=3 * tokens * width, transcendentals=tokens
        ),
        name="norm",
    )(core.reshape(1).astype(jnp.int32), states, gain.reshape(1, width))


def near_kernel(place_ref, x_ref, w0_ref, w1_ref, w3_ref, out_ref):
    def dot(x, w):
        return lax.dot_general(
            x, w, (((0,), (0,)), ((), ())), preferred_element_type=jnp.float32
        )

    y = place_ref[0]
    out_ref[...] = (
        dot(x_ref[y], w0_ref[...])
        + dot(x_ref[(y + 1) % 4], w1_ref[...])
        + dot(x_ref[(y + 3) % 4], w3_ref[...])
    )


def far_kernel(place_ref, x_ref, near_ref, w2a_ref, w2b_ref, out_ref):
    def dot(x, w):
        return lax.dot_general(
            x, w, (((0,), (0,)), ((), ())), preferred_element_type=jnp.float32
        )

    half = w2a_ref.shape[0]
    far = x_ref[0]
    out_ref[...] = (
        near_ref[...] + dot(far[:half], w2a_ref[...]) + dot(far[half:], w2b_ref[...])
    ).astype(out_ref.dtype)


def whole_kernel(place_ref, x_ref, w0_ref, w1_ref, w3_ref, w2a_ref, w2b_ref, out_ref):
    def dot(x, w):
        return lax.dot_general(
            x, w, (((0,), (0,)), ((), ())), preferred_element_type=jnp.float32
        )

    y = place_ref[0]
    half = w2a_ref.shape[0]
    far = x_ref[(y + 2) % 4]
    out_ref[...] = (
        dot(x_ref[y], w0_ref[...])
        + dot(x_ref[(y + 1) % 4], w1_ref[...])
        + dot(x_ref[(y + 3) % 4], w3_ref[...])
        + dot(far[:half], w2a_ref[...])
        + dot(far[half:], w2b_ref[...])
    )


def project(y, x, pieces, near=None, dtype=jnp.float32):
    _, depth, tokens = x.shape
    columns = pieces[0].shape[1]
    block = tokens // 2
    fixed = [pl.BlockSpec(w.shape, lambda i, _: (0, 0)) for w in pieces]
    tile = pl.BlockSpec((block, columns), lambda i, _: (i, 0))
    if near is None:
        kernel, extra = near_kernel if len(pieces) == 3 else whole_kernel, ()
        x_spec = pl.BlockSpec((4, depth, block), lambda i, _: (0, 0, i))
    else:
        kernel, extra = far_kernel, (near,)
        x_spec = pl.BlockSpec((1, depth, block), lambda i, p: ((p[0] + 2) % 4, 0, i))
    used = sum(w.shape[0] for w in pieces)
    return pl.pallas_call(
        kernel,
        out_shape=jax.ShapeDtypeStruct((tokens, columns), dtype),
        grid_spec=pltpu.PrefetchScalarGridSpec(
            num_scalar_prefetch=1,
            grid=(tokens // block,),
            in_specs=[x_spec, *[tile for _ in extra], *fixed],
            out_specs=tile,
        ),
        compiler_params=pltpu.CompilerParams(vmem_limit_bytes=56 << 20),
        cost_estimate=pl.CostEstimate(
            flops=2 * used * tokens * columns,
            bytes_accessed=6 * tokens * columns + 2 * used * (tokens + columns),
            transcendentals=0,
        ),
        name="far" if near is not None else "near" if len(pieces) == 3 else "whole",
    )(y.reshape(1).astype(jnp.int32), x, *extra, *pieces)


def attend_kernel(raw_ref, add_ref, allowed_ref, live_ref, member_ref, cos_ref, sin_ref, out_ref):
    width = HEAD_WIDTH
    cosine, sine = cos_ref[...], sin_ref[...]
    members = member_ref[...]
    heads = raw_ref.shape[1] // width - 2
    texts = members.shape[0] // heads

    def rotate(x):
        return (x * cosine + pltpu.roll(x, width // 2, 1) * sine).astype(jnp.bfloat16)

    for block in range(raw_ref.shape[0] // BLOCK):
        rows = slice(block * BLOCK, (block + 1) * BLOCK)

        def column(index):
            lanes = slice(index * width, (index + 1) * width)
            return raw_ref[rows, lanes] + add_ref[rows, lanes].astype(jnp.float32)

        allowed = jnp.concatenate([allowed_ref[rows, :]] * heads, axis=0)
        live = jnp.concatenate([live_ref[rows, :]] * heads, axis=0)
        keys = rotate(column(0))
        values = column(1).astype(jnp.bfloat16)
        rotated = jnp.concatenate([rotate(column(h + 2)) for h in range(heads)], axis=0)
        scores = lax.dot_general(
            rotated, keys, (((1,), (1,)), ((), ())), preferred_element_type=jnp.float32
        ) * (1.0 / math.sqrt(width))
        weights = jnp.where(allowed > 0.0, jnp.exp(scores), 0.0)
        total = jnp.sum(weights, axis=1, keepdims=True)
        probs = (weights * (live / total)).astype(jnp.bfloat16)
        shares = jnp.dot(members, probs, preferred_element_type=jnp.float32)
        high = shares.astype(jnp.bfloat16)
        low = (shares - high.astype(jnp.float32)).astype(jnp.bfloat16)
        pooled = jnp.dot(high, values, preferred_element_type=jnp.float32) + jnp.dot(
            low, values, preferred_element_type=jnp.float32
        )
        for head in range(heads):
            columns = slice(head * width, (head + 1) * width)
            out_ref[block * texts : (block + 1) * texts, columns] = pooled[
                head * texts : (head + 1) * texts
            ].astype(out_ref.dtype)


def attend_tables(text_ids):
    texts, length = text_ids.shape
    per = BLOCK // length
    live = (text_ids != 0).reshape(texts // per, BLOCK)
    place = np.arange(BLOCK)
    shape = (place[:, None] // length == place[None, :] // length) & (
        place[:, None] >= place[None, :]
    )
    allowed = (jnp.asarray(shape)[None] & live[:, None, :]).astype(jnp.float32)
    return allowed.reshape(-1, BLOCK), (text_ids != 0).astype(jnp.float32).reshape(-1, 1)


def attend_pooled(raw, add, allowed, live, length):
    tokens, columns = raw.shape
    texts = tokens // length
    per = BLOCK // length
    heads = columns // HEAD_WIDTH - 2
    owner = (np.arange(per)[:, None] == np.arange(BLOCK)[None, :] // length).astype(np.float32)
    members = jnp.asarray(np.kron(np.eye(heads), owner), jnp.bfloat16)
    cosine, sine = rotary_tables(length)
    step = 4 * BLOCK
    return pl.pallas_call(
        attend_kernel,
        out_shape=jax.ShapeDtypeStruct((texts, heads * HEAD_WIDTH), jnp.bfloat16),
        grid=(tokens // step,),
        in_specs=[
            pl.BlockSpec((step, columns), lambda i: (i, 0)),
            pl.BlockSpec((step, columns), lambda i: (i, 0)),
            pl.BlockSpec((step, BLOCK), lambda i: (i, 0)),
            pl.BlockSpec((step, 1), lambda i: (i, 0)),
            pl.BlockSpec(members.shape, lambda i: (0, 0)),
            pl.BlockSpec((BLOCK, HEAD_WIDTH), lambda i: (0, 0)),
            pl.BlockSpec((BLOCK, HEAD_WIDTH), lambda i: (0, 0)),
        ],
        out_specs=pl.BlockSpec((4 * per, heads * HEAD_WIDTH), lambda i: (i, 0)),
        compiler_params=pltpu.CompilerParams(vmem_limit_bytes=56 << 20),
        cost_estimate=pl.CostEstimate(
            flops=4 * tokens * BLOCK * heads * HEAD_WIDTH,
            bytes_accessed=raw.size * 8,
            transcendentals=tokens * BLOCK * heads,
        ),
        name="attend",
    )(
        raw,
        add,
        allowed,
        live,
        members,
        cosine,
        sine,
    )


def shift(x, axis, size, by):
    return lax.ppermute(x, axis, [(i, (i + by) % size) for i in range(size)])


def ring_near(own):
    return shift(own, "y", 4, -1), shift(own, "y", 4, 1)


def ring_far(up, down):
    half = up.shape[0] // 2
    return shift(up[:half], "y", 4, -1), shift(down[half:], "y", 4, 1)


def in_order(parts, index):
    n = len(parts)
    out = jnp.zeros((n,) + parts[0].shape, parts[0].dtype)
    for d, part in enumerate(parts):
        out = lax.dynamic_update_slice_in_dim(out, part[None], (index + d) % n, 0)
    return out


def spread(x, axes, size):
    return lax.all_to_all(jnp.broadcast_to(x[None], (size,) + x.shape), axes, 0, 0, tiled=True)


def focal(margin):
    missed = jax.nn.sigmoid(-margin)
    softened = jnp.maximum(-margin, 0.0) + jnp.log1p(jnp.exp(-jnp.abs(margin)))
    return missed * missed * softened, -(missed * missed) * (
        2.0 * jax.nn.sigmoid(margin) * softened + missed
    )


def tail_kernel(core_ref, sums_ref, new_ref, queries_ref, kept_ref, signs_ref, balance_ref, mine_ref, theirs_ref, slopes_ref):
    batch, width = queries_ref.shape
    rows = new_ref[...]
    logits = lax.dot_general(
        queries_ref[...], rows, (((1,), (1,)), ((), ())), preferred_element_type=jnp.float32
    ) / math.sqrt(width)
    signs = signs_ref[...]
    balance = balance_ref[...]
    terms, slope = focal(signs * logits)
    losses = jnp.sum(balance * terms, axis=1, keepdims=True) + sums_ref[0] / batch
    slopes = (balance * signs * slope).astype(jnp.bfloat16)
    slopes_ref[...] = slopes.astype(jnp.float32)
    left = kept_ref[:, :HALF] + jnp.dot(slopes, rows[:, :HALF], preferred_element_type=jnp.float32)
    right = kept_ref[:, HALF:] + jnp.dot(slopes, rows[:, HALF:], preferred_element_type=jnp.float32)
    rest = width - HALF
    lanes = (2 * HALF - width) // 2
    loss_lanes = jnp.broadcast_to(losses, (batch, lanes))
    class_lanes = jnp.full((batch, lanes), sums_ref[1] / batch, jnp.float32)

    def write(first, second):
        first[...] = left
        second[:, :rest] = right
        second[:, rest : rest + lanes] = loss_lanes
        second[:, rest + lanes :] = class_lanes

    @pl.when(core_ref[0] == 0)
    def _():
        write(mine_ref, theirs_ref)

    @pl.when(core_ref[0] != 0)
    def _():
        write(theirs_ref, mine_ref)


def tail(core, sums, rows, queries, kept, signs, balance):
    batch, width = queries.shape
    smem = pl.BlockSpec(memory_space=pltpu.SMEM)
    vmem = pl.BlockSpec(memory_space=pltpu.VMEM)
    half = jax.ShapeDtypeStruct((batch, HALF), jnp.float32)
    return pl.pallas_call(
        tail_kernel,
        out_shape=(half, half, jax.ShapeDtypeStruct((batch, rows.shape[0]), jnp.float32)),
        in_specs=[smem, smem, vmem, vmem, vmem, vmem, vmem],
        out_specs=(vmem, vmem, vmem),
        compiler_params=pltpu.CompilerParams(vmem_limit_bytes=24 << 20),
        cost_estimate=pl.CostEstimate(
            flops=4 * batch * width * rows.shape[0],
            bytes_accessed=10 * batch * width,
            transcendentals=8 * batch,
        ),
        name="tail",
    )(core.reshape(1).astype(jnp.int32), sums, rows, queries, kept, signs, balance)


def final_kernel(core_ref, part_ref, back_ref, slopes_ref, queries_ref, label_ref, query_ref, loss_ref, *, labels):
    batch, width = queries_ref.shape
    rest = width - HALF
    lanes = (2 * HALF - width) // 2
    first = core_ref[0] == 0
    step = pl.program_id(0)
    rows = pl.ds(pl.multiple_of(step * query_ref.shape[0], 16), query_ref.shape[0])

    def side(left_ref, right_ref):
        extra = jnp.sum(right_ref[:, rest:].astype(jnp.float32), axis=0, keepdims=True)
        losses = jnp.sum(extra[:, :lanes]) / (lanes // 2)
        weights = jnp.sum(extra[:, lanes:]) / (lanes // 2)
        factor = labels / weights
        scale = factor / math.sqrt(width)
        loss_ref[...] = jnp.full(loss_ref.shape, factor * losses / (batch * labels), jnp.float32)
        query_ref[:, :HALF] = scale * left_ref[rows, :].astype(jnp.float32)
        query_ref[:, HALF:] = scale * right_ref[rows, :rest].astype(jnp.float32)
        label_ref[...] = scale * lax.dot_general(
            slopes_ref[...],
            queries_ref[...],
            (((1,), (0,)), ((), ())),
            preferred_element_type=jnp.float32,
        )

    @pl.when(first)
    def _():
        side(part_ref, back_ref)

    @pl.when(jnp.logical_not(first))
    def _():
        side(back_ref, part_ref)


def final(core, part, back, slopes, queries, labels):
    batch, width = queries.shape
    owned = slopes.shape[0]
    steps = 4
    whole = lambda x: pl.BlockSpec(x.shape, lambda i, _: (0, 0))
    return pl.pallas_call(
        functools.partial(final_kernel, labels=labels),
        out_shape=(
            jax.ShapeDtypeStruct((owned, width), jnp.float32),
            jax.ShapeDtypeStruct((batch, width), jnp.float32),
            jax.ShapeDtypeStruct((8, 128), jnp.float32),
        ),
        grid_spec=pltpu.PrefetchScalarGridSpec(
            num_scalar_prefetch=1,
            grid=(steps,),
            in_specs=[
                whole(part),
                whole(back),
                pl.BlockSpec((owned // steps, batch), lambda i, _: (i, 0)),
                whole(queries),
            ],
            out_specs=(
                pl.BlockSpec((owned // steps, width), lambda i, _: (i, 0)),
                pl.BlockSpec((batch // steps, width), lambda i, _: (i, 0)),
                pl.BlockSpec((8, 128), lambda i, _: (0, 0)),
            ),
        ),
        compiler_params=pltpu.CompilerParams(vmem_limit_bytes=32 << 20),
        name="final",
    )(core.reshape(1).astype(jnp.int32), part, back, slopes, queries)


def shards(
    hidden_states,
    token_ids,
    norm_gain,
    q_weight,
    key_matrix,
    value_matrix,
    out_weight,
    label_table,
    refresh_rows,
    label_counts,
    queries,
    positives,
):
    f32, bf16 = jnp.float32, jnp.bfloat16
    width = hidden_states.shape[1]
    texts, length = token_ids.shape
    xh, core = lax.axis_index("xh"), lax.axis_index("c")
    member = lax.axis_index(MP)
    ndp, nmp = 64, 4
    rows = q_weight.shape[0]

    def to_group(block, by):
        return lax.ppermute(
            block,
            ("y", "xh", "xl", "c"),
            [
                (8 * v + 4 * h + 2 * l + k, 8 * ((v - by) % 4) + 4 * l + 2 * k + h)
                for v in range(4)
                for h in (0, 1)
                for l in (0, 1)
                for k in (0, 1)
            ],
        )

    y = lax.axis_index("y")
    packed = jnp.concatenate([key_matrix, value_matrix, q_weight], axis=1)
    cut = packed.shape[1]
    moved = to_group(jnp.concatenate([packed, out_weight[:, : SENT - cut]], axis=1), 0)
    half = norm_half(core, hidden_states, norm_gain)
    moved, half, out_weight = lax.optimization_barrier((moved, half, out_weight))
    in_z = lax.all_gather(moved, "z", axis=0, tiled=True)
    out_y = in_order([to_group(out_weight, d) for d in range(4)], y)
    out_all = lax.all_gather(out_y.reshape(4 * rows, -1), "z", axis=0, tiled=True)
    facing = [(i, 3 - i) for i in range(4)]
    half_other = lax.ppermute(half, RING_X, facing)
    ids_other = lax.ppermute(token_ids, RING_X, facing)

    balance = (1.0 - focal_beta) / -jnp.expm1(
        label_counts.astype(f32) * math.log(focal_beta)
    )
    owned = label_table.shape[0]
    root = math.sqrt(width)
    first_label = (lax.axis_index(DP) * nmp + member) * owned
    own_rows = jnp.arange(owned, dtype=jnp.int32)
    chosen = refresh_rows[:, None] == own_rows[None, :]
    kept = ~jnp.any(chosen, axis=0)
    kept_balance = jnp.where(kept, balance, 0.0)
    matched = jnp.any(positives[:, :, None] == (first_label + own_rows)[None, None, :], axis=1)
    signs = jnp.where(matched, 1.0, -1.0)
    logits = (
        lax.dot_general(
            queries, label_table, (((1,), (1,)), ((), ())), preferred_element_type=f32
        )
        / root
    )
    terms, slope = focal(signs * logits)
    kept_loss = jnp.sum(kept_balance[None, :] * terms)
    kept_slopes = (kept_balance[None, :] * signs * slope).astype(bf16)
    kept_query = jnp.dot(kept_slopes, label_table, preferred_element_type=f32)
    new_balance = jnp.sum(jnp.where(chosen, balance[None, :], 0.0), axis=1)
    new_signs = jnp.where(
        jnp.any(positives[:, :, None] == (first_label + refresh_rows)[None, None, :], axis=1),
        1.0,
        -1.0,
    )

    live = (token_ids != 0).astype(f32)
    share = texts // nmp
    live_own = lax.dynamic_slice_in_dim(live, member * share, share, 0)
    states_own = lax.dynamic_slice_in_dim(
        hidden_states, member * share * length, share * length, 0
    ).reshape(share, length, width)
    counted = jnp.sum(live_own, axis=1, keepdims=True)
    states_sum = jnp.sum(states_own.astype(f32) * live_own[:, :, None], axis=1)

    keeps = xh == core
    give = jnp.where(keeps, half_other, half)
    keep = jnp.where(keeps, half, half_other)
    ids = jnp.where(keeps, token_ids, ids_other)

    allowed, live_rows = attend_tables(ids)
    early = (kept_slopes, kept_loss, new_balance, new_signs, chosen, allowed, live_rows)
    in_z, early = lax.optimization_barrier((in_z, early))
    kept_slopes, kept_loss, new_balance, new_signs, chosen, allowed, live_rows = early
    sums = jnp.stack([kept_loss, jnp.sum(balance)])

    own = in_z[:, :cut]
    up, down = ring_near(own)
    far = ring_far(up, down)
    near = (own, up, down)
    give_near = project(y, give, near)
    early = (kept_query, sums, states_sum, counted, give_near)
    far, early = lax.optimization_barrier((far, early))
    kept_query, sums, states_sum, counted, give_near = early
    given = project(y, give, far, give_near, bf16)
    given, keep = lax.optimization_barrier((given, keep))
    taken = shift(given, "c", 2, 1)
    raw = project(y, keep, (*near, *far))
    pooled = attend_pooled(raw, taken, allowed, live_rows, length)

    pooled_other = shift(pooled, "c", 2, 1)
    both = jnp.concatenate(
        [jnp.where(core == 0, pooled, pooled_other), jnp.where(core == 0, pooled_other, pooled)],
        axis=0,
    )
    head_terms = lax.dot_general(
        both, out_all, (((1,), (1,)), ((), ())), preferred_element_type=f32
    )
    exchanged = lax.all_to_all(
        head_terms.astype(bf16).reshape(8, share, -1), ("xh", "xl", "c"), 0, 0, tiled=True
    )
    summed = jnp.sum(exchanged.astype(f32).reshape(nmp, 2, share, -1), axis=0)
    output_own = (
        summed.reshape(2, share, ndp // 2, rows).transpose(1, 2, 0, 3).reshape(share, width)
    )
    refreshed = ((states_sum + output_own) / counted).astype(bf16)

    mine, theirs, new_slopes = tail(
        core, sums, refreshed, queries, kept_query, new_signs, new_balance[None, :]
    )
    slopes = kept_slopes.T + lax.dot_general(
        chosen.astype(bf16),
        new_slopes.astype(bf16),
        (((0,), (1,)), ((), ())),
        preferred_element_type=f32,
    ).astype(bf16)

    batch = queries.shape[0]
    plane = ("y", "xh", "xl")
    part = mine + shift(theirs, "c", 2, 1)
    part = jnp.sum(
        lax.all_to_all(part.reshape(16, batch // 16, HALF), plane, 0, 0, tiled=True), axis=0
    )
    part = jnp.sum(spread(part, "z", 8), axis=0)
    lane = lax.broadcasted_iota(jnp.int32, part.shape, 1)
    spare = (lane >= width - HALF) & (lane % 128 >= 64) & (core == 1)
    low = part - lax.reduce_precision(part, 8, 7)
    part = jnp.where(spare, low, part).astype(bf16)
    part = spread(part, plane, 16).reshape(batch, HALF)
    back = shift(part, "c", 2, 1)
    label_grad, query_grad, loss = final(core, part, back, slopes, queries, owned * ndp * nmp)
    return (label_grad, query_grad, loss[0, 0])


def solution(mesh):
    grid = Mesh(mesh.devices.reshape(SIZES), AXES)
    in_specs = (
        P(DP, None),
        P(DP, None),
        P(),
        P(DP, MP),
        P(DP, MP),
        P(DP, MP),
        P(DP, MP),
        P(AXES, None),
        P(AXES),
        P(AXES),
        P(),
        P(),
    )
    out_specs = (P(AXES, None), P(), P())
    return jax.shard_map(shards, mesh=grid, in_specs=in_specs, out_specs=out_specs, check_vma=False)
```
